32 devices in a mesh: dp: 4 (over x, core), fsdp: 8 (over z, y).
Axes of the slice: x: 2, y: 2, z: 4, core: 2. Of those that a mesh axis runs over, the one named last changes fastest.
Arguments:
- hidden: bfloat16 [32, 128, 768], P(('dp', 'fsdp')), may hold values from -6 to 6
- sections: int32 [32], P(('dp', 'fsdp')), may hold values from 0 to 3
- lengths: int32 [32], P(('dp', 'fsdp')), may hold values from 32 to 128, as said below
- token_mask: int32 [32, 128], P(('dp', 'fsdp')), may hold values 0 or 1
- cotangent: bfloat16 [32, 128, 768], P(('dp', 'fsdp')), may hold values from -6 to 6
- ln1_gain: bfloat16 [768], P(('dp', 'fsdp')), may hold values from 0.5 to 1.5
- ln1_bias: bfloat16 [768], P(('dp', 'fsdp')), may hold values from -1.5 to 1.5
- qkv_weight: bfloat16 [768, 2304], P(('dp', 'fsdp')), may hold values from -0.21875 to 0.21875
- qv_bias: bfloat16 [1536], P(('dp', 'fsdp')), may hold values from -1.5 to 1.5
- out_weight: bfloat16 [768, 768], P(('dp', 'fsdp')), may hold values from -0.875 to 0.875
- out_bias: bfloat16 [768], P(('dp', 'fsdp')), may hold values from -1.5 to 1.5
- ln2_gain: bfloat16 [768], P(('dp', 'fsdp')), may hold values from 0.5 to 1.5
- ln2_bias: bfloat16 [768], P(('dp', 'fsdp')), may hold values from -1.5 to 1.5
- fc_weight: bfloat16 [768, 3072], P(('dp', 'fsdp')), may hold values from -0.21875 to 0.21875
- fc_bias: bfloat16 [3072], P(('dp', 'fsdp')), may hold values from -1.5 to 1.5
- proj_weight: bfloat16 [3072, 768], P(('dp', 'fsdp')), may hold values from -0.109375 to 0.109375
- proj_bias: bfloat16 [768], P(('dp', 'fsdp')), may hold values from -1.5 to 1.5
Outputs:
- hidden_out: bfloat16 [32, 128, 768], P(('dp', 'fsdp'))
- grad_hidden: float32 [32, 128, 768], P(('dp', 'fsdp'))
- grad_ln1_gain: float32 [768], P(('dp', 'fsdp'))
- grad_ln1_bias: float32 [768], P(('dp', 'fsdp'))
- grad_qkv_weight: float32 [768, 2304], P(('dp', 'fsdp'))
- grad_qv_bias: float32 [1536], P(('dp', 'fsdp'))
- grad_out_weight: float32 [768, 768], P(('dp', 'fsdp'))
- grad_out_bias: float32 [768], P(('dp', 'fsdp'))
- grad_ln2_gain: float32 [768], P(('dp', 'fsdp'))
- grad_ln2_bias: float32 [768], P(('dp', 'fsdp'))
- grad_fc_weight: float32 [768, 3072], P(('dp', 'fsdp'))
- grad_fc_bias: float32 [3072], P(('dp', 'fsdp'))
- grad_proj_weight: float32 [3072, 768], P(('dp', 'fsdp'))
- grad_proj_bias: float32 [768], P(('dp', 'fsdp'))
The draws below stay inside these ranges and needn't reach their ends.
Inputs may be any that keep to these rules, and one draw needn't show every extreme that they name: `lengths`: some sequence has exactly 128 valid tokens and some has exactly 32.
All inputs are finite; a program needn't handle non-finite values. No bound on the sum of `token_mask` on one device may be relied on, other than what follows from the above.
Results may differ from the reference program's by a relative error of at most 0.013.
Values may be sent and summed in bfloat16 or wider, within the bound.
A program may use at most 192 MiB of HBM per device.

```python
import math
import jax
import jax.numpy as jnp
from jax import lax

D = 768
HEAD_DIM = 64
FF = 3072
SEQ_LEN = 128
PASSES = 4
SEQS = 32


def draw_lengths(key, part):
    first_key, second_key = jax.random.split(jax.random.fold_in(key, 11))
    base = jax.random.randint(first_key, (SEQS,), SEQ_LEN // 4, SEQ_LEN + 1)
    chosen = jax.random.permutation(second_key, SEQS)
    base = jnp.where(chosen == 0, SEQ_LEN, base)
    base = jnp.where(chosen == 1, SEQ_LEN // 4, base)
    return base.astype(jnp.int32)


def plant(entries, own_key, low, top_value):
    dims = entries.shape
    index_at = [jax.random.randint(jax.random.fold_in(own_key, axis), (), 0, dims[axis]) for axis in range(len(dims))]
    entries = entries.at[tuple(index_at)].set(low)
    longest = dims.index(max(dims))
    index_at[longest] = (index_at[longest] + 1) % dims[longest]
    return entries.at[tuple(index_at)].set(top_value)


def levels(stream_key, dims, pieces, smallest, top_value):
    level = 1.0
    for dim, shards_of in pieces:
        heights = jax.random.uniform(jax.random.fold_in(jax.random.fold_in(stream_key, 6), dim), (shards_of,), jnp.float32, smallest / len(pieces), top_value / len(pieces))
        level = level * jnp.repeat(jnp.exp(heights), dims[dim] // shards_of).reshape((-1,) + (1,) * (len(dims) - 1 - dim))
    return level


def bell_draw(rng, shape, scale, bound, pieces=(), kind=jnp.bfloat16):
    values = scale * jax.random.normal(rng, shape, jnp.float32)
    if pieces:
        values = values * levels(rng, shape, pieces, -0.22, 0.18)
    return jnp.clip(values, -bound, bound).astype(kind)


def setup_inputs(seed: int = 0) -> dict:
    keys = jax.random.split(jax.random.key(seed), 18)
    hidden = bell_draw(keys[0], (SEQS, SEQ_LEN, D), 1.0, 6.0, ((0, 32),))
    sections = plant(jax.random.randint(keys[1], (SEQS,), 0, 4), jax.random.fold_in(keys[1], 1), 0, 3).astype(jnp.int32)
    lengths = draw_lengths(jax.random.fold_in(keys[17], 71), 0)
    token_mask = plant((jax.random.randint(keys[3], (SEQS, SEQ_LEN), 0, 8) < 7).astype(jnp.int32), jax.random.fold_in(keys[3], 1), 0, 1)
    cotangent = bell_draw(keys[4], (SEQS, SEQ_LEN, D), 1.0, 6.0, ((0, 32),))
    ln1_gain = jnp.clip(1.0 + 0.1 * jax.random.normal(keys[5], (D,), jnp.float32), 0.5, 1.5).astype(jnp.bfloat16)
    ln1_bias = bell_draw(keys[6], (D,), 0.3, 1.5, ((0, 32),))
    qkv_weight = bell_draw(keys[7], (D, 3 * D), D ** -0.5, 0.21875, ((0, 32),))
    qv_bias = bell_draw(keys[8], (2 * D,), 0.3, 1.5, ((0, 32),))
    out_weight = bell_draw(keys[9], (D, D), (D // 16) ** -0.5, 0.875, ((0, 32),))
    out_bias = bell_draw(keys[10], (D,), 0.3, 1.5, ((0, 32),))
    ln2_gain = jnp.clip(1.0 + 0.1 * jax.random.normal(keys[11], (D,), jnp.float32), 0.5, 1.5).astype(jnp.bfloat16)
    ln2_bias = bell_draw(keys[12], (D,), 0.3, 1.5, ((0, 32),))
    fc_weight = bell_draw(keys[13], (D, FF), D ** -0.5, 0.21875, ((0, 32),))
    fc_bias = bell_draw(keys[14], (FF,), 0.3, 1.5, ((0, 32),))
    proj_weight = bell_draw(keys[15], (FF, D), FF ** -0.5, 0.109375, ((0, 32),))
    proj_bias = bell_draw(keys[16], (D,), 0.3, 1.5, ((0, 32),))
    return {"hidden": hidden, "sections": sections, "lengths": lengths, "token_mask": token_mask, "cotangent": cotangent, "ln1_gain": ln1_gain, "ln1_bias": ln1_bias, "qkv_weight": qkv_weight, "qv_bias": qv_bias, "out_weight": out_weight, "out_bias": out_bias, "ln2_gain": ln2_gain, "ln2_bias": ln2_bias, "fc_weight": fc_weight, "fc_bias": fc_bias, "proj_weight": proj_weight, "proj_bias": proj_bias}


@jax.custom_vjp
def low(v):
    return lax.optimization_barrier(v.astype(jnp.bfloat16)).astype(jnp.float32)

@jax.custom_vjp
def low_back(v):
    return v

def low_keep(v):
    return (low(v), None)

def low_pass(kept, grad):
    return (grad,)

def back_keep(v):
    return (v, None)

def back_low(kept, grad):
    return (low(grad),)
low.defvjp(low_keep, low_pass)
low_back.defvjp(back_keep, back_low)
epsilon = 1e-05
score_scale = 0.125
gelu_coef = 0.7978845608028654
highest = lax.Precision.HIGHEST

def layer_norm(values, gain, shift):
    centre = values - lax.optimization_barrier(jnp.mean(values, axis=-1, keepdims=True))
    spread = lax.optimization_barrier(jnp.mean(centre * centre, axis=-1, keepdims=True))
    return centre * lax.rsqrt(spread + epsilon) * gain + shift

def gelu_tanh(values):
    return 0.5 * values * (1.0 + jnp.tanh(gelu_coef * (values + 0.044715 * values * values * values)))

def matmul_high(left, right):
    return jnp.matmul(left, right, precision=highest)

def attend(queries, key_rows, values, key_valid):
    seq_count, seq_len, heads, head_size = queries.shape
    block_rows = min(512, seq_len)
    blocks = seq_len // block_rows
    stacked = jnp.moveaxis(queries.reshape(seq_count, blocks, block_rows, heads, head_size), 1, 0)
    starts = (jnp.arange(blocks) * block_rows).astype(jnp.int32)
    key_pos = jnp.arange(seq_len).astype(jnp.int32)[None, :]

    def one_block(items):
        query_block, block_start = items
        query_pos = block_start + jnp.arange(block_rows).astype(jnp.int32)[:, None]
        allowed = (key_pos <= query_pos) & (key_valid[:, None, :] | (key_pos == query_pos))
        scores = jnp.einsum('gqhd,gkhd->ghqk', query_block, key_rows, precision=highest) * score_scale
        scores = low_back(scores)
        scores = jnp.where(allowed[:, None], scores, -1e+30)
        row_max = lax.optimization_barrier(jnp.max(scores, axis=-1, keepdims=True))
        expo = jnp.exp(scores - row_max)
        probs = low(expo / lax.optimization_barrier(jnp.sum(expo, axis=-1, keepdims=True)))
        return jnp.einsum('ghqk,gkhd->gqhd', probs, values, precision=highest)
    outs = lax.map(jax.checkpoint(one_block), (stacked, starts))
    return jnp.moveaxis(outs, 0, 1).reshape(seq_count, seq_len, heads * head_size)

def one_pass(state, params, key_valid, live):
    gain_one, shift_one, qkv_w, qv_b, out_w, out_b, gain_two, shift_two, fc_w, fc_b, proj_w, proj_b = params
    seq_count, seq_len, model_width = state.shape
    normed = low(layer_norm(state, gain_one, shift_one))
    bias_full = jnp.concatenate([qv_b[:model_width], jnp.zeros_like(qv_b[:model_width]), qv_b[model_width:]])
    joined = low(low_back(matmul_high(normed, qkv_w) + bias_full))
    split = joined.reshape(seq_count, seq_len, 3, model_width // HEAD_DIM, HEAD_DIM)
    mixed = low(low_back(attend(split[:, :, 0], split[:, :, 1], split[:, :, 2], key_valid)))
    middle = state + low_back(matmul_high(mixed, out_w) + out_b)
    normed_two = low(layer_norm(middle, gain_two, shift_two))
    upper = low_back(matmul_high(normed_two, fc_w) + fc_b)
    activated = low(gelu_tanh(upper))
    result = middle + low_back(matmul_high(activated, proj_w) + proj_b)
    return jnp.where(live[:, None, None], result, state)

def reference(hidden, sections, lengths, token_mask, cotangent, ln1_gain, ln1_bias, qkv_weight, qv_bias, out_weight, out_bias, ln2_gain, ln2_bias, fc_weight, fc_bias, proj_weight, proj_bias):
    params = tuple((weight_arg.astype(jnp.float32) for weight_arg in (ln1_gain, ln1_bias, qkv_weight, qv_bias, out_weight, out_bias, ln2_gain, ln2_bias, fc_weight, fc_bias, proj_weight, proj_bias)))
    group = math.gcd(SEQS, max(1, 2048 // SEQ_LEN))
    groups = SEQS // group

    def regroup(array):
        return array.reshape((groups, group) + array.shape[1:])
    key_pos = jnp.arange(SEQ_LEN).astype(jnp.int32)

    def group_step(totals, items):
        states, cots, section_group, length_group, mask_group = items
        key_valid = (key_pos[None, :] < length_group[:, None]) & (mask_group == 1)

        def chain(start_state, weights):
            current = start_state
            for section_index in range(PASSES):
                current = one_pass(current, weights, key_valid, section_group >= section_index)
            return current
        result, pull = jax.vjp(chain, states.astype(jnp.float32), params)
        grad_states, grad_params = pull(cots.astype(jnp.float32))
        totals = jax.tree.map(jnp.add, totals, grad_params)
        return (totals, (result.astype(jnp.bfloat16), grad_states))
    zero_grads = jax.tree.map(jnp.zeros_like, params)
    totals, (outs, grads) = lax.scan(group_step, zero_grads, (regroup(hidden), regroup(cotangent), regroup(sections), regroup(lengths), regroup(token_mask)))
    return (outs.reshape(hidden.shape), grads.reshape(hidden.shape), totals[0], totals[1], totals[2], totals[3], totals[4], totals[5], totals[6], totals[7], totals[8], totals[9], totals[10], totals[11])
```

```python
import functools
import itertools

import jax
import jax.numpy as jnp
from jax import lax
from jax.experimental import pallas as pl
from jax.experimental.pallas import tpu as pltpu
from jax.sharding import PartitionSpec as P
MESH = pl.DeviceIdType.MESH

TREES = ("zyx", "zxy", "xyz")


def offsets(length):
    return [0, "o"] if length == 2 else list(range(-(length - 1), length))


class Place:
    def __init__(self, sizes):
        self.sizes = sizes
        dp, fs = lax.axis_index("dp"), lax.axis_index("fsdp")
        self.core = lax.rem(dp, 2)
        self.pos = {"x": dp // 2, "z": fs // sizes["y"], "y": lax.rem(fs, sizes["y"])}

    def device(self, pos, core):
        return (pos["x"] * 2 + core, pos["z"] * self.sizes["y"] + pos["y"])

    def index(self, pos, core):
        dp, fs = self.device(pos, core)
        return dp * (self.sizes["z"] * self.sizes["y"]) + fs

    def chip(self, pos):
        return (pos["x"] * self.sizes["z"] + pos["z"]) * self.sizes["y"] + pos["y"]

    def neighbours(self):
        out = [(None, self.device(self.pos, 1 - self.core))]
        for d, length in self.sizes.items():
            if length == 2:
                out.append((None, self.device({**self.pos, d: 1 - self.pos[d]}, self.core)))
            elif length > 2:
                for s in (1, -1):
                    q = self.pos[d] + s
                    out.append(((q >= 0) & (q < length), self.device({**self.pos, d: q}, self.core)))
        return out


def when(conds, fn):
    conds = [c for c in conds if c is not None]
    if not conds:
        fn()
    else:
        pl.when(functools.reduce(jnp.logical_and, conds))(lambda: (fn(), None)[1])


def entry_barrier(place):
    barrier = pltpu.get_barrier_semaphore()
    total = 0
    for cond, dev in place.neighbours():
        when([cond], lambda dev=dev: pl.semaphore_signal(barrier, inc=1, device_id=dev, device_id_type=MESH))
        total = total + (1 if cond is None else cond.astype(jnp.int32))
    pl.semaphore_wait(barrier, total)


def gather_kernel(sizes, pieces, order, n_in, *refs):
    ins, outs = refs[:n_in], refs[n_in:2 * n_in]
    send_sem, recv_sem, pair_send, pair_recv, local_sem = refs[2 * n_in:]
    place = Place(sizes)
    pos, core = place.pos, place.core
    entry_barrier(place)
    partner = place.device(pos, 1 - core)
    locals_ = []
    for a in range(n_in):
        c = pltpu.make_async_copy(ins[a], outs[a].at[pos["x"], core, pos["z"], pos["y"]], local_sem.at[a])
        c.start()
        locals_.append(c)

    def part(pi, at, who):
        a, tree, lo, n = pieces[pi]
        return outs[a].at[at["x"], who, at["z"], at["y"], pl.ds(lo, n)]

    def remote(src, dst, send, recv, dev):
        return pltpu.make_async_remote_copy(src_ref=src, dst_ref=dst, send_sem=send, recv_sem=recv, device_id=dev, device_id_type=MESH)

    def line(d):
        if sizes[d] == 1:
            return []
        if sizes[d] == 2:
            return [(0, None, 1 - pos[d])]
        return [(0, pos[d] + 1 < sizes[d], pos[d] + 1), (1, pos[d] > 0, pos[d] - 1)]

    left = {}
    for pi, t in order:
        left[pi] = left.get(pi, 0) + 1
    seen = dict.fromkeys(left, 0)
    whole = [slice(None)] * 3
    for pi, t in order:
        a, tree, lo, n = pieces[pi]
        own = all(v == 0 for v in t)
        at, conds = dict(pos), []
        for d, v in zip(tree, t):
            if v == "o":
                at[d] = 1 - pos[d]
            elif v != 0:
                at[d] = pos[d] + v
                conds.append((at[d] >= 0) if v < 0 else (at[d] < sizes[d]))
        chip = place.chip(at)
        dst = part(pi, at, core)
        src = ins[a].at[pl.ds(lo, n)] if own else dst
        k = max([j for j, v in enumerate(t) if v != 0], default=-1)

        def handle(tree=tree, t=t, own=own, chip=chip, dst=dst, src=src, k=k, pi=pi):
            if not own:
                remote(dst, dst, pair_send.at[pi], recv_sem.at[pi, chip], partner).wait_recv()
            for j in (2, 1, 0):
                d = tree[j]
                if j < k:
                    continue
                for slot, ok, q in line(d):
                    if j == k and (t[j] == "o" or (t[j] < 0) != (slot == 0)):
                        continue
                    when([ok], remote(src, dst, send_sem.at[pi, 2 * "xyz".index(d) + slot], recv_sem.at[pi, chip],
                                      place.device({**pos, d: q}, core)).start)
            remote(src, dst, pair_send.at[pi], pair_recv.at[pi], partner).start()
        when(conds, handle)
        seen[pi] += 1

    full = dict.fromkeys("xyz", slice(None))
    for pi, (a, tree, lo, n) in enumerate(pieces):
        for j, d in enumerate(tree):
            at = {e: (slice(None) if tree.index(e) < j else pos[e]) for e in "xyz"}
            for slot, ok, q in line(d):
                sem = send_sem.at[pi, 2 * "xyz".index(d) + slot]
                if sizes[d] == 2:
                    ref = part(pi, at, core)
                    remote(ref, ref, sem, recv_sem.at[pi, 0], partner).wait_send()
                else:
                    for z in range(sizes[d]):
                        ref = part(pi, {**at, d: z}, core)
                        sent = (pos[d] >= z) if slot == 0 else (pos[d] <= z)
                        when([ok, sent], remote(ref, ref, sem, recv_sem.at[pi, 0], partner).wait_send)
        ref = part(pi, full, core)
        remote(ref, ref, pair_send.at[pi], pair_recv.at[pi], partner).wait_send()
        ref = part(pi, full, 1 - core)
        remote(ref, ref, pair_send.at[pi], pair_recv.at[pi], partner).wait_recv()
    for c in locals_:
        c.wait()


def gather_order(sizes, pieces, alpha):
    ev = []
    for pi, (a, tree, lo, n) in enumerate(pieces):
        for t in itertools.product(*[offsets(sizes[d]) for d in tree]):
            hops = sum(1 if v == "o" else abs(v) for v in t)
            ev.append((pi * alpha + hops, pi, t))
    ev.sort(key=lambda e: (e[0], e[1]))
    return [(pi, t) for _, pi, t in ev]


def gather(sizes, shards, alpha=0.05):
    chips = sizes["x"] * sizes["y"] * sizes["z"]
    pieces = []
    for a, s in enumerate(shards):
        tiles = s.shape[0] // 8
        if tiles % 3 == 0 and tiles < 12:
            cuts = [(i, i * tiles // 3, tiles // 3) for i in range(3)]
        elif tiles % 2 == 0:
            cuts = [(i, i * tiles // 2, tiles // 2) for i in range(2)]
        else:
            cuts = [(2, 0, tiles)]
        for tree, lo, n in cuts:
            pieces.append((a, TREES[tree], lo * 8, n * 8))
    order = gather_order(sizes, pieces, alpha)
    n_in = len(shards)
    return pl.pallas_call(
        functools.partial(gather_kernel, sizes, pieces, order, n_in),
        out_shape=[jax.ShapeDtypeStruct((sizes["x"], 2, sizes["z"], sizes["y"]) + s.shape, s.dtype) for s in shards],
        in_specs=[pl.BlockSpec(memory_space=pltpu.VMEM)] * n_in,
        out_specs=[pl.BlockSpec(memory_space=pl.ANY)] * n_in,
        scratch_shapes=[
            pltpu.SemaphoreType.DMA((len(pieces), 6)),
            pltpu.SemaphoreType.DMA((len(pieces), chips)),
            pltpu.SemaphoreType.DMA((len(pieces),)),
            pltpu.SemaphoreType.DMA((len(pieces),)),
            pltpu.SemaphoreType.DMA((n_in,)),
        ],
        compiler_params=pltpu.CompilerParams(collective_id=0, has_side_effects=True),
        name="gather",
    )(*shards)


HEAD_DIM = 64
PASSES = 4


epsilon = 1e-05
score_scale = 0.125
gelu_coef = 0.7978845608028654


def layer_norm(values, gain, shift):
    centre = values - jnp.mean(values, axis=-1, keepdims=True)
    spread = jnp.mean(centre * centre, axis=-1, keepdims=True)
    return centre * lax.rsqrt(spread + epsilon) * gain + shift


def gelu_tanh(values):
    return (
        0.5 * values * (1.0 + jnp.tanh(gelu_coef * (values + 0.044715 * values * values * values)))
    )


def fetch_attention(ln1_gain, ln1_bias, qkv_weight, qv_bias, out_weight, out_bias):
    return (
        lax.all_gather(ln1_gain, ("dp", "fsdp"), axis=0, tiled=True),
        lax.all_gather(ln1_bias, ("dp", "fsdp"), axis=0, tiled=True),
        lax.all_gather(qkv_weight, ("dp", "fsdp"), axis=0, tiled=True),
        lax.all_gather(qv_bias, ("dp", "fsdp"), axis=0, tiled=True),
        lax.all_gather(out_weight, ("dp", "fsdp"), axis=0, tiled=True),
        lax.all_gather(out_bias, ("dp", "fsdp"), axis=0, tiled=True),
    )


def fetch_mlp(ln2_gain, ln2_bias, fc_weight, fc_bias, proj_weight, proj_bias):
    return (
        lax.all_gather(ln2_gain, ("dp", "fsdp"), axis=0, tiled=True),
        lax.all_gather(ln2_bias, ("dp", "fsdp"), axis=0, tiled=True),
        lax.all_gather(fc_weight, ("dp", "fsdp"), axis=0, tiled=True),
        lax.all_gather(fc_bias, ("dp", "fsdp"), axis=0, tiled=True),
        lax.all_gather(proj_weight, ("dp", "fsdp"), axis=0, tiled=True),
        lax.all_gather(proj_bias, ("dp", "fsdp"), axis=0, tiled=True),
    )


def fetch_all(sizes, attention, mlp):
    ln1_gain, ln1_bias, qkv_weight, qv_bias, out_weight, out_bias = attention
    ln2_gain, ln2_bias, fc_weight, fc_bias, proj_weight, proj_bias = mlp
    big = (qkv_weight, out_weight, fc_weight, proj_weight)
    small = (ln1_gain, ln1_bias, qv_bias, out_bias, ln2_gain, ln2_bias, fc_bias, proj_bias)
    width = -(-sum(v.shape[0] for v in small) // 1024) * 128
    if any(w.shape[0] % 8 for w in big):
        return fetch_attention(*attention), fetch_mlp(*mlp)
    packed = jnp.concatenate(small)
    packed = jnp.pad(packed, (0, 8 * width - packed.shape[0])).reshape(8, width)
    *full, rows = gather(sizes, (*big, packed))
    qkv_full, out_full, fc_full, proj_full = [w.reshape(-1, w.shape[-1]) for w in full]
    rows = rows.reshape(-1, 8 * width)
    vectors, start = [], 0
    for v in small:
        vectors.append(rows[:, start : start + v.shape[0]].reshape(-1))
        start += v.shape[0]
    g1, b1, qv, ob, g2, b2, fb, pb = vectors
    return (g1, b1, qkv_full, qv, out_full, ob), (g2, b2, fc_full, fb, proj_full, pb)


def allowed_rows(key_valid, block_rows, seq_len):
    query_pos = jnp.arange(block_rows, dtype=jnp.int32)[:, None]
    key_pos = jnp.arange(seq_len, dtype=jnp.int32)[None, :]
    return (key_pos <= query_pos) & (key_valid[:, None, :] | (key_pos == query_pos))


def attend_forward(queries, key_rows, values, key_valid):
    seq_len = queries.shape[1]
    block_rows = min(512, seq_len)
    scores = (
        jnp.einsum("gqhd,gkhd->ghqk", queries, key_rows, preferred_element_type=jnp.float32)
        * score_scale
    )
    allowed = allowed_rows(key_valid, block_rows, seq_len)[:, None]
    scores = jnp.where(allowed, scores, -1e30)
    row_max = jnp.max(scores, axis=-1, keepdims=True)
    expo = jnp.exp(scores - row_max)
    row_total = jnp.sum(expo, axis=-1, keepdims=True)
    probs = (expo / row_total).astype(jnp.bfloat16)
    outputs = jnp.einsum("ghqk,gkhd->gqhd", probs, values, preferred_element_type=jnp.float32)
    totals = (row_max + jnp.log(row_total))[..., 0]
    return (outputs, totals)


def attend_backward(queries, key_rows, values, log_totals, grad_mixed, key_valid):
    seq_len = queries.shape[1]
    block_rows = min(512, seq_len)
    scores = (
        jnp.einsum("gqhd,gkhd->ghqk", queries, key_rows, preferred_element_type=jnp.float32)
        * score_scale
    )
    allowed = allowed_rows(key_valid, block_rows, seq_len)[:, None]
    block_totals = log_totals[:, :, 0:block_rows, None]
    probs = jnp.where(allowed, jnp.exp(scores - block_totals), 0.0)
    probs_low = probs.astype(jnp.bfloat16)
    grad_values = jnp.einsum(
        "ghqk,gqhd->gkhd", probs_low, grad_mixed, preferred_element_type=jnp.float32
    )
    grad_probs = jnp.einsum(
        "gqhd,gkhd->ghqk", grad_mixed, values, preferred_element_type=jnp.float32
    )
    inner = jnp.sum(grad_probs * probs, axis=-1, keepdims=True)
    grad_scores = (probs * (grad_probs - inner)).astype(jnp.bfloat16)
    grad_queries = (
        jnp.einsum("ghqk,gkhd->gqhd", grad_scores, key_rows, preferred_element_type=jnp.float32)
        * score_scale
    )
    grad_keys = (
        jnp.einsum("ghqk,gqhd->gkhd", grad_scores, queries, preferred_element_type=jnp.float32)
        * score_scale
    )
    return (grad_queries, grad_keys, grad_values)


def forward_pass(state, weights, key_valid, live, seq_count, seq_len):
    (gain_one, shift_one, qkv_w, qv_b, out_w, out_b), (
        gain_two,
        shift_two,
        fc_w,
        fc_b,
        proj_w,
        proj_b,
    ) = weights
    row_count, model_width = state.shape
    head_count = model_width // HEAD_DIM
    normed = layer_norm(state, gain_one.astype(jnp.float32), shift_one.astype(jnp.float32)).astype(
        jnp.bfloat16
    )
    qv_float = qv_b.astype(jnp.float32)
    bias_full = jnp.concatenate(
        [qv_float[:model_width], jnp.zeros((model_width,), jnp.float32), qv_float[model_width:]]
    )
    joined = (jnp.dot(normed, qkv_w, preferred_element_type=jnp.float32) + bias_full).astype(
        jnp.bfloat16
    )
    split = joined.reshape(seq_count, seq_len, 3, head_count, HEAD_DIM)
    queries = split[:, :, 0]
    key_rows = split[:, :, 1]
    values = split[:, :, 2]
    mixed_float, log_totals = attend_forward(queries, key_rows, values, key_valid)
    mixed = mixed_float.reshape(row_count, model_width).astype(jnp.bfloat16)
    middle = (
        state
        + jnp.dot(mixed, out_w, preferred_element_type=jnp.float32)
        + out_b.astype(jnp.float32)
    )
    normed_two = layer_norm(
        middle, gain_two.astype(jnp.float32), shift_two.astype(jnp.float32)
    ).astype(jnp.bfloat16)
    upper = jnp.dot(normed_two, fc_w, preferred_element_type=jnp.float32) + fc_b.astype(jnp.float32)
    activated = gelu_tanh(upper).astype(jnp.bfloat16)
    result = (
        middle
        + jnp.dot(activated, proj_w, preferred_element_type=jnp.float32)
        + proj_b.astype(jnp.float32)
    )
    record = (
        state,
        normed,
        queries,
        key_rows,
        values,
        log_totals,
        mixed,
        middle,
        normed_two,
        upper,
        activated,
    )
    return (jnp.where(live, result, state), record)


def backward_mlp(grad_next, record, weights, live):
    (
        state,
        normed,
        queries,
        key_rows,
        values,
        log_totals,
        mixed,
        middle,
        normed_two,
        upper,
        activated,
    ) = record
    (gain_one, shift_one, qkv_w, qv_b, out_w, out_b), (
        gain_two,
        shift_two,
        fc_w,
        fc_b,
        proj_w,
        proj_b,
    ) = weights
    grad_out = jnp.where(live, grad_next, 0.0)
    grad_branch = grad_out.astype(jnp.bfloat16)
    term_proj_b = jnp.sum(grad_branch.astype(jnp.float32), axis=0)
    term_proj_w = jnp.einsum(
        "ti,to->io", activated, grad_branch, preferred_element_type=jnp.float32
    )
    grad_act = jnp.einsum("to,io->ti", grad_branch, proj_w, preferred_element_type=jnp.float32)
    gelu_pull = jax.vjp(gelu_tanh, upper)[1]
    grad_upper = gelu_pull(grad_act)[0].astype(jnp.bfloat16)
    term_fc_b = jnp.sum(grad_upper.astype(jnp.float32), axis=0)
    term_fc_w = jnp.einsum("td,tf->df", normed_two, grad_upper, preferred_element_type=jnp.float32)
    grad_normed_two = jnp.einsum("tf,df->td", grad_upper, fc_w, preferred_element_type=jnp.float32)
    norm_pull_two = jax.vjp(
        layer_norm, middle, gain_two.astype(jnp.float32), shift_two.astype(jnp.float32)
    )[1]
    grad_mid_norm, term_gain_two, term_shift_two = norm_pull_two(grad_normed_two)
    grad_middle = grad_out + grad_mid_norm
    mlp_terms = (term_gain_two, term_shift_two, term_fc_w, term_fc_b, term_proj_w, term_proj_b)
    return (grad_middle, mlp_terms)


def backward_attention(grad_next, grad_middle, record, weights, key_valid, live):
    (
        state,
        normed,
        queries,
        key_rows,
        values,
        log_totals,
        mixed,
        middle,
        normed_two,
        upper,
        activated,
    ) = record
    (gain_one, shift_one, qkv_w, qv_b, out_w, out_b), mlp_weights = weights
    row_count, model_width = state.shape
    grad_attn = grad_middle.astype(jnp.bfloat16)
    term_out_b = jnp.sum(grad_attn.astype(jnp.float32), axis=0)
    term_out_w = jnp.einsum("td,te->de", mixed, grad_attn, preferred_element_type=jnp.float32)
    grad_mixed = jnp.einsum(
        "te,de->td", grad_attn, out_w, preferred_element_type=jnp.float32
    ).astype(jnp.bfloat16)
    grad_mixed = grad_mixed.reshape(queries.shape)
    grad_queries, grad_keys, grad_values = attend_backward(
        queries, key_rows, values, log_totals, grad_mixed, key_valid
    )
    grad_joined = (
        jnp.stack([grad_queries, grad_keys, grad_values], axis=2)
        .reshape(row_count, 3 * model_width)
        .astype(jnp.bfloat16)
    )
    column_sums = jnp.sum(grad_joined.astype(jnp.float32), axis=0)
    term_qv_b = jnp.concatenate([column_sums[:model_width], column_sums[2 * model_width :]])
    term_qkv_w = jnp.einsum("td,tk->dk", normed, grad_joined, preferred_element_type=jnp.float32)
    grad_normed = jnp.einsum("tk,dk->td", grad_joined, qkv_w, preferred_element_type=jnp.float32)
    norm_pull_one = jax.vjp(
        layer_norm, state, gain_one.astype(jnp.float32), shift_one.astype(jnp.float32)
    )[1]
    grad_state_norm, term_gain_one, term_shift_one = norm_pull_one(grad_normed)
    grad_prev = grad_middle + grad_state_norm + jnp.where(live, 0.0, grad_next)
    attention_terms = (term_gain_one, term_shift_one, term_qkv_w, term_qv_b, term_out_w, term_out_b)
    return (grad_prev, attention_terms)


def body(
    sizes,
    hidden,
    sections,
    lengths,
    token_mask,
    cotangent,
    ln1_gain,
    ln1_bias,
    qkv_weight,
    qv_bias,
    out_weight,
    out_bias,
    ln2_gain,
    ln2_bias,
    fc_weight,
    fc_bias,
    proj_weight,
    proj_bias,
):
    seq_count, seq_len, model_width = hidden.shape
    row_count = seq_count * seq_len
    key_pos = jnp.arange(seq_len, dtype=jnp.int32)
    key_valid = (key_pos[None, :] < lengths[:, None]) & (token_mask == 1)

    current = fetch_all(
        sizes,
        (ln1_gain, ln1_bias, qkv_weight, qv_bias, out_weight, out_bias),
        (ln2_gain, ln2_bias, fc_weight, fc_bias, proj_weight, proj_bias),
    )

    state = hidden.reshape(row_count, model_width).astype(jnp.float32)
    records = []
    for section_index in range(PASSES):
        live = jnp.repeat(sections >= section_index, seq_len)[:, None]
        state, record = forward_pass(state, current, key_valid, live, seq_count, seq_len)
        records.append(record)
    hidden_out = state.astype(jnp.bfloat16).reshape(seq_count, seq_len, model_width)
    grad_state = cotangent.reshape(row_count, model_width).astype(jnp.float32)
    attention_sum = None
    mlp_sum = None
    for section_index in reversed(range(PASSES)):
        live = jnp.repeat(sections >= section_index, seq_len)[:, None]
        grad_middle, mlp_terms = backward_mlp(grad_state, records[section_index], current, live)
        if mlp_sum is None:
            mlp_sum = mlp_terms
        else:
            mlp_sum = jax.tree.map(jnp.add, mlp_sum, mlp_terms)
        grad_state, attention_terms = backward_attention(
            grad_state, grad_middle, records[section_index], current, key_valid, live
        )
        if attention_sum is None:
            attention_sum = attention_terms
        else:
            attention_sum = jax.tree.map(jnp.add, attention_sum, attention_terms)
    sum_gain_one, sum_shift_one, sum_qkv_w, sum_qv_b, sum_out_w, sum_out_b = attention_sum
    attention_grads = (
        lax.psum_scatter(sum_gain_one, ("dp", "fsdp"), scatter_dimension=0, tiled=True),
        lax.psum_scatter(sum_shift_one, ("dp", "fsdp"), scatter_dimension=0, tiled=True),
        lax.psum_scatter(sum_qkv_w.astype(jnp.bfloat16), ("dp", "fsdp"), scatter_dimension=0, tiled=True).astype(jnp.float32),
        lax.psum_scatter(sum_qv_b, ("dp", "fsdp"), scatter_dimension=0, tiled=True),
        lax.psum_scatter(sum_out_w.astype(jnp.bfloat16), ("dp", "fsdp"), scatter_dimension=0, tiled=True).astype(jnp.float32),
        lax.psum_scatter(sum_out_b, ("dp", "fsdp"), scatter_dimension=0, tiled=True),
    )
    sum_gain_two, sum_shift_two, sum_fc_w, sum_fc_b, sum_proj_w, sum_proj_b = mlp_sum
    finished = (
        lax.psum_scatter(sum_gain_two, ("dp", "fsdp"), scatter_dimension=0, tiled=True),
        lax.psum_scatter(sum_shift_two, ("dp", "fsdp"), scatter_dimension=0, tiled=True),
        lax.psum_scatter(sum_fc_w.astype(jnp.bfloat16), ("dp", "fsdp"), scatter_dimension=0, tiled=True).astype(jnp.float32),
        lax.psum_scatter(sum_fc_b, ("dp", "fsdp"), scatter_dimension=0, tiled=True),
        lax.psum_scatter(sum_proj_w.astype(jnp.bfloat16), ("dp", "fsdp"), scatter_dimension=0, tiled=True).astype(jnp.float32),
        lax.psum_scatter(sum_proj_b, ("dp", "fsdp"), scatter_dimension=0, tiled=True),
    )
    grad_hidden = grad_state.reshape(seq_count, seq_len, model_width)
    return (
        hidden_out,
        grad_hidden,
        attention_grads[0],
        attention_grads[1],
        attention_grads[2],
        attention_grads[3],
        attention_grads[4],
        attention_grads[5],
        finished[0],
        finished[1],
        finished[2],
        finished[3],
        finished[4],
        finished[5],
    )


def solution(mesh):
    chips_x = mesh.shape["dp"] // 2
    sizes = {"x": chips_x, "y": chips_x, "z": mesh.shape["fsdp"] // chips_x}
    return jax.shard_map(
        functools.partial(body, sizes),
        mesh=mesh,
        in_specs=(
            P(("dp", "fsdp"), None, None),
            P(("dp", "fsdp")),
            P(("dp", "fsdp")),
            P(("dp", "fsdp"), None),
            P(("dp", "fsdp"), None, None),
            P(("dp", "fsdp")),
            P(("dp", "fsdp")),
            P(("dp", "fsdp"), None),
            P(("dp", "fsdp")),
            P(("dp", "fsdp"), None),
            P(("dp", "fsdp")),
            P(("dp", "fsdp")),
            P(("dp", "fsdp")),
            P(("dp", "fsdp"), None),
            P(("dp", "fsdp")),
            P(("dp", "fsdp"), None),
            P(("dp", "fsdp")),
        ),
        out_specs=(
            P(("dp", "fsdp"), None, None),
            P(("dp", "fsdp"), None, None),
            P(("dp", "fsdp")),
            P(("dp", "fsdp")),
            P(("dp", "fsdp"), None),
            P(("dp", "fsdp")),
            P(("dp", "fsdp"), None),
            P(("dp", "fsdp")),
            P(("dp", "fsdp")),
            P(("dp", "fsdp")),
            P(("dp", "fsdp"), None),
            P(("dp", "fsdp")),
            P(("dp", "fsdp"), None),
            P(("dp", "fsdp")),
        ),
        check_vma=False,
    )
```

```python
import functools
import itertools

import jax
import jax.numpy as jnp
from jax import lax
from jax.experimental import pallas as pl
from jax.experimental.pallas import tpu as pltpu
from jax.sharding import PartitionSpec as P
MESH = pl.DeviceIdType.MESH

TREES = ("zyx", "zxy", "xyz")


def offsets(length):
    return [0, "o"] if length == 2 else list(range(-(length - 1), length))


class Place:
    def __init__(self, sizes):
        self.sizes = sizes
        dp, fs = lax.axis_index("dp"), lax.axis_index("fsdp")
        self.core = lax.rem(dp, 2)
        self.pos = {"x": dp // 2, "z": fs // sizes["y"], "y": lax.rem(fs, sizes["y"])}

    def device(self, pos, core):
        return (pos["x"] * 2 + core, pos["z"] * self.sizes["y"] + pos["y"])

    def index(self, pos, core):
        dp, fs = self.device(pos, core)
        return dp * (self.sizes["z"] * self.sizes["y"]) + fs

    def chip(self, pos):
        return (pos["x"] * self.sizes["z"] + pos["z"]) * self.sizes["y"] + pos["y"]

    def neighbours(self):
        out = [(None, self.device(self.pos, 1 - self.core))]
        for d, length in self.sizes.items():
            if length == 2:
                out.append((None, self.device({**self.pos, d: 1 - self.pos[d]}, self.core)))
            elif length > 2:
                for s in (1, -1):
                    q = self.pos[d] + s
                    out.append(((q >= 0) & (q < length), self.device({**self.pos, d: q}, self.core)))
        return out


def when(conds, fn):
    conds = [c for c in conds if c is not None]
    if not conds:
        fn()
    else:
        pl.when(functools.reduce(jnp.logical_and, conds))(lambda: (fn(), None)[1])


def entry_barrier(place):
    barrier = pltpu.get_barrier_semaphore()
    total = 0
    for cond, dev in place.neighbours():
        when([cond], lambda dev=dev: pl.semaphore_signal(barrier, inc=1, device_id=dev, device_id_type=MESH))
        total = total + (1 if cond is None else cond.astype(jnp.int32))
    pl.semaphore_wait(barrier, total)


def gather_kernel(sizes, pieces, order, n_in, *refs):
    ins, outs = refs[:n_in], refs[n_in:2 * n_in]
    send_sem, recv_sem, pair_send, pair_recv, local_sem = refs[2 * n_in:]
    place = Place(sizes)
    pos, core = place.pos, place.core
    entry_barrier(place)
    partner = place.device(pos, 1 - core)
    locals_ = []
    for a in range(n_in):
        c = pltpu.make_async_copy(ins[a], outs[a].at[pos["x"], core, pos["z"], pos["y"]], local_sem.at[a])
        c.start()
        locals_.append(c)

    def part(pi, at, who):
        a, tree, lo, n = pieces[pi]
        return outs[a].at[at["x"], who, at["z"], at["y"], pl.ds(lo, n)]

    def remote(src, dst, send, recv, dev):
        return pltpu.make_async_remote_copy(src_ref=src, dst_ref=dst, send_sem=send, recv_sem=recv, device_id=dev, device_id_type=MESH)

    def line(d):
        if sizes[d] == 1:
            return []
        if sizes[d] == 2:
            return [(0, None, 1 - pos[d])]
        return [(0, pos[d] + 1 < sizes[d], pos[d] + 1), (1, pos[d] > 0, pos[d] - 1)]

    left = {}
    for pi, t in order:
        left[pi] = left.get(pi, 0) + 1
    seen = dict.fromkeys(left, 0)
    whole = [slice(None)] * 3
    for pi, t in order:
        a, tree, lo, n = pieces[pi]
        own = all(v == 0 for v in t)
        at, conds = dict(pos), []
        for d, v in zip(tree, t):
            if v == "o":
                at[d] = 1 - pos[d]
            elif v != 0:
                at[d] = pos[d] + v
                conds.append((at[d] >= 0) if v < 0 else (at[d] < sizes[d]))
        chip = place.chip(at)
        dst = part(pi, at, core)
        src = ins[a].at[pl.ds(lo, n)] if own else dst
        k = max([j for j, v in enumerate(t) if v != 0], default=-1)

        def handle(tree=tree, t=t, own=own, chip=chip, dst=dst, src=src, k=k, pi=pi):
            if not own:
                remote(dst, dst, pair_send.at[pi], recv_sem.at[pi, chip], partner).wait_recv()
            for j in (2, 1, 0):
                d = tree[j]
                if j < k:
                    continue
                for slot, ok, q in line(d):
                    if j == k and (t[j] == "o" or (t[j] < 0) != (slot == 0)):
                        continue
                    when([ok], remote(src, dst, send_sem.at[pi, 2 * "xyz".index(d) + slot], recv_sem.at[pi, chip],
                                      place.device({**pos, d: q}, core)).start)
            remote(src, dst, pair_send.at[pi], pair_recv.at[pi], partner).start()
        when(conds, handle)
        seen[pi] += 1

    full = dict.fromkeys("xyz", slice(None))
    for pi, (a, tree, lo, n) in enumerate(pieces):
        for j, d in enumerate(tree):
            at = {e: (slice(None) if tree.index(e) < j else pos[e]) for e in "xyz"}
            for slot, ok, q in line(d):
                sem = send_sem.at[pi, 2 * "xyz".index(d) + slot]
                if sizes[d] == 2:
                    ref = part(pi, at, core)
                    remote(ref, ref, sem, recv_sem.at[pi, 0], partner).wait_send()
                else:
                    for z in range(sizes[d]):
                        ref = part(pi, {**at, d: z}, core)
                        sent = (pos[d] >= z) if slot == 0 else (pos[d] <= z)
                        when([ok, sent], remote(ref, ref, sem, recv_sem.at[pi, 0], partner).wait_send)
        ref = part(pi, full, core)
        remote(ref, ref, pair_send.at[pi], pair_recv.at[pi], partner).wait_send()
        ref = part(pi, full, 1 - core)
        remote(ref, ref, pair_send.at[pi], pair_recv.at[pi], partner).wait_recv()
    for c in locals_:
        c.wait()


def gather_order(sizes, pieces, alpha):
    ev = []
    for pi, (a, tree, lo, n) in enumerate(pieces):
        for t in itertools.product(*[offsets(sizes[d]) for d in tree]):
            hops = sum(1 if v == "o" else abs(v) for v in t)
            ev.append((pi * alpha + hops, pi, t))
    ev.sort(key=lambda e: (e[0], e[1]))
    return [(pi, t) for _, pi, t in ev]


def gather(sizes, shards, alpha=0.05):
    chips = sizes["x"] * sizes["y"] * sizes["z"]
    pieces = []
    for a, s in enumerate(shards):
        tiles = s.shape[0] // 8
        if tiles % 3 == 0 and tiles < 12:
            cuts = [(i, i * tiles // 3, tiles // 3) for i in range(3)]
        elif tiles % 2 == 0:
            cuts = [(i, i * tiles // 2, tiles // 2) for i in range(2)]
        else:
            cuts = [(2, 0, tiles)]
        for tree, lo, n in cuts:
            pieces.append((a, TREES[tree], lo * 8, n * 8))
    order = gather_order(sizes, pieces, alpha)
    n_in = len(shards)
    return pl.pallas_call(
        functools.partial(gather_kernel, sizes, pieces, order, n_in),
        out_shape=[jax.ShapeDtypeStruct((sizes["x"], 2, sizes["z"], sizes["y"]) + s.shape, s.dtype) for s in shards],
        in_specs=[pl.BlockSpec(memory_space=pltpu.VMEM)] * n_in,
        out_specs=[pl.BlockSpec(memory_space=pl.ANY)] * n_in,
        scratch_shapes=[
            pltpu.SemaphoreType.DMA((len(pieces), 6)),
            pltpu.SemaphoreType.DMA((len(pieces), chips)),
            pltpu.SemaphoreType.DMA((len(pieces),)),
            pltpu.SemaphoreType.DMA((len(pieces),)),
            pltpu.SemaphoreType.DMA((n_in,)),
        ],
        compiler_params=pltpu.CompilerParams(collective_id=0, has_side_effects=True),
        name="gather",
    )(*shards)


class View:
    def __init__(self, ref, dims, fixed=None, core=None):
        self.ref, self.dims, self.fixed, self.core = ref, dims, fixed or {}, core

    def fix(self, d, v):
        return View(self.ref, self.dims, {**self.fixed, d: v}, self.core)

    def free(self):
        return [d for d in self.dims if d not in self.fixed]

    def index(self, at, cols=None):
        idx = [self.fixed.get(d, at.get(d, slice(None))) for d in self.dims]
        if self.core is not None:
            core, lo, n = self.core
            return (idx[0], core, *idx[1:], slice(None), pl.ds(lo, n))
        return tuple(idx)

    def whole(self):
        return self.ref.at[self.index({})]


def accumulate(sizes, dst, terms):
    dims = terms[0].free()

    def step(i, carry):
        at = {}
        for d in reversed(dims):
            at[d] = lax.rem(i, sizes[d])
            i = i // sizes[d]
        total = None
        for t in terms:
            v = t.ref[t.index(at)].astype(jnp.float32)
            total = v if total is None else total + v
        if isinstance(dst, View):
            dst.ref[dst.index(at)] = total.astype(dst.ref.dtype)
        else:
            dst(total)
        return carry

    count = 1
    for d in dims:
        count *= sizes[d]
    if count == 1:
        step(0, 0)
    else:
        lax.fori_loop(0, count, step, 0)


def piece_buffers(sizes, piece, rows):
    a, tree, lo, n = piece
    dims = list("xzy")
    shapes = [tuple(sizes[d] for d in dims) + (rows, n)]
    for d in tree:
        dims.remove(d)
        rest = tuple(sizes[e] for e in dims) + (rows, n)
        if sizes[d] == 2:
            shapes.append(rest)
        elif sizes[d] > 2:
            shapes += [(sizes[d],) + rest] * 2
    return shapes


def piece_copies(sizes, tree):
    return 1 + sum(0 if sizes[d] == 1 else 1 if sizes[d] == 2 else 2 * sizes[d] for d in tree)


def piece_events(sizes, tree):
    ev, t = [(0.0, ("pair",))], 0.0
    for j, d in enumerate(tree):
        if sizes[d] == 2:
            t += 1
            ev.append((t, ("swap", j)))
        elif sizes[d] > 2:
            for hop in range(1, sizes[d]):
                for far in range(hop, sizes[d] - 1):
                    dest = sizes[d] - 1 - (far - hop)
                    if dest > hop:
                        ev.append((t + hop + (far - hop) * 0.2, ("up", j, hop, dest)))
                        ev.append((t + hop + (far - hop) * 0.2, ("down", j, sizes[d] - 1 - hop, sizes[d] - 1 - dest)))
            t += sizes[d] - 1
            ev.append((t, ("land", j)))
    return ev


def reduce_kernel(sizes, pieces, order, n_in, *refs):
    ins, outs, rest = refs[:n_in], refs[n_in:2 * n_in], list(refs[2 * n_in:])
    send_sem, recv_sem = rest[-2:]
    place = Place(sizes)
    pos, core = place.pos, place.core
    partner = place.device(pos, 1 - core)
    state, base, sent = [], 0, []
    for pi, (a, tree, lo, n) in enumerate(pieces):
        k = len(piece_buffers(sizes, pieces[pi], 8))
        bufs, rest = rest[:k], rest[k:]
        copies = {"pair": (0, 0)}
        c, b = 1, 1
        for j, d in enumerate(tree):
            if sizes[d] > 1:
                copies[j] = (c, b)
                c += 1 if sizes[d] == 2 else 2 * sizes[d]
                b += 1 if sizes[d] == 2 else 2
        state.append({"bufs": bufs, "base": base, "copies": copies, "cur": None})
        base += c

    def copy(src, dst, sem, dev):
        return pltpu.make_async_remote_copy(src_ref=src, dst_ref=dst, send_sem=send_sem.at[sem], recv_sem=recv_sem.at[sem], device_id=dev, device_id_type=MESH)

    def send(conds, src, dst, sem, dev):
        c = copy(src, dst, sem, dev)
        when(conds, c.start)
        sent.append((conds, c))

    def await_copy(buf, sem):
        copy(buf, buf, sem, partner).wait_recv()

    entry_barrier(place)
    for pi, (a, tree, lo, n) in enumerate(pieces):
        src = View(ins[a], list("xzy"), core=(1 - core, lo, n))
        send([], src.whole(), state[pi]["bufs"][0], state[pi]["base"], partner)

    def launch(pi, j):
        a, tree, lo, n = pieces[pi]
        st = state[pi]
        while j < 3 and sizes[tree[j]] == 1:
            st["cur"] = st["cur"].fix(tree[j], 0)
            j += 1
        if j == 3:
            return
        d, cur = tree[j], st["cur"]
        c, b = st["copies"][j]
        c += st["base"]
        p, size = pos[d], sizes[d]
        if size == 2:
            send([], cur.fix(d, 1 - p).whole(), st["bufs"][b], c, place.device({**pos, d: 1 - p}, core))
            return
        for t in range(size - 1, 0, -1):
            send([p == 0], cur.fix(d, t).whole(), st["bufs"][b].at[t], c + t, place.device({**pos, d: p + 1}, core))
            t = size - 1 - t
            send([p == size - 1], cur.fix(d, t).whole(), st["bufs"][b + 1].at[t], c + size + t, place.device({**pos, d: p - 1}, core))

    def run(pi, what):
        a, tree, lo, n = pieces[pi]
        st = state[pi]
        if what[0] == "pair":
            buf = st["bufs"][0]
            await_copy(buf, st["base"])
            mine = View(ins[a], list("xzy"), core=(core, lo, n))
            st["cur"] = View(buf, list("xzy"))
            accumulate(sizes, st["cur"], [st["cur"], mine])
            launch(pi, 0)
            return
        j = what[1]
        d, cur = tree[j], st["cur"]
        c, b = st["copies"][j]
        c += st["base"]
        p, size = pos[d], sizes[d]
        last = all(sizes[e] == 1 for e in tree[j + 1:])
        left = [e for e in cur.free() if e != d]

        def store(total):
            outs[a][:, pl.ds(lo, n)] = total

        if what[0] == "swap":
            buf = st["bufs"][b]
            await_copy(buf, c)
            new = View(buf, left)
            accumulate(sizes, store if last else new, [cur.fix(d, p), new])
            st["cur"] = new
            launch(pi, j + 1)
        elif what[0] in ("up", "down"):
            up = what[0] == "up"
            here, t = what[2], what[3]
            sem = c + t if up else c + size + t
            buf = st["bufs"][b if up else b + 1]

            def relay():
                await_copy(buf.at[t], sem)
                new = View(buf, [d] + left, {d: t})
                accumulate(sizes, new, [cur.fix(d, t), new])

            when([p == here], relay)
            send([p == here], buf.at[t], buf.at[t], sem, place.device({**pos, d: p + 1 if up else p - 1}, core))
        else:
            ups, downs = st["bufs"][b], st["bufs"][b + 1]
            new = cur.fix(d, p)
            below, above = View(ups, [d] + left, {d: p}), View(downs, [d] + left, {d: p})
            for p_below, p_above, conds in ((False, True, [p == 0]), (True, True, [p > 0, p < size - 1]), (True, False, [p == size - 1])):
                def land(p_below=p_below, p_above=p_above):
                    terms = [new]
                    if p_below:
                        await_copy(ups.at[p], c + p)
                        terms.append(below)
                    if p_above:
                        await_copy(downs.at[p], c + size + p)
                        terms.append(above)
                    accumulate(sizes, store if last else new, terms)
                when(conds, land)
            st["cur"] = new
            launch(pi, j + 1)

    for pi, what in order:
        run(pi, what)
    for conds, c in sent:
        when(conds, c.wait_send)


def reduce_pieces(shapes):
    kinds = itertools.cycle(("xzy", "yzx", "xyz", "xzy", "yzx", "yxz", "xzy", "yzx"))
    pieces = []
    for a, (rows, cols) in enumerate(shapes):
        width = min(cols, max(128, 18432 // rows // 128 * 128))
        while cols % width:
            width -= 128
        pieces += [(a, lo, width) for lo in range(0, cols, width)]
    return [(a, next(kinds), lo, n) for a, lo, n in pieces]


def reduce_scatter(sizes, parts, alpha=0.5):
    shapes = [p.shape[-2:] for p in parts]
    pieces = reduce_pieces(shapes)
    ev = []
    for pi, (a, tree, lo, n) in enumerate(pieces):
        ev += [(pi * alpha + t, pi, what) for t, what in piece_events(sizes, tree)]
    ev.sort(key=lambda e: (e[0], e[1]))
    order = [(pi, what) for _, pi, what in ev]
    buffers, copies = [], 0
    for piece in pieces:
        rows = shapes[piece[0]][0]
        buffers += [pltpu.VMEM(s, parts[piece[0]].dtype) for s in piece_buffers(sizes, piece, rows)]
        copies += piece_copies(sizes, piece[1])
    n_in = len(parts)
    return pl.pallas_call(
        functools.partial(reduce_kernel, sizes, pieces, order, n_in),
        out_shape=[jax.ShapeDtypeStruct(s, jnp.float32) for s in shapes],
        in_specs=[pl.BlockSpec(memory_space=pltpu.VMEM)] * n_in,
        out_specs=[pl.BlockSpec(memory_space=pltpu.VMEM)] * n_in,
        scratch_shapes=buffers + [pltpu.SemaphoreType.DMA((copies,)), pltpu.SemaphoreType.DMA((copies,))],
        compiler_params=pltpu.CompilerParams(collective_id=1, has_side_effects=True, vmem_limit_bytes=67000000),
        name="reduce",
    )(*parts)


HEAD_DIM = 64
PASSES = 4


epsilon = 1e-05
score_scale = 0.125
gelu_coef = 0.7978845608028654


def layer_norm(values, gain, shift):
    centre = values - jnp.mean(values, axis=-1, keepdims=True)
    spread = jnp.mean(centre * centre, axis=-1, keepdims=True)
    return centre * lax.rsqrt(spread + epsilon) * gain + shift


def gelu_tanh(values):
    return (
        0.5 * values * (1.0 + jnp.tanh(gelu_coef * (values + 0.044715 * values * values * values)))
    )


def fetch_attention(ln1_gain, ln1_bias, qkv_weight, qv_bias, out_weight, out_bias):
    return (
        lax.all_gather(ln1_gain, ("dp", "fsdp"), axis=0, tiled=True),
        lax.all_gather(ln1_bias, ("dp", "fsdp"), axis=0, tiled=True),
        lax.all_gather(qkv_weight, ("dp", "fsdp"), axis=0, tiled=True),
        lax.all_gather(qv_bias, ("dp", "fsdp"), axis=0, tiled=True),
        lax.all_gather(out_weight, ("dp", "fsdp"), axis=0, tiled=True),
        lax.all_gather(out_bias, ("dp", "fsdp"), axis=0, tiled=True),
    )


def fetch_mlp(ln2_gain, ln2_bias, fc_weight, fc_bias, proj_weight, proj_bias):
    return (
        lax.all_gather(ln2_gain, ("dp", "fsdp"), axis=0, tiled=True),
        lax.all_gather(ln2_bias, ("dp", "fsdp"), axis=0, tiled=True),
        lax.all_gather(fc_weight, ("dp", "fsdp"), axis=0, tiled=True),
        lax.all_gather(fc_bias, ("dp", "fsdp"), axis=0, tiled=True),
        lax.all_gather(proj_weight, ("dp", "fsdp"), axis=0, tiled=True),
        lax.all_gather(proj_bias, ("dp", "fsdp"), axis=0, tiled=True),
    )


def fetch_all(sizes, attention, mlp):
    ln1_gain, ln1_bias, qkv_weight, qv_bias, out_weight, out_bias = attention
    ln2_gain, ln2_bias, fc_weight, fc_bias, proj_weight, proj_bias = mlp
    big = (qkv_weight, out_weight, fc_weight, proj_weight)
    small = (ln1_gain, ln1_bias, qv_bias, out_bias, ln2_gain, ln2_bias, fc_bias, proj_bias)
    width = -(-sum(v.shape[0] for v in small) // 1024) * 128
    if any(w.shape[0] % 8 for w in big):
        return fetch_attention(*attention), fetch_mlp(*mlp)
    packed = jnp.concatenate(small)
    packed = jnp.pad(packed, (0, 8 * width - packed.shape[0])).reshape(8, width)
    *full, rows = gather(sizes, (*big, packed))
    qkv_full, out_full, fc_full, proj_full = [w.reshape(-1, w.shape[-1]) for w in full]
    rows = rows.reshape(-1, 8 * width)
    vectors, start = [], 0
    for v in small:
        vectors.append(rows[:, start : start + v.shape[0]].reshape(-1))
        start += v.shape[0]
    g1, b1, qv, ob, g2, b2, fb, pb = vectors
    return (g1, b1, qkv_full, qv, out_full, ob), (g2, b2, fc_full, fb, proj_full, pb)


def scatter_all(terms):
    return tuple(lax.psum_scatter(v, ("dp", "fsdp"), scatter_dimension=0, tiled=True) for v in terms)


def sum_all(sizes, attention, mlp):
    gain_one, shift_one, qkv_w, qv_b, out_w, out_b = attention
    gain_two, shift_two, fc_w, fc_b, proj_w, proj_b = mlp
    chips = sizes["x"] * sizes["y"] * sizes["z"]
    big = (qkv_w, out_w, fc_w, proj_w)
    small = (gain_one, shift_one, qv_b, out_b, gain_two, shift_two, fc_b, proj_b)
    if any(w.shape[0] % (16 * chips) for w in big):
        return scatter_all(attention), scatter_all(mlp)
    lead = (sizes["x"], 2, sizes["z"], sizes["y"])
    rows = jnp.concatenate([v.reshape(2 * chips, -1) for v in small], axis=1)
    width = -(-rows.shape[1] // 1024) * 128
    rows = jnp.pad(rows, ((0, 0), (0, 8 * width - rows.shape[1])))
    parts = [w.astype(jnp.bfloat16).reshape(*lead, -1, w.shape[1]) for w in big]
    parts.append(rows.reshape(*lead, 8, width))
    qkv, out, fc, proj, packed = reduce_scatter(sizes, parts)
    packed, vectors, start = packed.reshape(-1), [], 0
    for v in small:
        n = v.shape[0] // (2 * chips)
        vectors.append(packed[start : start + n])
        start += n
    g1, b1, qv, ob, g2, b2, fb, pb = vectors
    return (g1, b1, qkv, qv, out, ob), (g2, b2, fc, fb, proj, pb)


def allowed_rows(key_valid, block_rows, seq_len):
    query_pos = jnp.arange(block_rows, dtype=jnp.int32)[:, None]
    key_pos = jnp.arange(seq_len, dtype=jnp.int32)[None, :]
    return (key_pos <= query_pos) & (key_valid[:, None, :] | (key_pos == query_pos))


def attend_forward(queries, key_rows, values, key_valid):
    seq_len = queries.shape[1]
    block_rows = min(512, seq_len)
    scores = (
        jnp.einsum("gqhd,gkhd->ghqk", queries, key_rows, preferred_element_type=jnp.float32)
        * score_scale
    )
    allowed = allowed_rows(key_valid, block_rows, seq_len)[:, None]
    scores = jnp.where(allowed, scores, -1e30)
    row_max = jnp.max(scores, axis=-1, keepdims=True)
    expo = jnp.exp(scores - row_max)
    row_total = jnp.sum(expo, axis=-1, keepdims=True)
    probs = (expo / row_total).astype(jnp.bfloat16)
    outputs = jnp.einsum("ghqk,gkhd->gqhd", probs, values, preferred_element_type=jnp.float32)
    totals = (row_max + jnp.log(row_total))[..., 0]
    return (outputs, totals)


def attend_backward(queries, key_rows, values, log_totals, grad_mixed, key_valid):
    seq_len = queries.shape[1]
    block_rows = min(512, seq_len)
    scores = (
        jnp.einsum("gqhd,gkhd->ghqk", queries, key_rows, preferred_element_type=jnp.float32)
        * score_scale
    )
    allowed = allowed_rows(key_valid, block_rows, seq_len)[:, None]
    block_totals = log_totals[:, :, 0:block_rows, None]
    probs = jnp.where(allowed, jnp.exp(scores - block_totals), 0.0)
    probs_low = probs.astype(jnp.bfloat16)
    grad_values = jnp.einsum(
        "ghqk,gqhd->gkhd", probs_low, grad_mixed, preferred_element_type=jnp.float32
    )
    grad_probs = jnp.einsum(
        "gqhd,gkhd->ghqk", grad_mixed, values, preferred_element_type=jnp.float32
    )
    inner = jnp.sum(grad_probs * probs, axis=-1, keepdims=True)
    grad_scores = (probs * (grad_probs - inner)).astype(jnp.bfloat16)
    grad_queries = (
        jnp.einsum("ghqk,gkhd->gqhd", grad_scores, key_rows, preferred_element_type=jnp.float32)
        * score_scale
    )
    grad_keys = (
        jnp.einsum("ghqk,gqhd->gkhd", grad_scores, queries, preferred_element_type=jnp.float32)
        * score_scale
    )
    return (grad_queries, grad_keys, grad_values)


def forward_pass(state, weights, key_valid, live, seq_count, seq_len):
    (gain_one, shift_one, qkv_w, qv_b, out_w, out_b), (
        gain_two,
        shift_two,
        fc_w,
        fc_b,
        proj_w,
        proj_b,
    ) = weights
    row_count, model_width = state.shape
    head_count = model_width // HEAD_DIM
    normed = layer_norm(state, gain_one.astype(jnp.float32), shift_one.astype(jnp.float32)).astype(
        jnp.bfloat16
    )
    qv_float = qv_b.astype(jnp.float32)
    bias_full = jnp.concatenate(
        [qv_float[:model_width], jnp.zeros((model_width,), jnp.float32), qv_float[model_width:]]
    )
    joined = (jnp.dot(normed, qkv_w, preferred_element_type=jnp.float32) + bias_full).astype(
        jnp.bfloat16
    )
    split = joined.reshape(seq_count, seq_len, 3, head_count, HEAD_DIM)
    queries = split[:, :, 0]
    key_rows = split[:, :, 1]
    values = split[:, :, 2]
    mixed_float, log_totals = attend_forward(queries, key_rows, values, key_valid)
    mixed = mixed_float.reshape(row_count, model_width).astype(jnp.bfloat16)
    middle = (
        state
        + jnp.dot(mixed, out_w, preferred_element_type=jnp.float32)
        + out_b.astype(jnp.float32)
    )
    normed_two = layer_norm(
        middle, gain_two.astype(jnp.float32), shift_two.astype(jnp.float32)
    ).astype(jnp.bfloat16)
    upper = jnp.dot(normed_two, fc_w, preferred_element_type=jnp.float32) + fc_b.astype(jnp.float32)
    activated = gelu_tanh(upper).astype(jnp.bfloat16)
    result = (
        middle
        + jnp.dot(activated, proj_w, preferred_element_type=jnp.float32)
        + proj_b.astype(jnp.float32)
    )
    record = (
        state,
        normed,
        queries,
        key_rows,
        values,
        log_totals,
        mixed,
        middle,
        normed_two,
        upper,
        activated,
    )
    return (jnp.where(live, result, state), record)


def backward_mlp(grad_next, record, weights, live):
    (
        state,
        normed,
        queries,
        key_rows,
        values,
        log_totals,
        mixed,
        middle,
        normed_two,
        upper,
        activated,
    ) = record
    (gain_one, shift_one, qkv_w, qv_b, out_w, out_b), (
        gain_two,
        shift_two,
        fc_w,
        fc_b,
        proj_w,
        proj_b,
    ) = weights
    grad_out = jnp.where(live, grad_next, 0.0)
    grad_branch = grad_out.astype(jnp.bfloat16)
    term_proj_b = jnp.sum(grad_branch.astype(jnp.float32), axis=0)
    term_proj_w = jnp.einsum(
        "ti,to->io", activated, grad_branch, preferred_element_type=jnp.float32
    )
    grad_act = jnp.einsum("to,io->ti", grad_branch, proj_w, preferred_element_type=jnp.float32)
    gelu_pull = jax.vjp(gelu_tanh, upper)[1]
    grad_upper = gelu_pull(grad_act)[0].astype(jnp.bfloat16)
    term_fc_b = jnp.sum(grad_upper.astype(jnp.float32), axis=0)
    term_fc_w = jnp.einsum("td,tf->df", normed_two, grad_upper, preferred_element_type=jnp.float32)
    grad_normed_two = jnp.einsum("tf,df->td", grad_upper, fc_w, preferred_element_type=jnp.float32)
    norm_pull_two = jax.vjp(
        layer_norm, middle, gain_two.astype(jnp.float32), shift_two.astype(jnp.float32)
    )[1]
    grad_mid_norm, term_gain_two, term_shift_two = norm_pull_two(grad_normed_two)
    grad_middle = grad_out + grad_mid_norm
    mlp_terms = (term_gain_two, term_shift_two, term_fc_w, term_fc_b, term_proj_w, term_proj_b)
    return (grad_middle, mlp_terms)


def backward_attention(grad_next, grad_middle, record, weights, key_valid, live):
    (
        state,
        normed,
        queries,
        key_rows,
        values,
        log_totals,
        mixed,
        middle,
        normed_two,
        upper,
        activated,
    ) = record
    (gain_one, shift_one, qkv_w, qv_b, out_w, out_b), mlp_weights = weights
    row_count, model_width = state.shape
    grad_attn = grad_middle.astype(jnp.bfloat16)
    term_out_b = jnp.sum(grad_attn.astype(jnp.float32), axis=0)
    term_out_w = jnp.einsum("td,te->de", mixed, grad_attn, preferred_element_type=jnp.float32)
    grad_mixed = jnp.einsum(
        "te,de->td", grad_attn, out_w, preferred_element_type=jnp.float32
    ).astype(jnp.bfloat16)
    grad_mixed = grad_mixed.reshape(queries.shape)
    grad_queries, grad_keys, grad_values = attend_backward(
        queries, key_rows, values, log_totals, grad_mixed, key_valid
    )
    grad_joined = (
        jnp.stack([grad_queries, grad_keys, grad_values], axis=2)
        .reshape(row_count, 3 * model_width)
        .astype(jnp.bfloat16)
    )
    column_sums = jnp.sum(grad_joined.astype(jnp.float32), axis=0)
    term_qv_b = jnp.concatenate([column_sums[:model_width], column_sums[2 * model_width :]])
    term_qkv_w = jnp.einsum("td,tk->dk", normed, grad_joined, preferred_element_type=jnp.float32)
    grad_normed = jnp.einsum("tk,dk->td", grad_joined, qkv_w, preferred_element_type=jnp.float32)
    norm_pull_one = jax.vjp(
        layer_norm, state, gain_one.astype(jnp.float32), shift_one.astype(jnp.float32)
    )[1]
    grad_state_norm, term_gain_one, term_shift_one = norm_pull_one(grad_normed)
    grad_prev = grad_middle + grad_state_norm + jnp.where(live, 0.0, grad_next)
    attention_terms = (term_gain_one, term_shift_one, term_qkv_w, term_qv_b, term_out_w, term_out_b)
    return (grad_prev, attention_terms)


def body(
    sizes,
    hidden,
    sections,
    lengths,
    token_mask,
    cotangent,
    ln1_gain,
    ln1_bias,
    qkv_weight,
    qv_bias,
    out_weight,
    out_bias,
    ln2_gain,
    ln2_bias,
    fc_weight,
    fc_bias,
    proj_weight,
    proj_bias,
):
    seq_count, seq_len, model_width = hidden.shape
    row_count = seq_count * seq_len
    key_pos = jnp.arange(seq_len, dtype=jnp.int32)
    key_valid = (key_pos[None, :] < lengths[:, None]) & (token_mask == 1)

    current = fetch_all(
        sizes,
        (ln1_gain, ln1_bias, qkv_weight, qv_bias, out_weight, out_bias),
        (ln2_gain, ln2_bias, fc_weight, fc_bias, proj_weight, proj_bias),
    )

    state = hidden.reshape(row_count, model_width).astype(jnp.float32)
    records = []
    for section_index in range(PASSES):
        live = jnp.repeat(sections >= section_index, seq_len)[:, None]
        state, record = forward_pass(state, current, key_valid, live, seq_count, seq_len)
        records.append(record)
    hidden_out = state.astype(jnp.bfloat16).reshape(seq_count, seq_len, model_width)
    grad_state = cotangent.reshape(row_count, model_width).astype(jnp.float32)
    attention_sum = None
    mlp_sum = None
    for section_index in reversed(range(PASSES)):
        live = jnp.repeat(sections >= section_index, seq_len)[:, None]
        grad_middle, mlp_terms = backward_mlp(grad_state, records[section_index], current, live)
        if mlp_sum is None:
            mlp_sum = mlp_terms
        else:
            mlp_sum = jax.tree.map(jnp.add, mlp_sum, mlp_terms)
        grad_state, attention_terms = backward_attention(
            grad_state, grad_middle, records[section_index], current, key_valid, live
        )
        if attention_sum is None:
            attention_sum = attention_terms
        else:
            attention_sum = jax.tree.map(jnp.add, attention_sum, attention_terms)
    attention_grads, finished = sum_all(sizes, attention_sum, mlp_sum)
    grad_hidden = grad_state.reshape(seq_count, seq_len, model_width)
    return (
        hidden_out,
        grad_hidden,
        attention_grads[0],
        attention_grads[1],
        attention_grads[2],
        attention_grads[3],
        attention_grads[4],
        attention_grads[5],
        finished[0],
        finished[1],
        finished[2],
        finished[3],
        finished[4],
        finished[5],
    )


def solution(mesh):
    chips_x = mesh.shape["dp"] // 2
    sizes = {"x": chips_x, "y": chips_x, "z": mesh.shape["fsdp"] // chips_x}
    return jax.shard_map(
        functools.partial(body, sizes),
        mesh=mesh,
        in_specs=(
            P(("dp", "fsdp"), None, None),
            P(("dp", "fsdp")),
            P(("dp", "fsdp")),
            P(("dp", "fsdp"), None),
            P(("dp", "fsdp"), None, None),
            P(("dp", "fsdp")),
            P(("dp", "fsdp")),
            P(("dp", "fsdp"), None),
            P(("dp", "fsdp")),
            P(("dp", "fsdp"), None),
            P(("dp", "fsdp")),
            P(("dp", "fsdp")),
            P(("dp", "fsdp")),
            P(("dp", "fsdp"), None),
            P(("dp", "fsdp")),
            P(("dp", "fsdp"), None),
            P(("dp", "fsdp")),
        ),
        out_specs=(
            P(("dp", "fsdp"), None, None),
            P(("dp", "fsdp"), None, None),
            P(("dp", "fsdp")),
            P(("dp", "fsdp")),
            P(("dp", "fsdp"), None),
            P(("dp", "fsdp")),
            P(("dp", "fsdp"), None),
            P(("dp", "fsdp")),
            P(("dp", "fsdp")),
            P(("dp", "fsdp")),
            P(("dp", "fsdp"), None),
            P(("dp", "fsdp")),
            P(("dp", "fsdp"), None),
            P(("dp", "fsdp")),
        ),
        check_vma=False,
    )
```

```python
import functools
import itertools

import jax
import jax.numpy as jnp
from jax import lax
from jax.experimental import pallas as pl
from jax.experimental.pallas import tpu as pltpu
from jax.sharding import PartitionSpec as P
MESH = pl.DeviceIdType.MESH

TREES = ("zyx", "zxy", "xyz")


def offsets(length):
    return [0, "o"] if length == 2 else list(range(-(length - 1), length))


class Place:
    def __init__(self, sizes):
        self.sizes = sizes
        dp, fs = lax.axis_index("dp"), lax.axis_index("fsdp")
        self.core = lax.rem(dp, 2)
        self.pos = {"x": dp // 2, "z": fs // sizes["y"], "y": lax.rem(fs, sizes["y"])}

    def device(self, pos, core):
        return (pos["x"] * 2 + core, pos["z"] * self.sizes["y"] + pos["y"])

    def index(self, pos, core):
        dp, fs = self.device(pos, core)
        return dp * (self.sizes["z"] * self.sizes["y"]) + fs

    def chip(self, pos):
        return (pos["x"] * self.sizes["z"] + pos["z"]) * self.sizes["y"] + pos["y"]

    def neighbours(self):
        out = [(None, self.device(self.pos, 1 - self.core))]
        for d, length in self.sizes.items():
            if length == 2:
                out.append((None, self.device({**self.pos, d: 1 - self.pos[d]}, self.core)))
            elif length > 2:
                for s in (1, -1):
                    q = self.pos[d] + s
                    out.append(((q >= 0) & (q < length), self.device({**self.pos, d: q}, self.core)))
        return out


def when(conds, fn):
    conds = [c for c in conds if c is not None]
    if not conds:
        fn()
    else:
        pl.when(functools.reduce(jnp.logical_and, conds))(lambda: (fn(), None)[1])


def entry_barrier(place):
    barrier = pltpu.get_barrier_semaphore()
    total = 0
    for cond, dev in place.neighbours():
        when([cond], lambda dev=dev: pl.semaphore_signal(barrier, inc=1, device_id=dev, device_id_type=MESH))
        total = total + (1 if cond is None else cond.astype(jnp.int32))
    pl.semaphore_wait(barrier, total)


def gather_kernel(sizes, pieces, order, n_in, *refs):
    ins, outs = refs[:n_in], refs[n_in:2 * n_in]
    send_sem, recv_sem, pair_send, pair_recv, local_sem = refs[2 * n_in:]
    place = Place(sizes)
    pos, core = place.pos, place.core
    entry_barrier(place)
    partner = place.device(pos, 1 - core)
    locals_ = []
    for a in range(n_in):
        c = pltpu.make_async_copy(ins[a], outs[a].at[pos["x"], core, pos["z"], pos["y"]], local_sem.at[a])
        c.start()
        locals_.append(c)

    def part(pi, at, who):
        a, tree, lo, n = pieces[pi]
        return outs[a].at[at["x"], who, at["z"], at["y"], pl.ds(lo, n)]

    def remote(src, dst, send, recv, dev):
        return pltpu.make_async_remote_copy(src_ref=src, dst_ref=dst, send_sem=send, recv_sem=recv, device_id=dev, device_id_type=MESH)

    def line(d):
        if sizes[d] == 1:
            return []
        if sizes[d] == 2:
            return [(0, None, 1 - pos[d])]
        return [(0, pos[d] + 1 < sizes[d], pos[d] + 1), (1, pos[d] > 0, pos[d] - 1)]

    left = {}
    for pi, t in order:
        left[pi] = left.get(pi, 0) + 1
    seen = dict.fromkeys(left, 0)
    whole = [slice(None)] * 3
    for pi, t in order:
        a, tree, lo, n = pieces[pi]
        own = all(v == 0 for v in t)
        at, conds = dict(pos), []
        for d, v in zip(tree, t):
            if v == "o":
                at[d] = 1 - pos[d]
            elif v != 0:
                at[d] = pos[d] + v
                conds.append((at[d] >= 0) if v < 0 else (at[d] < sizes[d]))
        chip = place.chip(at)
        dst = part(pi, at, core)
        src = ins[a].at[pl.ds(lo, n)] if own else dst
        k = max([j for j, v in enumerate(t) if v != 0], default=-1)

        def handle(tree=tree, t=t, own=own, chip=chip, dst=dst, src=src, k=k, pi=pi):
            if not own:
                remote(dst, dst, pair_send.at[pi], recv_sem.at[pi, chip], partner).wait_recv()
            for j in (2, 1, 0):
                d = tree[j]
                if j < k:
                    continue
                for slot, ok, q in line(d):
                    if j == k and (t[j] == "o" or (t[j] < 0) != (slot == 0)):
                        continue
                    when([ok], remote(src, dst, send_sem.at[pi, 2 * "xyz".index(d) + slot], recv_sem.at[pi, chip],
                                      place.device({**pos, d: q}, core)).start)
            remote(src, dst, pair_send.at[pi], pair_recv.at[pi], partner).start()
        when(conds, handle)
        seen[pi] += 1

    full = dict.fromkeys("xyz", slice(None))
    for pi, (a, tree, lo, n) in enumerate(pieces):
        for j, d in enumerate(tree):
            at = {e: (slice(None) if tree.index(e) < j else pos[e]) for e in "xyz"}
            for slot, ok, q in line(d):
                sem = send_sem.at[pi, 2 * "xyz".index(d) + slot]
                if sizes[d] == 2:
                    ref = part(pi, at, core)
                    remote(ref, ref, sem, recv_sem.at[pi, 0], partner).wait_send()
                else:
                    for z in range(sizes[d]):
                        ref = part(pi, {**at, d: z}, core)
                        sent = (pos[d] >= z) if slot == 0 else (pos[d] <= z)
                        when([ok, sent], remote(ref, ref, sem, recv_sem.at[pi, 0], partner).wait_send)
        ref = part(pi, full, core)
        remote(ref, ref, pair_send.at[pi], pair_recv.at[pi], partner).wait_send()
        ref = part(pi, full, 1 - core)
        remote(ref, ref, pair_send.at[pi], pair_recv.at[pi], partner).wait_recv()
    for c in locals_:
        c.wait()


def gather_order(sizes, pieces, alpha):
    ev = []
    for pi, (a, tree, lo, n) in enumerate(pieces):
        for t in itertools.product(*[offsets(sizes[d]) for d in tree]):
            hops = sum(1 if v == "o" else abs(v) for v in t)
            ev.append((pi * alpha + hops, pi, t))
    ev.sort(key=lambda e: (e[0], e[1]))
    return [(pi, t) for _, pi, t in ev]


def gather(sizes, shards, alpha=0.05):
    chips = sizes["x"] * sizes["y"] * sizes["z"]
    pieces = []
    for a, s in enumerate(shards):
        tiles = s.shape[0] // 8
        if tiles % 3 == 0 and tiles < 12:
            cuts = [(i, i * tiles // 3, tiles // 3) for i in range(3)]
        elif tiles % 2 == 0:
            cuts = [(i, i * tiles // 2, tiles // 2) for i in range(2)]
        else:
            cuts = [(2, 0, tiles)]
        for tree, lo, n in cuts:
            pieces.append((a, TREES[tree], lo * 8, n * 8))
    order = gather_order(sizes, pieces, alpha)
    n_in = len(shards)
    return pl.pallas_call(
        functools.partial(gather_kernel, sizes, pieces, order, n_in),
        out_shape=[jax.ShapeDtypeStruct((sizes["x"], 2, sizes["z"], sizes["y"]) + s.shape, s.dtype) for s in shards],
        in_specs=[pl.BlockSpec(memory_space=pltpu.VMEM)] * n_in,
        out_specs=[pl.BlockSpec(memory_space=pl.ANY)] * n_in,
        scratch_shapes=[
            pltpu.SemaphoreType.DMA((len(pieces), 6)),
            pltpu.SemaphoreType.DMA((len(pieces), chips)),
            pltpu.SemaphoreType.DMA((len(pieces),)),
            pltpu.SemaphoreType.DMA((len(pieces),)),
            pltpu.SemaphoreType.DMA((n_in,)),
        ],
        compiler_params=pltpu.CompilerParams(collective_id=0, has_side_effects=True),
        name="gather",
    )(*shards)


class View:
    def __init__(self, ref, dims, fixed=None, core=None):
        self.ref, self.dims, self.fixed, self.core = ref, dims, fixed or {}, core

    def fix(self, d, v):
        return View(self.ref, self.dims, {**self.fixed, d: v}, self.core)

    def free(self):
        return [d for d in self.dims if d not in self.fixed]

    def index(self, at, cols=None):
        idx = [self.fixed.get(d, at.get(d, slice(None))) for d in self.dims]
        if self.core is not None:
            core, lo, n = self.core
            return (idx[0], core, *idx[1:], slice(None), pl.ds(lo, n))
        return tuple(idx)

    def whole(self):
        return self.ref.at[self.index({})]


def accumulate(sizes, dst, terms):
    dims = terms[0].free()

    def step(i, carry):
        at = {}
        for d in reversed(dims):
            at[d] = lax.rem(i, sizes[d])
            i = i // sizes[d]
        total = None
        for t in terms:
            v = t.ref[t.index(at)].astype(jnp.float32)
            total = v if total is None else total + v
        if isinstance(dst, View):
            dst.ref[dst.index(at)] = total.astype(dst.ref.dtype)
        else:
            dst(total)
        return carry

    count = 1
    for d in dims:
        count *= sizes[d]
    if count == 1:
        step(0, 0)
    else:
        lax.fori_loop(0, count, step, 0)


def piece_buffers(sizes, piece, rows):
    a, tree, lo, n = piece
    dims = list("xzy")
    shapes = [tuple(sizes[d] for d in dims) + (rows, n)]
    for d in tree:
        dims.remove(d)
        rest = tuple(sizes[e] for e in dims) + (rows, n)
        if sizes[d] == 2:
            shapes.append(rest)
        elif sizes[d] > 2:
            shapes += [(sizes[d],) + rest] * 2
    return shapes


def piece_copies(sizes, tree):
    return 1 + sum(0 if sizes[d] == 1 else 1 if sizes[d] == 2 else 2 * sizes[d] for d in tree)


def piece_events(sizes, tree):
    ev, t = [(0.0, ("pair",))], 0.0
    for j, d in enumerate(tree):
        if sizes[d] == 2:
            t += 1
            ev.append((t, ("swap", j)))
        elif sizes[d] > 2:
            for hop in range(1, sizes[d]):
                for far in range(hop, sizes[d] - 1):
                    dest = sizes[d] - 1 - (far - hop)
                    if dest > hop:
                        ev.append((t + hop + (far - hop) * 0.2, ("up", j, hop, dest)))
                        ev.append((t + hop + (far - hop) * 0.2, ("down", j, sizes[d] - 1 - hop, sizes[d] - 1 - dest)))
            t += sizes[d] - 1
            ev.append((t, ("land", j)))
    return ev


def reduce_kernel(sizes, pieces, order, n_in, *refs):
    ins, outs, rest = refs[:n_in], refs[n_in:2 * n_in], list(refs[2 * n_in:])
    send_sem, recv_sem = rest[-2:]
    place = Place(sizes)
    pos, core = place.pos, place.core
    partner = place.device(pos, 1 - core)
    state, base, sent = [], 0, []
    for pi, (a, tree, lo, n) in enumerate(pieces):
        k = len(piece_buffers(sizes, pieces[pi], 8))
        bufs, rest = rest[:k], rest[k:]
        copies = {"pair": (0, 0)}
        c, b = 1, 1
        for j, d in enumerate(tree):
            if sizes[d] > 1:
                copies[j] = (c, b)
                c += 1 if sizes[d] == 2 else 2 * sizes[d]
                b += 1 if sizes[d] == 2 else 2
        state.append({"bufs": bufs, "base": base, "copies": copies, "cur": None})
        base += c

    def copy(src, dst, sem, dev):
        return pltpu.make_async_remote_copy(src_ref=src, dst_ref=dst, send_sem=send_sem.at[sem], recv_sem=recv_sem.at[sem], device_id=dev, device_id_type=MESH)

    def send(conds, src, dst, sem, dev):
        c = copy(src, dst, sem, dev)
        when(conds, c.start)
        sent.append((conds, c))

    def await_copy(buf, sem):
        copy(buf, buf, sem, partner).wait_recv()

    entry_barrier(place)
    for pi, (a, tree, lo, n) in enumerate(pieces):
        src = View(ins[a], list("xzy"), core=(1 - core, lo, n))
        send([], src.whole(), state[pi]["bufs"][0], state[pi]["base"], partner)

    def launch(pi, j):
        a, tree, lo, n = pieces[pi]
        st = state[pi]
        while j < 3 and sizes[tree[j]] == 1:
            st["cur"] = st["cur"].fix(tree[j], 0)
            j += 1
        if j == 3:
            return
        d, cur = tree[j], st["cur"]
        c, b = st["copies"][j]
        c += st["base"]
        p, size = pos[d], sizes[d]
        if size == 2:
            send([], cur.fix(d, 1 - p).whole(), st["bufs"][b], c, place.device({**pos, d: 1 - p}, core))
            return
        for t in range(size - 1, 0, -1):
            send([p == 0], cur.fix(d, t).whole(), st["bufs"][b].at[t], c + t, place.device({**pos, d: p + 1}, core))
            t = size - 1 - t
            send([p == size - 1], cur.fix(d, t).whole(), st["bufs"][b + 1].at[t], c + size + t, place.device({**pos, d: p - 1}, core))

    def run(pi, what):
        a, tree, lo, n = pieces[pi]
        st = state[pi]
        if what[0] == "pair":
            buf = st["bufs"][0]
            await_copy(buf, st["base"])
            mine = View(ins[a], list("xzy"), core=(core, lo, n))
            st["cur"] = View(buf, list("xzy"))
            accumulate(sizes, st["cur"], [st["cur"], mine])
            launch(pi, 0)
            return
        j = what[1]
        d, cur = tree[j], st["cur"]
        c, b = st["copies"][j]
        c += st["base"]
        p, size = pos[d], sizes[d]
        last = all(sizes[e] == 1 for e in tree[j + 1:])
        left = [e for e in cur.free() if e != d]

        def store(total):
            outs[a][:, pl.ds(lo, n)] = total

        if what[0] == "swap":
            buf = st["bufs"][b]
            await_copy(buf, c)
            new = View(buf, left)
            accumulate(sizes, store if last else new, [cur.fix(d, p), new])
            st["cur"] = new
            launch(pi, j + 1)
        elif what[0] in ("up", "down"):
            up = what[0] == "up"
            here, t = what[2], what[3]
            sem = c + t if up else c + size + t
            buf = st["bufs"][b if up else b + 1]

            def relay():
                await_copy(buf.at[t], sem)
                new = View(buf, [d] + left, {d: t})
                accumulate(sizes, new, [cur.fix(d, t), new])

            when([p == here], relay)
            send([p == here], buf.at[t], buf.at[t], sem, place.device({**pos, d: p + 1 if up else p - 1}, core))
        else:
            ups, downs = st["bufs"][b], st["bufs"][b + 1]
            new = cur.fix(d, p)
            below, above = View(ups, [d] + left, {d: p}), View(downs, [d] + left, {d: p})
            for p_below, p_above, conds in ((False, True, [p == 0]), (True, True, [p > 0, p < size - 1]), (True, False, [p == size - 1])):
                def land(p_below=p_below, p_above=p_above):
                    terms = [new]
                    if p_below:
                        await_copy(ups.at[p], c + p)
                        terms.append(below)
                    if p_above:
                        await_copy(downs.at[p], c + size + p)
                        terms.append(above)
                    accumulate(sizes, store if last else new, terms)
                when(conds, land)
            st["cur"] = new
            launch(pi, j + 1)

    for pi, what in order:
        run(pi, what)
    for conds, c in sent:
        when(conds, c.wait_send)


def reduce_pieces(shapes):
    kinds = itertools.cycle(("xzy", "yzx", "xyz", "xzy", "yzx", "yxz", "xzy", "yzx"))
    pieces = []
    for a, (rows, cols) in enumerate(shapes):
        width = min(cols, max(128, 18432 // rows // 128 * 128))
        while cols % width:
            width -= 128
        pieces += [(a, lo, width) for lo in range(0, cols, width)]
    return [(a, next(kinds), lo, n) for a, lo, n in pieces]


def reduce_scatter(sizes, parts, alpha=0.5):
    shapes = [p.shape[-2:] for p in parts]
    pieces = reduce_pieces(shapes)
    ev = []
    for pi, (a, tree, lo, n) in enumerate(pieces):
        ev += [(pi * alpha + t, pi, what) for t, what in piece_events(sizes, tree)]
    ev.sort(key=lambda e: (e[0], e[1]))
    order = [(pi, what) for _, pi, what in ev]
    buffers, copies = [], 0
    for piece in pieces:
        rows = shapes[piece[0]][0]
        buffers += [pltpu.VMEM(s, parts[piece[0]].dtype) for s in piece_buffers(sizes, piece, rows)]
        copies += piece_copies(sizes, piece[1])
    n_in = len(parts)
    return pl.pallas_call(
        functools.partial(reduce_kernel, sizes, pieces, order, n_in),
        out_shape=[jax.ShapeDtypeStruct(s, jnp.float32) for s in shapes],
        in_specs=[pl.BlockSpec(memory_space=pltpu.VMEM)] * n_in,
        out_specs=[pl.BlockSpec(memory_space=pltpu.VMEM)] * n_in,
        scratch_shapes=buffers + [pltpu.SemaphoreType.DMA((copies,)), pltpu.SemaphoreType.DMA((copies,))],
        compiler_params=pltpu.CompilerParams(collective_id=1, has_side_effects=True, vmem_limit_bytes=67000000),
        name="reduce",
    )(*parts)


HEAD_DIM = 64
PASSES = 4
EPSILON = 1e-05
SCORE_SCALE = 0.125
GELU_COEF = 0.7978845608028654
GELU_CUBE = 0.044715


def dot(left, right, dims=((1,), (0,))):
    return lax.dot_general(left, right, (dims, ((), ())), preferred_element_type=jnp.float32)


NT, TN = ((1,), (1,)), ((0,), (0,))


def normalise(values):
    centre = values - jnp.mean(values, axis=-1, keepdims=True)
    scale = lax.rsqrt(jnp.mean(centre * centre, axis=-1, keepdims=True) + EPSILON)
    return centre * scale, scale


def normalise_back(grad, unit, scale):
    return scale * (grad - jnp.mean(grad, axis=-1, keepdims=True) - unit * jnp.mean(grad * unit, axis=-1, keepdims=True))


def block_kernel(chunk, sections, key_ok, hidden, cotangent, g1, b1, qkv_b, out_b, g2, b2, fc_b, proj_b,
                 qkv_hbm, out_hbm, fc_hbm, proj_hbm,
                 hidden_out, grad_hidden, a_st, o_st, c_st, g_st, dqkv_st, do_st, du_st, dm_st,
                 dg1, db1, dqkv_b, dout_b, dg2, db2, dfc_b, dproj_b,
                 qkv_w, out_w, fc_w, proj_w, state, unit1, unit2, scale1, scale2, qkv_st, prob_st, slope_st, mixed, allow, sems):
    rows, width = hidden.shape
    hidden_width = fc_w.shape[1]
    pair = 2 * HEAD_DIM
    pairs = width // pair
    loads = [pltpu.make_async_copy(src, dst, sems.at[i]) for i, (src, dst) in enumerate(
        ((qkv_hbm, qkv_w), (out_hbm, out_w), (fc_hbm, fc_w), (proj_hbm, proj_w)))]
    for c in loads:
        c.start()
    for ref in (dg1, db1, dqkv_b, dout_b, dg2, db2, dfc_b, dproj_b):
        ref[...] = jnp.zeros_like(ref)
    query = lax.broadcasted_iota(jnp.int32, (rows, 2 * rows), 0)
    key = lax.rem(lax.broadcasted_iota(jnp.int32, (rows, 2 * rows), 1), rows)
    ok = jnp.broadcast_to(key_ok[...], (rows, 2 * rows)) > 0.5
    allow[...] = jnp.where((key < query) & ok | (key == query), 1.0, 0.0)
    state[...] = hidden[...].astype(jnp.float32)
    first = lax.broadcasted_iota(jnp.int32, (rows, pair), 1) < HEAD_DIM

    def both(block):
        wide = block.astype(jnp.float32)
        return jnp.concatenate([jnp.where(first, wide, 0.0), jnp.where(first, 0.0, wide)], axis=0).astype(jnp.bfloat16)

    def merge(block):
        return jnp.where(first, block[:rows], block[rows:])

    def halves(fn, block, *others):
        return [fn(block[:, s], *(o[:, s] for o in others)) for s in (slice(0, rows), slice(rows, 2 * rows))]

    def forward(k, wait):
        x = state[...]
        unit, scale = normalise(x)
        unit1[k] = unit
        scale1[k] = jnp.broadcast_to(scale, scale1.shape[1:])
        a_st[k] = (unit * g1[...] + b1[...]).astype(jnp.bfloat16)
        if wait:
            loads[0].wait()
        for lo in range(0, 3 * width, chunk):
            cols = slice(lo, lo + chunk)
            qkv_st[k, :, cols] = (dot(a_st[k], qkv_w[:, cols]) + qkv_b[:, cols]).astype(jnp.bfloat16)
        for i in range(pairs):
            q = qkv_st[k, :, i * pair:(i + 1) * pair]
            keys = both(qkv_st[k, :, width + i * pair:width + (i + 1) * pair])
            values = both(qkv_st[k, :, 2 * width + i * pair:2 * width + (i + 1) * pair])
            scores = jnp.where(allow[...] > 0.5, dot(q, keys, NT) * SCORE_SCALE, -1e30)

            def softmax(s):
                e = jnp.exp(s - jnp.max(s, axis=-1, keepdims=True))
                return e / jnp.sum(e, axis=-1, keepdims=True)

            probs = jnp.concatenate(halves(softmax, scores), axis=1)
            prob_st[k, i] = probs
            o_st[k, :, i * pair:(i + 1) * pair] = dot(probs.astype(jnp.bfloat16), values).astype(jnp.bfloat16)
        if wait:
            loads[1].wait()
        h = x + (dot(o_st[k], out_w[...]) + out_b[...])
        unit, scale = normalise(h)
        unit2[k] = unit
        scale2[k] = jnp.broadcast_to(scale, scale2.shape[1:])
        c_st[k] = (unit * g2[...] + b2[...]).astype(jnp.bfloat16)
        if wait:
            loads[2].wait()
        for lo in range(0, hidden_width, chunk):
            cols = slice(lo, lo + chunk)
            u = dot(c_st[k], fc_w[:, cols]) + fc_b[:, cols]
            square = u * u
            t = jnp.tanh(GELU_COEF * (u + GELU_CUBE * (square * u)))
            half = 0.5 * (1.0 + t)
            g_st[k, :, cols] = (u * half).astype(jnp.bfloat16)
            slope_st[k, :, cols] = half + 0.5 * u * (1.0 - t * t) * (GELU_COEF * (1.0 + 3.0 * GELU_CUBE * square))
        if wait:
            loads[3].wait()
        y = h + (dot(g_st[k], proj_w[...]) + proj_b[...])

        @pl.when(sections[0] >= k)
        def _():
            state[...] = y

    forward(0, True)
    lax.fori_loop(1, PASSES, lambda k, c: (forward(k, False), c)[1], 0)
    hidden_out[...] = state[...].astype(jnp.bfloat16)
    state[...] = cotangent[...].astype(jnp.float32)

    def column_sums(ref, cols, block):
        ref[:, cols] += jnp.sum(block.astype(jnp.float32), axis=0, keepdims=True)

    def backward(step, carry):
        k = PASSES - 1 - step
        live = (sections[0] >= k).astype(jnp.float32)
        dx = state[...]
        dy = dx * live
        dm_st[k] = dy.astype(jnp.bfloat16)
        column_sums(dproj_b, slice(None), dm_st[k])
        for lo in range(0, hidden_width, chunk):
            cols = slice(lo, lo + chunk)
            du = (dot(dm_st[k], proj_w[cols, :], NT) * slope_st[k, :, cols]).astype(jnp.bfloat16)
            du_st[k, :, cols] = du
            column_sums(dfc_b, cols, du)
        dc = dot(du_st[k], fc_w[...], NT)
        unit = unit2[k]
        dg2[...] += jnp.sum(dc * unit, axis=0, keepdims=True)
        column_sums(db2, slice(None), dc)
        dh = dy + normalise_back(dc * g2[...], unit, scale2[k, :, 0:1])
        state[...] = dh + dx * (1.0 - live)
        do_st[k] = dh.astype(jnp.bfloat16)
        column_sums(dout_b, slice(None), do_st[k])
        mixed[...] = dot(do_st[k], out_w[...], NT).astype(jnp.bfloat16)
        for i in range(pairs):
            at = [slice(j * width + i * pair, j * width + (i + 1) * pair) for j in range(3)]
            q = qkv_st[k, :, at[0]]
            keys, values = both(qkv_st[k, :, at[1]]), both(qkv_st[k, :, at[2]])
            grad = mixed[:, at[0]]
            probs = prob_st[k, i]
            dp = dot(grad, values, NT)

            def scores_back(d, p):
                return p * (d - jnp.sum(d * p, axis=-1, keepdims=True))

            ds = jnp.concatenate(halves(scores_back, dp, probs), axis=1).astype(jnp.bfloat16)
            dv = merge(dot(probs.astype(jnp.bfloat16), grad, TN))
            dq = dot(ds, keys) * SCORE_SCALE
            dk = merge(dot(ds, q, TN)) * SCORE_SCALE
            for j, d in enumerate((dq, dk, dv)):
                dqkv_st[k, :, at[j]] = d.astype(jnp.bfloat16)
        column_sums(dqkv_b, slice(None), dqkv_st[k])
        da = dot(dqkv_st[k], qkv_w[...], NT)
        unit = unit1[k]
        dg1[...] += jnp.sum(da * unit, axis=0, keepdims=True)
        column_sums(db1, slice(None), da)
        state[...] += normalise_back(da * g1[...], unit, scale1[k, :, 0:1])
        return carry

    lax.fori_loop(0, PASSES, backward, 0)
    grad_hidden[...] = state[...]


def run_block(sections, key_valid, hidden, cotangent, attention, mlp):
    g1, b1, qkv_w, qv_b, out_w, out_b = attention
    g2, b2, fc_w, fc_b, proj_w, proj_b = mlp
    rows, width = hidden.shape
    ff = fc_w.shape[1]
    bias = jnp.concatenate([qv_b[:width], jnp.zeros_like(qv_b[:width]), qv_b[width:]])
    vectors = [v.astype(jnp.float32)[None] for v in (g1, b1, bias, out_b, g2, b2, fc_b, proj_b)]
    key_ok = jnp.concatenate([key_valid, key_valid], axis=1).astype(jnp.float32)
    low, high = jnp.bfloat16, jnp.float32
    stacks = [width, width, width, ff, 3 * width, width, ff, width]
    pairs = width // (2 * HEAD_DIM)
    vmem, everywhere = pl.BlockSpec(memory_space=pltpu.VMEM), pl.BlockSpec(memory_space=pl.ANY)
    outs = pl.pallas_call(
        functools.partial(block_kernel, 512 if ff % 512 == 0 and width * 3 % 512 == 0 else 256),
        out_shape=[jax.ShapeDtypeStruct((rows, width), low), jax.ShapeDtypeStruct((rows, width), high)]
        + [jax.ShapeDtypeStruct((PASSES, rows, n), low) for n in stacks]
        + [jax.ShapeDtypeStruct(v.shape, high) for v in vectors],
        in_specs=[pl.BlockSpec(memory_space=pltpu.SMEM)] + [vmem] * 11 + [everywhere] * 4,
        out_specs=[vmem] * 18,
        scratch_shapes=[pltpu.VMEM(w.shape, low) for w in (qkv_w, out_w, fc_w, proj_w)] + [
            pltpu.VMEM((rows, width), high),
            pltpu.VMEM((PASSES, rows, width), high),
            pltpu.VMEM((PASSES, rows, width), high),
            pltpu.VMEM((PASSES, rows, 128), high),
            pltpu.VMEM((PASSES, rows, 128), high),
            pltpu.VMEM((PASSES, rows, 3 * width), low),
            pltpu.VMEM((PASSES, pairs, rows, 2 * rows), high),
            pltpu.VMEM((PASSES, rows, ff), high),
            pltpu.VMEM((rows, width), low),
            pltpu.VMEM((rows, 2 * rows), high),
            pltpu.SemaphoreType.DMA((4,)),
        ],
        compiler_params=pltpu.CompilerParams(vmem_limit_bytes=67000000),
        name="block",
    )(sections, key_ok, hidden, cotangent, *vectors, qkv_w, out_w, fc_w, proj_w)
    hidden_out, grad_hidden = outs[:2]
    a, o, c, g, dqkv, do, du, dm = [s.reshape(PASSES * rows, -1) for s in outs[2:10]]
    dg1, db1, dbias, dout_b, dg2, db2, dfc_b, dproj_b = [v[0] for v in outs[10:]]
    dqv_b = jnp.concatenate([dbias[:width], dbias[2 * width:]])
    factors = ((a, dqkv), (o, do), (c, du), (g, dm))
    return hidden_out, grad_hidden, factors, (dg1, db1, dqv_b, dout_b, dg2, db2, dfc_b, dproj_b)


def fetch_attention(ln1_gain, ln1_bias, qkv_weight, qv_bias, out_weight, out_bias):
    return (
        lax.all_gather(ln1_gain, ("dp", "fsdp"), axis=0, tiled=True),
        lax.all_gather(ln1_bias, ("dp", "fsdp"), axis=0, tiled=True),
        lax.all_gather(qkv_weight, ("dp", "fsdp"), axis=0, tiled=True),
        lax.all_gather(qv_bias, ("dp", "fsdp"), axis=0, tiled=True),
        lax.all_gather(out_weight, ("dp", "fsdp"), axis=0, tiled=True),
        lax.all_gather(out_bias, ("dp", "fsdp"), axis=0, tiled=True),
    )


def fetch_mlp(ln2_gain, ln2_bias, fc_weight, fc_bias, proj_weight, proj_bias):
    return (
        lax.all_gather(ln2_gain, ("dp", "fsdp"), axis=0, tiled=True),
        lax.all_gather(ln2_bias, ("dp", "fsdp"), axis=0, tiled=True),
        lax.all_gather(fc_weight, ("dp", "fsdp"), axis=0, tiled=True),
        lax.all_gather(fc_bias, ("dp", "fsdp"), axis=0, tiled=True),
        lax.all_gather(proj_weight, ("dp", "fsdp"), axis=0, tiled=True),
        lax.all_gather(proj_bias, ("dp", "fsdp"), axis=0, tiled=True),
    )


def fetch_all(sizes, attention, mlp):
    ln1_gain, ln1_bias, qkv_weight, qv_bias, out_weight, out_bias = attention
    ln2_gain, ln2_bias, fc_weight, fc_bias, proj_weight, proj_bias = mlp
    big = (qkv_weight, out_weight, fc_weight, proj_weight)
    small = (ln1_gain, ln1_bias, qv_bias, out_bias, ln2_gain, ln2_bias, fc_bias, proj_bias)
    width = -(-sum(v.shape[0] for v in small) // 1024) * 128
    if any(w.shape[0] % 8 for w in big):
        return fetch_attention(*attention), fetch_mlp(*mlp)
    packed = jnp.concatenate(small)
    packed = jnp.pad(packed, (0, 8 * width - packed.shape[0])).reshape(8, width)
    *full, rows = gather(sizes, (*big, packed))
    qkv_full, out_full, fc_full, proj_full = [w.reshape(-1, w.shape[-1]) for w in full]
    rows = rows.reshape(-1, 8 * width)
    vectors, start = [], 0
    for v in small:
        vectors.append(rows[:, start : start + v.shape[0]].reshape(-1))
        start += v.shape[0]
    g1, b1, qv, ob, g2, b2, fb, pb = vectors
    return (g1, b1, qkv_full, qv, out_full, ob), (g2, b2, fc_full, fb, proj_full, pb)


def sum_all(sizes, factors, vectors):
    chips = sizes["x"] * sizes["y"] * sizes["z"]
    big = [dot(left, right, TN).astype(jnp.bfloat16) for left, right in factors]
    if any(w.shape[0] % (16 * chips) for w in big):
        qkv, out, fc, proj, *sums = [
            lax.psum_scatter(v, ("dp", "fsdp"), scatter_dimension=0, tiled=True).astype(jnp.float32) for v in (*big, *vectors)
        ]
    else:
        lead = (sizes["x"], 2, sizes["z"], sizes["y"])
        rows = jnp.concatenate([v.reshape(2 * chips, -1) for v in vectors], axis=1)
        width = -(-rows.shape[1] // 1024) * 128
        rows = jnp.pad(rows, ((0, 0), (0, 8 * width - rows.shape[1])))
        parts = [w.reshape(*lead, -1, w.shape[1]) for w in big]
        parts.append(rows.reshape(*lead, 8, width))
        qkv, out, fc, proj, packed = reduce_scatter(sizes, parts)
        packed, sums, start = packed.reshape(-1), [], 0
        for v in vectors:
            n = v.shape[0] // (2 * chips)
            sums.append(packed[start : start + n])
            start += n
    g1, b1, qv, ob, g2, b2, fb, pb = sums
    return (g1, b1, qkv, qv, out, ob), (g2, b2, fc, fb, proj, pb)


def body(
    sizes,
    hidden,
    sections,
    lengths,
    token_mask,
    cotangent,
    ln1_gain,
    ln1_bias,
    qkv_weight,
    qv_bias,
    out_weight,
    out_bias,
    ln2_gain,
    ln2_bias,
    fc_weight,
    fc_bias,
    proj_weight,
    proj_bias,
):
    seq_count, seq_len, model_width = hidden.shape
    row_count = seq_count * seq_len
    key_pos = jnp.arange(seq_len, dtype=jnp.int32)
    key_valid = (key_pos[None, :] < lengths[:, None]) & (token_mask == 1)

    current = fetch_all(
        sizes,
        (ln1_gain, ln1_bias, qkv_weight, qv_bias, out_weight, out_bias),
        (ln2_gain, ln2_bias, fc_weight, fc_bias, proj_weight, proj_bias),
    )

    hidden_out, grad_hidden, factors, vectors = run_block(
        sections, key_valid, hidden.reshape(row_count, model_width), cotangent.reshape(row_count, model_width), *current
    )
    attention_grads, finished = sum_all(sizes, factors, vectors)
    hidden_out = hidden_out.reshape(hidden.shape)
    grad_hidden = grad_hidden.reshape(hidden.shape)
    return (
        hidden_out,
        grad_hidden,
        attention_grads[0],
        attention_grads[1],
        attention_grads[2],
        attention_grads[3],
        attention_grads[4],
        attention_grads[5],
        finished[0],
        finished[1],
        finished[2],
        finished[3],
        finished[4],
        finished[5],
    )


def solution(mesh):
    chips_x = mesh.shape["dp"] // 2
    sizes = {"x": chips_x, "y": chips_x, "z": mesh.shape["fsdp"] // chips_x}
    return jax.shard_map(
        functools.partial(body, sizes),
        mesh=mesh,
        in_specs=(
            P(("dp", "fsdp"), None, None),
            P(("dp", "fsdp")),
            P(("dp", "fsdp")),
            P(("dp", "fsdp"), None),
            P(("dp", "fsdp"), None, None),
            P(("dp", "fsdp")),
            P(("dp", "fsdp")),
            P(("dp", "fsdp"), None),
            P(("dp", "fsdp")),
            P(("dp", "fsdp"), None),
            P(("dp", "fsdp")),
            P(("dp", "fsdp")),
            P(("dp", "fsdp")),
            P(("dp", "fsdp"), None),
            P(("dp", "fsdp")),
            P(("dp", "fsdp"), None),
            P(("dp", "fsdp")),
        ),
        out_specs=(
            P(("dp", "fsdp"), None, None),
            P(("dp", "fsdp"), None, None),
            P(("dp", "fsdp")),
            P(("dp", "fsdp")),
            P(("dp", "fsdp"), None),
            P(("dp", "fsdp")),
            P(("dp", "fsdp"), None),
            P(("dp", "fsdp")),
            P(("dp", "fsdp")),
            P(("dp", "fsdp")),
            P(("dp", "fsdp"), None),
            P(("dp", "fsdp")),
            P(("dp", "fsdp"), None),
            P(("dp", "fsdp")),
        ),
        check_vma=False,
    )
```

```python
import functools
import heapq
import itertools

import jax
import jax.numpy as jnp
from jax import lax
from jax.experimental import pallas as pl
from jax.experimental.pallas import tpu as pltpu
from jax.sharding import PartitionSpec as P
MESH = pl.DeviceIdType.MESH

TREES = ("zyx", "zxy", "xyz")


def offsets(length):
    return [0, "o"] if length == 2 else list(range(-(length - 1), length))


class Place:
    def __init__(self, sizes):
        self.sizes = sizes
        dp, fs = lax.axis_index("dp"), lax.axis_index("fsdp")
        self.core = lax.rem(dp, 2)
        self.pos = {"x": dp // 2, "z": fs // sizes["y"], "y": lax.rem(fs, sizes["y"])}

    def device(self, pos, core):
        return (pos["x"] * 2 + core, pos["z"] * self.sizes["y"] + pos["y"])

    def index(self, pos, core):
        dp, fs = self.device(pos, core)
        return dp * (self.sizes["z"] * self.sizes["y"]) + fs

    def chip(self, pos):
        return (pos["x"] * self.sizes["z"] + pos["z"]) * self.sizes["y"] + pos["y"]

    def neighbours(self):
        out = [(None, self.device(self.pos, 1 - self.core))]
        for d, length in self.sizes.items():
            if length == 2:
                out.append((None, self.device({**self.pos, d: 1 - self.pos[d]}, self.core)))
            elif length > 2:
                for s in (1, -1):
                    q = self.pos[d] + s
                    out.append(((q >= 0) & (q < length), self.device({**self.pos, d: q}, self.core)))
        return out


def when(conds, fn):
    conds = [c for c in conds if c is not None]
    if not conds:
        fn()
    else:
        pl.when(functools.reduce(jnp.logical_and, conds))(lambda: (fn(), None)[1])


def entry_barrier(place):
    barrier = pltpu.get_barrier_semaphore()
    total = 0
    for cond, dev in place.neighbours():
        when([cond], lambda dev=dev: pl.semaphore_signal(barrier, inc=1, device_id=dev, device_id_type=MESH))
        total = total + (1 if cond is None else cond.astype(jnp.int32))
    pl.semaphore_wait(barrier, total)


def gather_kernel(sizes, pieces, order, n_in, *refs):
    ins, outs = refs[:n_in], refs[n_in:2 * n_in]
    send_sem, recv_sem, pair_send, pair_recv, local_sem = refs[2 * n_in:]
    place = Place(sizes)
    pos, core = place.pos, place.core
    entry_barrier(place)
    partner = place.device(pos, 1 - core)
    locals_ = []
    for a in range(n_in):
        c = pltpu.make_async_copy(ins[a], outs[a].at[pos["x"], core, pos["z"], pos["y"]], local_sem.at[a])
        c.start()
        locals_.append(c)

    def part(pi, at, who):
        a, tree, lo, n = pieces[pi]
        return outs[a].at[at["x"], who, at["z"], at["y"], pl.ds(lo, n)]

    def remote(src, dst, send, recv, dev):
        return pltpu.make_async_remote_copy(src_ref=src, dst_ref=dst, send_sem=send, recv_sem=recv, device_id=dev, device_id_type=MESH)

    def line(d):
        if sizes[d] == 1:
            return []
        if sizes[d] == 2:
            return [(0, None, 1 - pos[d])]
        return [(0, pos[d] + 1 < sizes[d], pos[d] + 1), (1, pos[d] > 0, pos[d] - 1)]

    left = {}
    for pi, t in order:
        left[pi] = left.get(pi, 0) + 1
    seen = dict.fromkeys(left, 0)
    whole = [slice(None)] * 3
    for pi, t in order:
        a, tree, lo, n = pieces[pi]
        own = all(v == 0 for v in t)
        at, conds = dict(pos), []
        for d, v in zip(tree, t):
            if v == "o":
                at[d] = 1 - pos[d]
            elif v != 0:
                at[d] = pos[d] + v
                conds.append((at[d] >= 0) if v < 0 else (at[d] < sizes[d]))
        chip = place.chip(at)
        dst = part(pi, at, core)
        src = ins[a].at[pl.ds(lo, n)] if own else dst
        k = max([j for j, v in enumerate(t) if v != 0], default=-1)

        def handle(tree=tree, t=t, own=own, chip=chip, dst=dst, src=src, k=k, pi=pi):
            if not own:
                remote(dst, dst, pair_send.at[pi], recv_sem.at[pi, chip], partner).wait_recv()
            for j in (2, 1, 0):
                d = tree[j]
                if j < k:
                    continue
                for slot, ok, q in line(d):
                    if j == k and (t[j] == "o" or (t[j] < 0) != (slot == 0)):
                        continue
                    when([ok], remote(src, dst, send_sem.at[pi, 2 * "xyz".index(d) + slot], recv_sem.at[pi, chip],
                                      place.device({**pos, d: q}, core)).start)
            remote(src, dst, pair_send.at[pi], pair_recv.at[pi], partner).start()
        when(conds, handle)
        seen[pi] += 1

    full = dict.fromkeys("xyz", slice(None))
    for pi, (a, tree, lo, n) in enumerate(pieces):
        for j, d in enumerate(tree):
            at = {e: (slice(None) if tree.index(e) < j else pos[e]) for e in "xyz"}
            for slot, ok, q in line(d):
                sem = send_sem.at[pi, 2 * "xyz".index(d) + slot]
                if sizes[d] == 2:
                    ref = part(pi, at, core)
                    remote(ref, ref, sem, recv_sem.at[pi, 0], partner).wait_send()
                else:
                    for z in range(sizes[d]):
                        ref = part(pi, {**at, d: z}, core)
                        sent = (pos[d] >= z) if slot == 0 else (pos[d] <= z)
                        when([ok, sent], remote(ref, ref, sem, recv_sem.at[pi, 0], partner).wait_send)
        ref = part(pi, full, core)
        remote(ref, ref, pair_send.at[pi], pair_recv.at[pi], partner).wait_send()
        ref = part(pi, full, 1 - core)
        remote(ref, ref, pair_send.at[pi], pair_recv.at[pi], partner).wait_recv()
    for c in locals_:
        c.wait()


def gather_order(sizes, pieces, alpha):
    ev = []
    for pi, (a, tree, lo, n) in enumerate(pieces):
        for t in itertools.product(*[offsets(sizes[d]) for d in tree]):
            hops = sum(1 if v == "o" else abs(v) for v in t)
            ev.append((pi * alpha + hops, pi, t))
    ev.sort(key=lambda e: (e[0], e[1]))
    return [(pi, t) for _, pi, t in ev]


def gather(sizes, shards, alpha=0.05):
    chips = sizes["x"] * sizes["y"] * sizes["z"]
    pieces = []
    for a, s in enumerate(shards):
        tiles = s.shape[0] // 8
        if tiles % 3 == 0 and tiles < 12:
            cuts = [(i, i * tiles // 3, tiles // 3) for i in range(3)]
        elif tiles % 2 == 0:
            cuts = [(i, i * tiles // 2, tiles // 2) for i in range(2)]
        else:
            cuts = [(2, 0, tiles)]
        for tree, lo, n in cuts:
            pieces.append((a, TREES[tree], lo * 8, n * 8))
    order = gather_order(sizes, pieces, alpha)
    n_in = len(shards)
    return pl.pallas_call(
        functools.partial(gather_kernel, sizes, pieces, order, n_in),
        out_shape=[jax.ShapeDtypeStruct((sizes["x"], 2, sizes["z"], sizes["y"]) + s.shape, s.dtype) for s in shards],
        in_specs=[pl.BlockSpec(memory_space=pltpu.VMEM)] * n_in,
        out_specs=[pl.BlockSpec(memory_space=pl.ANY)] * n_in,
        scratch_shapes=[
            pltpu.SemaphoreType.DMA((len(pieces), 6)),
            pltpu.SemaphoreType.DMA((len(pieces), chips)),
            pltpu.SemaphoreType.DMA((len(pieces),)),
            pltpu.SemaphoreType.DMA((len(pieces),)),
            pltpu.SemaphoreType.DMA((n_in,)),
        ],
        compiler_params=pltpu.CompilerParams(collective_id=0, has_side_effects=True),
        name="gather",
    )(*shards)


class View:
    def __init__(self, ref, dims, fixed=None, core=None):
        self.ref, self.dims, self.fixed, self.core = ref, dims, fixed or {}, core

    def fix(self, d, v):
        return View(self.ref, self.dims, {**self.fixed, d: v}, self.core)

    def free(self):
        return [d for d in self.dims if d not in self.fixed]

    def index(self, at, cols=None):
        idx = [self.fixed.get(d, at.get(d, slice(None))) for d in self.dims]
        if self.core is not None:
            core, lo, n = self.core
            return (idx[0], core, *idx[1:], slice(None), pl.ds(lo, n))
        return tuple(idx)

    def whole(self):
        return self.ref.at[self.index({})]


def accumulate(sizes, dst, terms):
    dims = terms[0].free()

    def step(i, carry):
        at = {}
        for d in reversed(dims):
            at[d] = lax.rem(i, sizes[d])
            i = i // sizes[d]
        total = None
        for t in terms:
            v = t.ref[t.index(at)].astype(jnp.float32)
            total = v if total is None else total + v
        if isinstance(dst, View):
            dst.ref[dst.index(at)] = total.astype(dst.ref.dtype)
        else:
            dst(total)
        return carry

    count = 1
    for d in dims:
        count *= sizes[d]
    if count == 1:
        step(0, 0)
    else:
        lax.fori_loop(0, count, step, 0)


def piece_buffers(sizes, piece, rows):
    a, tree, lo, n = piece
    dims = list("xzy")
    shapes = [tuple(sizes[d] for d in dims) + (rows, n)]
    for d in tree:
        dims.remove(d)
        rest = tuple(sizes[e] for e in dims) + (rows, n)
        if sizes[d] == 2:
            shapes.append(rest)
        elif sizes[d] > 2:
            shapes += [(sizes[d],) + rest] * 2
    return shapes


def piece_copies(sizes, tree):
    return 1 + sum(0 if sizes[d] == 1 else 1 if sizes[d] == 2 else 2 * sizes[d] for d in tree)


def tree_loads(sizes, tree):
    share, loads = 1.0, {}
    for d in tree:
        loads[d] = share * (sizes[d] - 1) / sizes[d]
        share /= sizes[d]
    return loads


def cut(shapes):
    order = sorted(range(len(shapes)), key=lambda a: -shapes[a][0] * shapes[a][1])
    out = []
    for i, a in enumerate(order):
        rows, cols = shapes[a]
        wide = max(256, 18432 // rows // 256 * 256)
        lo, small = 0, [256, 512] if i == 0 else [256] * 9 if i == len(order) - 1 else []
        while lo < cols:
            n = min(small.pop(0) if small else wide, cols - lo)
            out.append((a, lo, n))
            lo += n
    return out


def plan(sizes, shapes, rates):
    make_us, pair_us, link_us, hop_us = rates
    used, pieces, size = dict.fromkeys("xyz", 0.0), [], {}
    for a, lo, n in cut(shapes):
        rows = shapes[a][0]
        units = rows * n / 6144

        def worst(tree):
            loads = tree_loads(sizes, tree)
            return max(used[d] + units * loads[d] for d in tree), used[tree[0]]

        tree = min(("xzy", "yzx", "xyz", "yxz"), key=worst)
        for d, v in tree_loads(sizes, tree).items():
            used[d] += units * v
        size[len(pieces)] = units
        pieces.append((a, tree, lo, n))
    order, free, heap, count = [], dict.fromkeys(("pair", "x", "y", "z"), 0.0), [], itertools.count()
    now = 0.0

    def push(t, pi, what):
        heapq.heappush(heap, (t, next(count), pi, what))

    def carry(link, t, us):
        free[link] = max(t, free[link]) + us
        return free[link] + hop_us

    def launch(t, pi, j):
        tree = pieces[pi][1]
        if j == 3:
            return
        d = tree[j]
        part = size[pi]
        for e in tree[:j + 1]:
            part /= sizes[e]
        if sizes[d] == 1:
            launch(t, pi, j + 1)
        elif sizes[d] == 2:
            push(carry(d, t, part * link_us), pi, ("swap", j))
        else:
            top = sizes[d] - 1
            arrive = [carry(d, t, part * link_us) for _ in range(top)]
            for hop in range(1, top):
                for dest in range(top, hop, -1):
                    when_us = arrive[top - dest] + (hop - 1) * (hop_us + part * link_us)
                    push(when_us, pi, ("up", j, hop, dest))
                    push(when_us, pi, ("down", j, top - hop, top - dest))
            push(arrive[-1] + (top - 1) * hop_us + part * link_us, pi, ("land", j))

    for pi in range(len(pieces)):
        now += make_us * size[pi]
        push(now, pi, ("make",))
    while heap:
        t, _, pi, what = heapq.heappop(heap)
        order.append((pi, what))
        if what[0] == "make":
            push(carry("pair", t, size[pi] / 2 * pair_us), pi, ("pair",))
        elif what[0] == "pair":
            launch(t, pi, 0)
        elif what[0] in ("swap", "land"):
            launch(t, pi, what[1] + 1)
    return pieces, order


def reduce_kernel(sizes, pieces, order, weights, *refs):
    lefts, rights, packed = refs[:weights], refs[weights:2 * weights], refs[2 * weights]
    outs, rest = refs[2 * weights + 1:3 * weights + 2], list(refs[3 * weights + 2:])
    send_sem, recv_sem = rest[-2:]
    ins, rest = [*rest[:weights], packed], rest[weights:]
    place = Place(sizes)
    pos, core = place.pos, place.core
    partner = place.device(pos, 1 - core)
    state, base, sent = [], 0, []
    for pi, (a, tree, lo, n) in enumerate(pieces):
        k = len(piece_buffers(sizes, pieces[pi], 8))
        bufs, rest = rest[:k], rest[k:]
        copies = {"pair": (0, 0)}
        c, b = 1, 1
        for j, d in enumerate(tree):
            if sizes[d] > 1:
                copies[j] = (c, b)
                c += 1 if sizes[d] == 2 else 2 * sizes[d]
                b += 1 if sizes[d] == 2 else 2
        state.append({"bufs": bufs, "base": base, "copies": copies, "cur": None})
        base += c

    def copy(src, dst, sem, dev):
        return pltpu.make_async_remote_copy(src_ref=src, dst_ref=dst, send_sem=send_sem.at[sem], recv_sem=recv_sem.at[sem], device_id=dev, device_id_type=MESH)

    def send(conds, src, dst, sem, dev):
        c = copy(src, dst, sem, dev)
        when(conds, c.start)
        sent.append((conds, c))

    def await_copy(buf, sem):
        copy(buf, buf, sem, partner).wait_recv()

    entry_barrier(place)

    def make(a, lo, n):
        total, rows = lefts[a].shape[0], ins[a].shape[4]
        places = list(itertools.product(*[range(v) for v in ins[a].shape[:4]]))
        step = min(total, 768)
        for top in range(0, total, step):
            for left in range(lo, lo + n, 256):
                cols = slice(left, min(left + 256, lo + n))
                block = dot(lefts[a][top:top + step, :], rights[a][:, cols]).astype(ins[a].dtype)
                for i in range(step // rows):
                    ins[a][(*places[top // rows + i], slice(None), cols)] = block[i * rows:(i + 1) * rows]

    def launch(pi, j):
        a, tree, lo, n = pieces[pi]
        st = state[pi]
        while j < 3 and sizes[tree[j]] == 1:
            st["cur"] = st["cur"].fix(tree[j], 0)
            j += 1
        if j == 3:
            return
        d, cur = tree[j], st["cur"]
        c, b = st["copies"][j]
        c += st["base"]
        p, size = pos[d], sizes[d]
        if size == 2:
            send([], cur.fix(d, 1 - p).whole(), st["bufs"][b], c, place.device({**pos, d: 1 - p}, core))
            return
        for t in range(size - 1, 0, -1):
            send([p == 0], cur.fix(d, t).whole(), st["bufs"][b].at[t], c + t, place.device({**pos, d: p + 1}, core))
            t = size - 1 - t
            send([p == size - 1], cur.fix(d, t).whole(), st["bufs"][b + 1].at[t], c + size + t, place.device({**pos, d: p - 1}, core))

    def run(pi, what):
        a, tree, lo, n = pieces[pi]
        st = state[pi]
        if what[0] == "make":
            if a < weights:
                make(a, lo, n)
            src = View(ins[a], list("xzy"), core=(1 - core, lo, n))
            send([], src.whole(), st["bufs"][0], st["base"], partner)
            return
        if what[0] == "pair":
            buf = st["bufs"][0]
            await_copy(buf, st["base"])
            mine = View(ins[a], list("xzy"), core=(core, lo, n))
            st["cur"] = View(buf, list("xzy"))
            accumulate(sizes, st["cur"], [st["cur"], mine])
            launch(pi, 0)
            return
        j = what[1]
        d, cur = tree[j], st["cur"]
        c, b = st["copies"][j]
        c += st["base"]
        p, size = pos[d], sizes[d]
        last = all(sizes[e] == 1 for e in tree[j + 1:])
        left = [e for e in cur.free() if e != d]

        def store(total):
            outs[a][:, pl.ds(lo, n)] = total

        if what[0] == "swap":
            buf = st["bufs"][b]
            await_copy(buf, c)
            new = View(buf, left)
            accumulate(sizes, store if last else new, [cur.fix(d, p), new])
            st["cur"] = new
            launch(pi, j + 1)
        elif what[0] in ("up", "down"):
            up = what[0] == "up"
            here, t = what[2], what[3]
            sem = c + t if up else c + size + t
            buf = st["bufs"][b if up else b + 1]

            def relay():
                await_copy(buf.at[t], sem)
                new = View(buf, [d] + left, {d: t})
                accumulate(sizes, new, [cur.fix(d, t), new])

            when([p == here], relay)
            send([p == here], buf.at[t], buf.at[t], sem, place.device({**pos, d: p + 1 if up else p - 1}, core))
        else:
            ups, downs = st["bufs"][b], st["bufs"][b + 1]
            new = cur.fix(d, p)
            below, above = View(ups, [d] + left, {d: p}), View(downs, [d] + left, {d: p})
            for p_below, p_above, conds in ((False, True, [p == 0]), (True, True, [p > 0, p < size - 1]), (True, False, [p == size - 1])):
                def land(p_below=p_below, p_above=p_above):
                    terms = [new]
                    if p_below:
                        await_copy(ups.at[p], c + p)
                        terms.append(below)
                    if p_above:
                        await_copy(downs.at[p], c + size + p)
                        terms.append(above)
                    accumulate(sizes, store if last else new, terms)
                when(conds, land)
            st["cur"] = new
            launch(pi, j + 1)

    for pi, what in order:
        run(pi, what)
    for conds, c in sent:
        when(conds, c.wait_send)


def reduce_scatter(sizes, factors, packed, rates=(0.3, 1.2, 4.3, 1.2)):
    chips = sizes["x"] * sizes["y"] * sizes["z"]
    lead = (sizes["x"], 2, sizes["z"], sizes["y"])
    low = [(left.shape[0] // (2 * chips), right.shape[1]) for left, right in factors]
    shapes = low + [packed.shape[-2:]]
    pieces, order = plan(sizes, shapes, rates)
    buffers, copies = [], 0
    for piece in pieces:
        kind = jnp.bfloat16 if piece[0] < len(low) else packed.dtype
        buffers += [pltpu.VMEM(s, kind) for s in piece_buffers(sizes, piece, shapes[piece[0]][0])]
        copies += piece_copies(sizes, piece[1])
    vmem = pl.BlockSpec(memory_space=pltpu.VMEM)
    return pl.pallas_call(
        functools.partial(reduce_kernel, sizes, pieces, order, len(low)),
        out_shape=[jax.ShapeDtypeStruct(s, jnp.float32) for s in shapes],
        in_specs=[vmem] * (2 * len(low) + 1),
        out_specs=[vmem] * len(shapes),
        scratch_shapes=[pltpu.VMEM(lead + s, jnp.bfloat16) for s in low] + buffers
        + [pltpu.SemaphoreType.DMA((copies,)), pltpu.SemaphoreType.DMA((copies,))],
        compiler_params=pltpu.CompilerParams(collective_id=1, has_side_effects=True, vmem_limit_bytes=67000000),
        name="reduce",
    )(*[left for left, _ in factors], *[right for _, right in factors], packed)


def finish_kernel(chunks, packed, *refs):
    n = (len(refs) - 1 - len(chunks)) // 3
    ins, outs, vectors, bufs, sems = refs[:n], refs[n:2 * n], refs[2 * n:2 * n + len(chunks)], refs[2 * n + len(chunks):-1], refs[-1]
    loads = [pltpu.make_async_copy(a, b, sems.at[0, i]) for i, (a, b) in enumerate(zip(ins, bufs))]
    stores = [pltpu.make_async_copy(b, o, sems.at[1, i]) for i, (b, o) in enumerate(zip(bufs, outs))]
    for c in loads:
        c.start()
    for i, w in enumerate(chunks):
        vectors[i][...] = packed[i:i + 1, :w]
    for c, o in zip(loads, stores):
        c.wait()
        o.start()
    for o in stores:
        o.wait()


def finish(chunks, arrays, packed):
    n = len(arrays)
    vmem, everywhere = pl.BlockSpec(memory_space=pltpu.VMEM), pl.BlockSpec(memory_space=pl.ANY)
    out = pl.pallas_call(
        functools.partial(finish_kernel, chunks),
        out_shape=[jax.ShapeDtypeStruct(a.shape, a.dtype) for a in arrays] + [jax.ShapeDtypeStruct((1, w), packed.dtype) for w in chunks],
        in_specs=[vmem] + [everywhere] * n,
        out_specs=[everywhere] * n + [vmem] * len(chunks),
        scratch_shapes=[pltpu.VMEM(a.shape, a.dtype) for a in arrays] + [pltpu.SemaphoreType.DMA((2, n))],
        name="finish",
    )(packed, *arrays)
    return out[:n], [v[0] for v in out[n:]]


HEAD_DIM = 64
PASSES = 4
EPSILON = 1e-05
SCORE_SCALE = 0.125
GELU_COEF = 0.7978845608028654
GELU_CUBE = 0.044715


def dot(left, right, dims=((1,), (0,))):
    return lax.dot_general(left, right, (dims, ((), ())), preferred_element_type=jnp.float32)


NT, TN = ((1,), (1,)), ((0,), (0,))


def normalise(values):
    centre = values - jnp.mean(values, axis=-1, keepdims=True)
    scale = lax.rsqrt(jnp.mean(centre * centre, axis=-1, keepdims=True) + EPSILON)
    return centre * scale, scale


def normalise_back(grad, unit, scale):
    return scale * (grad - jnp.mean(grad, axis=-1, keepdims=True) - unit * jnp.mean(grad * unit, axis=-1, keepdims=True))


def block_kernel(chunk, sections, key_ok, hidden, cotangent, g1, b1, qkv_b, out_b, g2, b2, fc_b, proj_b,
                 qkv_hbm, out_hbm, fc_hbm, proj_hbm,
                 hidden_out, grad_hidden, a_t, o_t, c_t, g_t, dqkv_st, do_st, du_st, dm_st,
                 dg1, db1, dqkv_b, dout_b, dg2, db2, dfc_b, dproj_b,
                 qkv_w, out_w, fc_w, proj_w, state, unit1, unit2, scale1, scale2, qkv_st, prob_st, slope_st, mixed, wide, allow, sems):
    rows, width = hidden.shape
    hidden_width = fc_w.shape[1]
    pair = 2 * HEAD_DIM
    pairs = width // pair
    loads = [pltpu.make_async_copy(src, dst, sems.at[i]) for i, (src, dst) in enumerate(
        ((qkv_hbm, qkv_w), (out_hbm, out_w), (fc_hbm, fc_w), (proj_hbm, proj_w)))]
    for c in loads:
        c.start()
    for ref in (dg1, db1, dqkv_b, dout_b, dg2, db2, dfc_b, dproj_b):
        ref[...] = jnp.zeros_like(ref)
    query = lax.broadcasted_iota(jnp.int32, (rows, 2 * rows), 0)
    key = lax.rem(lax.broadcasted_iota(jnp.int32, (rows, 2 * rows), 1), rows)
    ok = jnp.broadcast_to(key_ok[...], (rows, 2 * rows)) > 0.5
    allow[...] = jnp.where((key < query) & ok | (key == query), 1.0, 0.0)
    state[...] = hidden[...].astype(jnp.float32)
    first = lax.broadcasted_iota(jnp.int32, (rows, pair), 1) < HEAD_DIM

    def both(block):
        wide = block.astype(jnp.float32)
        return jnp.concatenate([jnp.where(first, wide, 0.0), jnp.where(first, 0.0, wide)], axis=0).astype(jnp.bfloat16)

    def merge(block):
        return jnp.where(first, block[:rows], block[rows:])

    def halves(fn, block, *others):
        return [fn(block[:, s], *(o[:, s] for o in others)) for s in (slice(0, rows), slice(rows, 2 * rows))]

    def forward(k, wait):
        x = state[...]
        unit, scale = normalise(x)
        unit1[k] = unit
        scale1[k] = jnp.broadcast_to(scale, scale1.shape[1:])
        at = pl.ds(pl.multiple_of(k * rows, rows), rows)
        a = (unit * g1[...] + b1[...]).astype(jnp.bfloat16)
        mixed[...] = a
        a_t[:, at] = a.T
        if wait:
            loads[0].wait()
        for lo in range(0, 3 * width, chunk):
            cols = slice(lo, lo + chunk)
            qkv_st[k, :, cols] = (dot(mixed[...], qkv_w[:, cols]) + qkv_b[:, cols]).astype(jnp.bfloat16)
        for i in range(pairs):
            q = qkv_st[k, :, i * pair:(i + 1) * pair]
            keys = both(qkv_st[k, :, width + i * pair:width + (i + 1) * pair])
            values = both(qkv_st[k, :, 2 * width + i * pair:2 * width + (i + 1) * pair])
            scores = jnp.where(allow[...] > 0.5, dot(q, keys, NT) * SCORE_SCALE, -1e30)

            def softmax(s):
                e = jnp.exp(s - jnp.max(s, axis=-1, keepdims=True))
                return e / jnp.sum(e, axis=-1, keepdims=True)

            probs = jnp.concatenate(halves(softmax, scores), axis=1)
            prob_st[k, i] = probs
            o = dot(probs.astype(jnp.bfloat16), values).astype(jnp.bfloat16)
            mixed[:, i * pair:(i + 1) * pair] = o
            o_t[i * pair:(i + 1) * pair, at] = o.T
        if wait:
            loads[1].wait()
        h = x + (dot(mixed[...], out_w[...]) + out_b[...])
        unit, scale = normalise(h)
        unit2[k] = unit
        scale2[k] = jnp.broadcast_to(scale, scale2.shape[1:])
        c = (unit * g2[...] + b2[...]).astype(jnp.bfloat16)
        mixed[...] = c
        c_t[:, at] = c.T
        if wait:
            loads[2].wait()
        for lo in range(0, hidden_width, chunk):
            cols = slice(lo, lo + chunk)
            u = dot(mixed[...], fc_w[:, cols]) + fc_b[:, cols]
            square = u * u
            t = jnp.tanh(GELU_COEF * (u + GELU_CUBE * (square * u)))
            half = 0.5 * (1.0 + t)
            g = (u * half).astype(jnp.bfloat16)
            wide[:, cols] = g
            g_t[cols, at] = g.T
            slope_st[k, :, cols] = half + 0.5 * u * (1.0 - t * t) * (GELU_COEF * (1.0 + 3.0 * GELU_CUBE * square))
        if wait:
            loads[3].wait()
        y = h + (dot(wide[...], proj_w[...]) + proj_b[...])

        @pl.when(sections[0] >= k)
        def _():
            state[...] = y

    forward(0, True)
    lax.fori_loop(1, PASSES, lambda k, c: (forward(k, False), c)[1], 0)
    hidden_out[...] = state[...].astype(jnp.bfloat16)
    state[...] = cotangent[...].astype(jnp.float32)

    def column_sums(ref, cols, block):
        ref[:, cols] += jnp.sum(block.astype(jnp.float32), axis=0, keepdims=True)

    def backward(step, carry):
        k = PASSES - 1 - step
        live = (sections[0] >= k).astype(jnp.float32)
        dx = state[...]
        dy = dx * live
        dm_st[k] = dy.astype(jnp.bfloat16)
        column_sums(dproj_b, slice(None), dm_st[k])
        for lo in range(0, hidden_width, chunk):
            cols = slice(lo, lo + chunk)
            du = (dot(dm_st[k], proj_w[cols, :], NT) * slope_st[k, :, cols]).astype(jnp.bfloat16)
            du_st[k, :, cols] = du
            column_sums(dfc_b, cols, du)
        dc = dot(du_st[k], fc_w[...], NT)
        unit = unit2[k]
        dg2[...] += jnp.sum(dc * unit, axis=0, keepdims=True)
        column_sums(db2, slice(None), dc)
        dh = dy + normalise_back(dc * g2[...], unit, scale2[k, :, 0:1])
        state[...] = dh + dx * (1.0 - live)
        do_st[k] = dh.astype(jnp.bfloat16)
        column_sums(dout_b, slice(None), do_st[k])
        mixed[...] = dot(do_st[k], out_w[...], NT).astype(jnp.bfloat16)
        for i in range(pairs):
            at = [slice(j * width + i * pair, j * width + (i + 1) * pair) for j in range(3)]
            q = qkv_st[k, :, at[0]]
            keys, values = both(qkv_st[k, :, at[1]]), both(qkv_st[k, :, at[2]])
            grad = mixed[:, at[0]]
            probs = prob_st[k, i]
            dp = dot(grad, values, NT)

            def scores_back(d, p):
                return p * (d - jnp.sum(d * p, axis=-1, keepdims=True))

            ds = jnp.concatenate(halves(scores_back, dp, probs), axis=1).astype(jnp.bfloat16)
            dv = merge(dot(probs.astype(jnp.bfloat16), grad, TN))
            dq = dot(ds, keys) * SCORE_SCALE
            dk = merge(dot(ds, q, TN)) * SCORE_SCALE
            for j, d in enumerate((dq, dk, dv)):
                dqkv_st[k, :, at[j]] = d.astype(jnp.bfloat16)
        column_sums(dqkv_b, slice(None), dqkv_st[k])
        da = dot(dqkv_st[k], qkv_w[...], NT)
        unit = unit1[k]
        dg1[...] += jnp.sum(da * unit, axis=0, keepdims=True)
        column_sums(db1, slice(None), da)
        state[...] += normalise_back(da * g1[...], unit, scale1[k, :, 0:1])
        return carry

    lax.fori_loop(0, PASSES, backward, 0)
    grad_hidden[...] = state[...]


def run_block(sections, key_valid, hidden, cotangent, attention, mlp):
    g1, b1, qkv_w, qv_b, out_w, out_b = attention
    g2, b2, fc_w, fc_b, proj_w, proj_b = mlp
    rows, width = hidden.shape
    ff = fc_w.shape[1]
    bias = jnp.concatenate([qv_b[:width], jnp.zeros_like(qv_b[:width]), qv_b[width:]])
    vectors = [v.astype(jnp.float32)[None] for v in (g1, b1, bias, out_b, g2, b2, fc_b, proj_b)]
    key_ok = jnp.concatenate([key_valid, key_valid], axis=1).astype(jnp.float32)
    low, high = jnp.bfloat16, jnp.float32
    lefts, rights = [width, width, width, ff], [3 * width, width, ff, width]
    pairs = width // (2 * HEAD_DIM)
    vmem, everywhere = pl.BlockSpec(memory_space=pltpu.VMEM), pl.BlockSpec(memory_space=pl.ANY)
    outs = pl.pallas_call(
        functools.partial(block_kernel, 512 if ff % 512 == 0 and width * 3 % 512 == 0 else 256),
        out_shape=[jax.ShapeDtypeStruct((rows, width), low), jax.ShapeDtypeStruct((rows, width), high)]
        + [jax.ShapeDtypeStruct((n, PASSES * rows), low) for n in lefts]
        + [jax.ShapeDtypeStruct((PASSES, rows, n), low) for n in rights]
        + [jax.ShapeDtypeStruct(v.shape, high) for v in vectors],
        in_specs=[pl.BlockSpec(memory_space=pltpu.SMEM)] + [vmem] * 11 + [everywhere] * 4,
        out_specs=[vmem] * 18,
        scratch_shapes=[pltpu.VMEM(w.shape, low) for w in (qkv_w, out_w, fc_w, proj_w)] + [
            pltpu.VMEM((rows, width), high),
            pltpu.VMEM((PASSES, rows, width), high),
            pltpu.VMEM((PASSES, rows, width), high),
            pltpu.VMEM((PASSES, rows, 128), high),
            pltpu.VMEM((PASSES, rows, 128), high),
            pltpu.VMEM((PASSES, rows, 3 * width), low),
            pltpu.VMEM((PASSES, pairs, rows, 2 * rows), high),
            pltpu.VMEM((PASSES, rows, ff), high),
            pltpu.VMEM((rows, width), low),
            pltpu.VMEM((rows, ff), low),
            pltpu.VMEM((rows, 2 * rows), high),
            pltpu.SemaphoreType.DMA((4,)),
        ],
        compiler_params=pltpu.CompilerParams(vmem_limit_bytes=67000000),
        name="block",
    )(sections, key_ok, hidden, cotangent, *vectors, qkv_w, out_w, fc_w, proj_w)
    hidden_out, grad_hidden = outs[:2]
    a, o, c, g = outs[2:6]
    dqkv, do, du, dm = [s.reshape(PASSES * rows, -1) for s in outs[6:10]]
    dg1, db1, dbias, dout_b, dg2, db2, dfc_b, dproj_b = [v[0] for v in outs[10:]]
    dqv_b = jnp.concatenate([dbias[:width], dbias[2 * width:]])
    factors = ((a, dqkv), (o, do), (c, du), (g, dm))
    return hidden_out, grad_hidden, factors, (dg1, db1, dqv_b, dout_b, dg2, db2, dfc_b, dproj_b)


def fetch_attention(ln1_gain, ln1_bias, qkv_weight, qv_bias, out_weight, out_bias):
    return (
        lax.all_gather(ln1_gain, ("dp", "fsdp"), axis=0, tiled=True),
        lax.all_gather(ln1_bias, ("dp", "fsdp"), axis=0, tiled=True),
        lax.all_gather(qkv_weight, ("dp", "fsdp"), axis=0, tiled=True),
        lax.all_gather(qv_bias, ("dp", "fsdp"), axis=0, tiled=True),
        lax.all_gather(out_weight, ("dp", "fsdp"), axis=0, tiled=True),
        lax.all_gather(out_bias, ("dp", "fsdp"), axis=0, tiled=True),
    )


def fetch_mlp(ln2_gain, ln2_bias, fc_weight, fc_bias, proj_weight, proj_bias):
    return (
        lax.all_gather(ln2_gain, ("dp", "fsdp"), axis=0, tiled=True),
        lax.all_gather(ln2_bias, ("dp", "fsdp"), axis=0, tiled=True),
        lax.all_gather(fc_weight, ("dp", "fsdp"), axis=0, tiled=True),
        lax.all_gather(fc_bias, ("dp", "fsdp"), axis=0, tiled=True),
        lax.all_gather(proj_weight, ("dp", "fsdp"), axis=0, tiled=True),
        lax.all_gather(proj_bias, ("dp", "fsdp"), axis=0, tiled=True),
    )


def fetch_all(sizes, attention, mlp):
    ln1_gain, ln1_bias, qkv_weight, qv_bias, out_weight, out_bias = attention
    ln2_gain, ln2_bias, fc_weight, fc_bias, proj_weight, proj_bias = mlp
    big = (qkv_weight, out_weight, fc_weight, proj_weight)
    small = (ln1_gain, ln1_bias, qv_bias, out_bias, ln2_gain, ln2_bias, fc_bias, proj_bias)
    width = -(-sum(v.shape[0] for v in small) // 1024) * 128
    if any(w.shape[0] % 8 for w in big):
        return fetch_attention(*attention), fetch_mlp(*mlp)
    packed = jnp.concatenate(small)
    packed = jnp.pad(packed, (0, 8 * width - packed.shape[0])).reshape(8, width)
    *full, rows = gather(sizes, (*big, packed))
    qkv_full, out_full, fc_full, proj_full = [w.reshape(-1, w.shape[-1]) for w in full]
    rows = rows.reshape(-1, 8 * width)
    vectors, start = [], 0
    for v in small:
        vectors.append(rows[:, start : start + v.shape[0]].reshape(-1))
        start += v.shape[0]
    g1, b1, qv, ob, g2, b2, fb, pb = vectors
    return (g1, b1, qkv_full, qv, out_full, ob), (g2, b2, fc_full, fb, proj_full, pb)


def sum_all(sizes, factors, vectors):
    chips = sizes["x"] * sizes["y"] * sizes["z"]
    if any(left.shape[0] % (16 * chips) for left, _ in factors):
        big = [dot(left, right).astype(jnp.bfloat16) for left, right in factors]
        qkv, out, fc, proj, *sums = [
            lax.psum_scatter(v, ("dp", "fsdp"), scatter_dimension=0, tiled=True).astype(jnp.float32) for v in (*big, *vectors)
        ]
    else:
        lead = (sizes["x"], 2, sizes["z"], sizes["y"])
        chunks = [v.shape[0] // (2 * chips) for v in vectors]
        width = -(-max(chunks) // 128) * 128
        rows = [jnp.pad(v.reshape(2 * chips, 1, w), ((0, 0), (0, 0), (0, width - w))) for v, w in zip(vectors, chunks)]
        packed = jnp.concatenate(rows, axis=1).reshape(*lead, 8, width)
        *big, packed = reduce_scatter(sizes, factors, packed)
        (qkv, out, fc, proj), sums = finish(chunks, big, packed)
    g1, b1, qv, ob, g2, b2, fb, pb = sums
    return (g1, b1, qkv, qv, out, ob), (g2, b2, fc, fb, proj, pb)


def body(
    sizes,
    hidden,
    sections,
    lengths,
    token_mask,
    cotangent,
    ln1_gain,
    ln1_bias,
    qkv_weight,
    qv_bias,
    out_weight,
    out_bias,
    ln2_gain,
    ln2_bias,
    fc_weight,
    fc_bias,
    proj_weight,
    proj_bias,
):
    seq_count, seq_len, model_width = hidden.shape
    row_count = seq_count * seq_len
    key_pos = jnp.arange(seq_len, dtype=jnp.int32)
    key_valid = (key_pos[None, :] < lengths[:, None]) & (token_mask == 1)

    current = fetch_all(
        sizes,
        (ln1_gain, ln1_bias, qkv_weight, qv_bias, out_weight, out_bias),
        (ln2_gain, ln2_bias, fc_weight, fc_bias, proj_weight, proj_bias),
    )

    hidden_out, grad_hidden, factors, vectors = run_block(
        sections, key_valid, hidden.reshape(row_count, model_width), cotangent.reshape(row_count, model_width), *current
    )
    attention_grads, finished = sum_all(sizes, factors, vectors)
    hidden_out = hidden_out.reshape(hidden.shape)
    grad_hidden = grad_hidden.reshape(hidden.shape)
    return (
        hidden_out,
        grad_hidden,
        attention_grads[0],
        attention_grads[1],
        attention_grads[2],
        attention_grads[3],
        attention_grads[4],
        attention_grads[5],
        finished[0],
        finished[1],
        finished[2],
        finished[3],
        finished[4],
        finished[5],
    )


def solution(mesh):
    chips_x = mesh.shape["dp"] // 2
    sizes = {"x": chips_x, "y": chips_x, "z": mesh.shape["fsdp"] // chips_x}
    return jax.shard_map(
        functools.partial(body, sizes),
        mesh=mesh,
        in_specs=(
            P(("dp", "fsdp"), None, None),
            P(("dp", "fsdp")),
            P(("dp", "fsdp")),
            P(("dp", "fsdp"), None),
            P(("dp", "fsdp"), None, None),
            P(("dp", "fsdp")),
            P(("dp", "fsdp")),
            P(("dp", "fsdp"), None),
            P(("dp", "fsdp")),
            P(("dp", "fsdp"), None),
            P(("dp", "fsdp")),
            P(("dp", "fsdp")),
            P(("dp", "fsdp")),
            P(("dp", "fsdp"), None),
            P(("dp", "fsdp")),
            P(("dp", "fsdp"), None),
            P(("dp", "fsdp")),
        ),
        out_specs=(
            P(("dp", "fsdp"), None, None),
            P(("dp", "fsdp"), None, None),
            P(("dp", "fsdp")),
            P(("dp", "fsdp")),
            P(("dp", "fsdp"), None),
            P(("dp", "fsdp")),
            P(("dp", "fsdp"), None),
            P(("dp", "fsdp")),
            P(("dp", "fsdp")),
            P(("dp", "fsdp")),
            P(("dp", "fsdp"), None),
            P(("dp", "fsdp")),
            P(("dp", "fsdp"), None),
            P(("dp", "fsdp")),
        ),
        check_vma=False,
    )
```

```python
import functools
import heapq
import itertools

import jax
import jax.numpy as jnp
from jax import lax
from jax.experimental import pallas as pl
from jax.experimental.pallas import tpu as pltpu
from jax.sharding import PartitionSpec as P
MESH = pl.DeviceIdType.MESH

TREES = ("zyx", "zxy", "xyz")


def offsets(length):
    return [0, "o"] if length == 2 else list(range(-(length - 1), length))


class Place:
    def __init__(self, sizes):
        self.sizes = sizes
        dp, fs = lax.axis_index("dp"), lax.axis_index("fsdp")
        self.core = lax.rem(dp, 2)
        self.pos = {"x": dp // 2, "z": fs // sizes["y"], "y": lax.rem(fs, sizes["y"])}

    def device(self, pos, core):
        return (pos["x"] * 2 + core, pos["z"] * self.sizes["y"] + pos["y"])

    def index(self, pos, core):
        dp, fs = self.device(pos, core)
        return dp * (self.sizes["z"] * self.sizes["y"]) + fs

    def chip(self, pos):
        return (pos["x"] * self.sizes["z"] + pos["z"]) * self.sizes["y"] + pos["y"]

    def neighbours(self):
        out = [(None, self.device(self.pos, 1 - self.core))]
        for d, length in self.sizes.items():
            if length == 2:
                out.append((None, self.device({**self.pos, d: 1 - self.pos[d]}, self.core)))
            elif length > 2:
                for s in (1, -1):
                    q = self.pos[d] + s
                    out.append(((q >= 0) & (q < length), self.device({**self.pos, d: q}, self.core)))
        return out


def when(conds, fn):
    conds = [c for c in conds if c is not None]
    if not conds:
        fn()
    else:
        pl.when(functools.reduce(jnp.logical_and, conds))(lambda: (fn(), None)[1])


def entry_barrier(place):
    barrier = pltpu.get_barrier_semaphore()
    total = 0
    for cond, dev in place.neighbours():
        when([cond], lambda dev=dev: pl.semaphore_signal(barrier, inc=1, device_id=dev, device_id_type=MESH))
        total = total + (1 if cond is None else cond.astype(jnp.int32))
    pl.semaphore_wait(barrier, total)


def gather_kernel(sizes, pieces, order, n_in, *refs):
    ins, outs = refs[:n_in], refs[n_in:2 * n_in]
    send_sem, recv_sem, pair_send, pair_recv, local_sem = refs[2 * n_in:]
    place = Place(sizes)
    pos, core = place.pos, place.core
    entry_barrier(place)
    partner = place.device(pos, 1 - core)
    locals_ = []
    for a in range(n_in):
        c = pltpu.make_async_copy(ins[a], outs[a].at[pos["x"], core, pos["z"], pos["y"]], local_sem.at[a])
        c.start()
        locals_.append(c)

    def part(pi, at, who):
        a, tree, lo, n = pieces[pi]
        return outs[a].at[at["x"], who, at["z"], at["y"], pl.ds(lo, n)]

    def remote(src, dst, send, recv, dev):
        return pltpu.make_async_remote_copy(src_ref=src, dst_ref=dst, send_sem=send, recv_sem=recv, device_id=dev, device_id_type=MESH)

    def line(d):
        if sizes[d] == 1:
            return []
        if sizes[d] == 2:
            return [(0, None, 1 - pos[d])]
        return [(0, pos[d] + 1 < sizes[d], pos[d] + 1), (1, pos[d] > 0, pos[d] - 1)]

    left = {}
    for pi, t in order:
        left[pi] = left.get(pi, 0) + 1
    seen = dict.fromkeys(left, 0)
    whole = [slice(None)] * 3
    for pi, t in order:
        a, tree, lo, n = pieces[pi]
        own = all(v == 0 for v in t)
        at, conds = dict(pos), []
        for d, v in zip(tree, t):
            if v == "o":
                at[d] = 1 - pos[d]
            elif v != 0:
                at[d] = pos[d] + v
                conds.append((at[d] >= 0) if v < 0 else (at[d] < sizes[d]))
        chip = place.chip(at)
        dst = part(pi, at, core)
        src = ins[a].at[pl.ds(lo, n)] if own else dst
        k = max([j for j, v in enumerate(t) if v != 0], default=-1)

        def handle(tree=tree, t=t, own=own, chip=chip, dst=dst, src=src, k=k, pi=pi):
            if not own:
                remote(dst, dst, pair_send.at[pi], recv_sem.at[pi, chip], partner).wait_recv()
            for j in (2, 1, 0):
                d = tree[j]
                if j < k:
                    continue
                for slot, ok, q in line(d):
                    if j == k and (t[j] == "o" or (t[j] < 0) != (slot == 0)):
                        continue
                    when([ok], remote(src, dst, send_sem.at[pi, 2 * "xyz".index(d) + slot], recv_sem.at[pi, chip],
                                      place.device({**pos, d: q}, core)).start)
            remote(src, dst, pair_send.at[pi], pair_recv.at[pi], partner).start()
        when(conds, handle)
        seen[pi] += 1

    full = dict.fromkeys("xyz", slice(None))
    for pi, (a, tree, lo, n) in enumerate(pieces):
        for j, d in enumerate(tree):
            at = {e: (slice(None) if tree.index(e) < j else pos[e]) for e in "xyz"}
            for slot, ok, q in line(d):
                sem = send_sem.at[pi, 2 * "xyz".index(d) + slot]
                if sizes[d] == 2:
                    ref = part(pi, at, core)
                    remote(ref, ref, sem, recv_sem.at[pi, 0], partner).wait_send()
                else:
                    for z in range(sizes[d]):
                        ref = part(pi, {**at, d: z}, core)
                        sent = (pos[d] >= z) if slot == 0 else (pos[d] <= z)
                        when([ok, sent], remote(ref, ref, sem, recv_sem.at[pi, 0], partner).wait_send)
        ref = part(pi, full, core)
        remote(ref, ref, pair_send.at[pi], pair_recv.at[pi], partner).wait_send()
        ref = part(pi, full, 1 - core)
        remote(ref, ref, pair_send.at[pi], pair_recv.at[pi], partner).wait_recv()
    for c in locals_:
        c.wait()


def gather_order(sizes, pieces, alpha):
    ev = []
    for pi, (a, tree, lo, n) in enumerate(pieces):
        for t in itertools.product(*[offsets(sizes[d]) for d in tree]):
            hops = sum(1 if v == "o" else abs(v) for v in t)
            ev.append((pi * alpha + hops, pi, t))
    ev.sort(key=lambda e: (e[0], e[1]))
    return [(pi, t) for _, pi, t in ev]


def gather(sizes, shards, alpha=0.05):
    chips = sizes["x"] * sizes["y"] * sizes["z"]
    pieces = []
    for a, s in enumerate(shards):
        tiles = s.shape[0] // 8
        if tiles % 3 == 0 and tiles < 12:
            cuts = [(i, i * tiles // 3, tiles // 3) for i in range(3)]
        elif tiles % 2 == 0:
            cuts = [(i, i * tiles // 2, tiles // 2) for i in range(2)]
        else:
            cuts = [(2, 0, tiles)]
        for tree, lo, n in cuts:
            pieces.append((a, TREES[tree], lo * 8, n * 8))
    order = gather_order(sizes, pieces, alpha)
    n_in = len(shards)
    return pl.pallas_call(
        functools.partial(gather_kernel, sizes, pieces, order, n_in),
        out_shape=[jax.ShapeDtypeStruct((sizes["x"], 2, sizes["z"], sizes["y"]) + s.shape, s.dtype) for s in shards],
        in_specs=[pl.BlockSpec(memory_space=pltpu.VMEM)] * n_in,
        out_specs=[pl.BlockSpec(memory_space=pl.ANY)] * n_in,
        scratch_shapes=[
            pltpu.SemaphoreType.DMA((len(pieces), 6)),
            pltpu.SemaphoreType.DMA((len(pieces), chips)),
            pltpu.SemaphoreType.DMA((len(pieces),)),
            pltpu.SemaphoreType.DMA((len(pieces),)),
            pltpu.SemaphoreType.DMA((n_in,)),
        ],
        compiler_params=pltpu.CompilerParams(collective_id=0, has_side_effects=True),
        name="gather",
    )(*shards)


class View:
    def __init__(self, ref, dims, fixed=None, core=None):
        self.ref, self.dims, self.fixed, self.core = ref, dims, fixed or {}, core

    def fix(self, d, v):
        return View(self.ref, self.dims, {**self.fixed, d: v}, self.core)

    def free(self):
        return [d for d in self.dims if d not in self.fixed]

    def index(self, at, cols=None):
        idx = [self.fixed.get(d, at.get(d, slice(None))) for d in self.dims]
        if self.core is not None:
            core, lo, n = self.core
            return (idx[0], core, *idx[1:], slice(None), pl.ds(lo, n))
        return tuple(idx)

    def whole(self):
        return self.ref.at[self.index({})]


def accumulate(sizes, dst, terms):
    dims = terms[0].free()

    def step(i, carry):
        at = {}
        for d in reversed(dims):
            at[d] = lax.rem(i, sizes[d])
            i = i // sizes[d]
        total = None
        for t in terms:
            v = t.ref[t.index(at)].astype(jnp.float32)
            total = v if total is None else total + v
        if isinstance(dst, View):
            dst.ref[dst.index(at)] = total.astype(dst.ref.dtype)
        else:
            dst(total)
        return carry

    count = 1
    for d in dims:
        count *= sizes[d]
    if count == 1:
        step(0, 0)
    else:
        lax.fori_loop(0, count, step, 0)


def piece_buffers(sizes, piece, rows):
    a, tree, lo, n = piece
    dims = list("xzy")
    shapes = [tuple(sizes[d] for d in dims) + (rows, n)]
    for d in tree:
        dims.remove(d)
        rest = tuple(sizes[e] for e in dims) + (rows, n)
        if sizes[d] == 2:
            shapes.append(rest)
        elif sizes[d] > 2:
            shapes += [(sizes[d],) + rest] * 2
    return shapes


def piece_copies(sizes, tree):
    return 1 + sum(0 if sizes[d] == 1 else 1 if sizes[d] == 2 else 2 * sizes[d] for d in tree)


def tree_loads(sizes, tree):
    share, loads = 1.0, {}
    for d in tree:
        loads[d] = share * (sizes[d] - 1) / sizes[d]
        share /= sizes[d]
    return loads


def cut(shapes):
    order = sorted(range(len(shapes)), key=lambda a: -shapes[a][0] * shapes[a][1])
    out = []
    for i, a in enumerate(order):
        rows, cols = shapes[a]
        wide = max(256, 18432 // rows // 256 * 256)
        lo, small = 0, [256, 512] if i == 0 else [256] * 9 if i == len(order) - 1 else []
        while lo < cols:
            n = min(small.pop(0) if small else wide, cols - lo)
            out.append((a, lo, n))
            lo += n
    return out


def plan(sizes, shapes, rates):
    make_us, pair_us, link_us, hop_us = rates
    used, pieces, size = dict.fromkeys("xyz", 0.0), [], {}
    for a, lo, n in cut(shapes):
        rows = shapes[a][0]
        units = rows * n / 6144

        def worst(tree):
            loads = tree_loads(sizes, tree)
            return max(used[d] + units * loads[d] for d in tree), used[tree[0]]

        tree = min(("xzy", "yzx", "xyz", "yxz"), key=worst)
        for d, v in tree_loads(sizes, tree).items():
            used[d] += units * v
        size[len(pieces)] = units
        pieces.append((a, tree, lo, n))
    order, free, heap, count = [], dict.fromkeys(("pair", "x", "y", "z"), 0.0), [], itertools.count()
    now = 0.0

    def push(t, pi, what):
        heapq.heappush(heap, (t, next(count), pi, what))

    def carry(link, t, us):
        free[link] = max(t, free[link]) + us
        return free[link] + hop_us

    def launch(t, pi, j):
        tree = pieces[pi][1]
        if j == 3:
            return
        d = tree[j]
        part = size[pi]
        for e in tree[:j + 1]:
            part /= sizes[e]
        if sizes[d] == 1:
            launch(t, pi, j + 1)
        elif sizes[d] == 2:
            push(carry(d, t, part * link_us), pi, ("swap", j))
        else:
            top = sizes[d] - 1
            arrive = [carry(d, t, part * link_us) for _ in range(top)]
            for hop in range(1, top):
                for dest in range(top, hop, -1):
                    when_us = arrive[top - dest] + (hop - 1) * (hop_us + part * link_us)
                    push(when_us, pi, ("up", j, hop, dest))
                    push(when_us, pi, ("down", j, top - hop, top - dest))
            push(arrive[-1] + (top - 1) * hop_us + part * link_us, pi, ("land", j))

    for pi in range(len(pieces)):
        now += make_us * size[pi]
        push(now, pi, ("make",))
    while heap:
        t, _, pi, what = heapq.heappop(heap)
        order.append((pi, what))
        if what[0] == "make":
            push(carry("pair", t, size[pi] / 2 * pair_us), pi, ("pair",))
        elif what[0] == "pair":
            launch(t, pi, 0)
        elif what[0] in ("swap", "land"):
            launch(t, pi, what[1] + 1)
    return pieces, order


def reduce_kernel(sizes, pieces, order, weights, *refs):
    lefts, rights, packed = refs[:weights], refs[weights:2 * weights], refs[2 * weights]
    outs, rest = refs[2 * weights + 1:3 * weights + 2], list(refs[3 * weights + 2:])
    send_sem, recv_sem = rest[-2:]
    ins, rest = [*rest[:weights], packed], rest[weights:]
    place = Place(sizes)
    pos, core = place.pos, place.core
    partner = place.device(pos, 1 - core)
    state, base, sent = [], 0, []
    for pi, (a, tree, lo, n) in enumerate(pieces):
        k = len(piece_buffers(sizes, pieces[pi], 8))
        bufs, rest = rest[:k], rest[k:]
        copies = {"pair": (0, 0)}
        c, b = 1, 1
        for j, d in enumerate(tree):
            if sizes[d] > 1:
                copies[j] = (c, b)
                c += 1 if sizes[d] == 2 else 2 * sizes[d]
                b += 1 if sizes[d] == 2 else 2
        state.append({"bufs": bufs, "base": base, "copies": copies, "cur": None})
        base += c

    def copy(src, dst, sem, dev):
        return pltpu.make_async_remote_copy(src_ref=src, dst_ref=dst, send_sem=send_sem.at[sem], recv_sem=recv_sem.at[sem], device_id=dev, device_id_type=MESH)

    def send(conds, src, dst, sem, dev):
        c = copy(src, dst, sem, dev)
        when(conds, c.start)
        sent.append((conds, c))

    def await_copy(buf, sem):
        copy(buf, buf, sem, partner).wait_recv()

    entry_barrier(place)

    def make(a, lo, n):
        total, rows = lefts[a].shape[0], ins[a].shape[4]
        places = list(itertools.product(*[range(v) for v in ins[a].shape[:4]]))
        step = min(total, 768)
        for top in range(0, total, step):
            for left in range(lo, lo + n, 256):
                cols = slice(left, min(left + 256, lo + n))
                block = dot(lefts[a][top:top + step, :], rights[a][:, cols]).astype(ins[a].dtype)
                for i in range(step // rows):
                    ins[a][(*places[top // rows + i], slice(None), cols)] = block[i * rows:(i + 1) * rows]

    def launch(pi, j):
        a, tree, lo, n = pieces[pi]
        st = state[pi]
        while j < 3 and sizes[tree[j]] == 1:
            st["cur"] = st["cur"].fix(tree[j], 0)
            j += 1
        if j == 3:
            return
        d, cur = tree[j], st["cur"]
        c, b = st["copies"][j]
        c += st["base"]
        p, size = pos[d], sizes[d]
        if size == 2:
            send([], cur.fix(d, 1 - p).whole(), st["bufs"][b], c, place.device({**pos, d: 1 - p}, core))
            return
        for t in range(size - 1, 0, -1):
            send([p == 0], cur.fix(d, t).whole(), st["bufs"][b].at[t], c + t, place.device({**pos, d: p + 1}, core))
            t = size - 1 - t
            send([p == size - 1], cur.fix(d, t).whole(), st["bufs"][b + 1].at[t], c + size + t, place.device({**pos, d: p - 1}, core))

    def run(pi, what):
        a, tree, lo, n = pieces[pi]
        st = state[pi]
        if what[0] == "make":
            if a < weights:
                make(a, lo, n)
            src = View(ins[a], list("xzy"), core=(1 - core, lo, n))
            send([], src.whole(), st["bufs"][0], st["base"], partner)
            return
        if what[0] == "pair":
            buf = st["bufs"][0]
            await_copy(buf, st["base"])
            mine = View(ins[a], list("xzy"), core=(core, lo, n))
            st["cur"] = View(buf, list("xzy"))
            accumulate(sizes, st["cur"], [st["cur"], mine])
            launch(pi, 0)
            return
        j = what[1]
        d, cur = tree[j], st["cur"]
        c, b = st["copies"][j]
        c += st["base"]
        p, size = pos[d], sizes[d]
        last = all(sizes[e] == 1 for e in tree[j + 1:])
        left = [e for e in cur.free() if e != d]

        def store(total):
            outs[a][:, pl.ds(lo, n)] = total

        if what[0] == "swap":
            buf = st["bufs"][b]
            await_copy(buf, c)
            new = View(buf, left)
            accumulate(sizes, store if last else new, [cur.fix(d, p), new])
            st["cur"] = new
            launch(pi, j + 1)
        elif what[0] in ("up", "down"):
            up = what[0] == "up"
            here, t = what[2], what[3]
            sem = c + t if up else c + size + t
            buf = st["bufs"][b if up else b + 1]

            def relay():
                await_copy(buf.at[t], sem)
                new = View(buf, [d] + left, {d: t})
                accumulate(sizes, new, [cur.fix(d, t), new])

            when([p == here], relay)
            send([p == here], buf.at[t], buf.at[t], sem, place.device({**pos, d: p + 1 if up else p - 1}, core))
        else:
            ups, downs = st["bufs"][b], st["bufs"][b + 1]
            new = cur.fix(d, p)
            below, above = View(ups, [d] + left, {d: p}), View(downs, [d] + left, {d: p})
            for p_below, p_above, conds in ((False, True, [p == 0]), (True, True, [p > 0, p < size - 1]), (True, False, [p == size - 1])):
                def land(p_below=p_below, p_above=p_above):
                    terms = [new]
                    if p_below:
                        await_copy(ups.at[p], c + p)
                        terms.append(below)
                    if p_above:
                        await_copy(downs.at[p], c + size + p)
                        terms.append(above)
                    accumulate(sizes, store if last else new, terms)
                when(conds, land)
            st["cur"] = new
            launch(pi, j + 1)

    for pi, what in order:
        run(pi, what)
    for conds, c in sent:
        when(conds, c.wait_send)


def reduce_scatter(sizes, factors, packed, rates=(0.3, 1.2, 4.3, 1.2)):
    chips = sizes["x"] * sizes["y"] * sizes["z"]
    lead = (sizes["x"], 2, sizes["z"], sizes["y"])
    low = [(left.shape[0] // (2 * chips), right.shape[1]) for left, right in factors]
    shapes = low + [packed.shape[-2:]]
    pieces, order = plan(sizes, shapes, rates)
    buffers, copies = [], 0
    for piece in pieces:
        kind = jnp.bfloat16 if piece[0] < len(low) else packed.dtype
        buffers += [pltpu.VMEM(s, kind) for s in piece_buffers(sizes, piece, shapes[piece[0]][0])]
        copies += piece_copies(sizes, piece[1])
    vmem = pl.BlockSpec(memory_space=pltpu.VMEM)
    return pl.pallas_call(
        functools.partial(reduce_kernel, sizes, pieces, order, len(low)),
        out_shape=[jax.ShapeDtypeStruct(s, jnp.float32) for s in shapes],
        in_specs=[vmem] * (2 * len(low) + 1),
        out_specs=[vmem] * len(shapes),
        scratch_shapes=[pltpu.VMEM(lead + s, jnp.bfloat16) for s in low] + buffers
        + [pltpu.SemaphoreType.DMA((copies,)), pltpu.SemaphoreType.DMA((copies,))],
        compiler_params=pltpu.CompilerParams(collective_id=1, has_side_effects=True, vmem_limit_bytes=67000000),
        name="reduce",
    )(*[left for left, _ in factors], *[right for _, right in factors], packed)


def finish_kernel(chunks, packed, *refs):
    n = (len(refs) - 1 - len(chunks)) // 3
    ins, outs, vectors, bufs, sems = refs[:n], refs[n:2 * n], refs[2 * n:2 * n + len(chunks)], refs[2 * n + len(chunks):-1], refs[-1]
    loads = [pltpu.make_async_copy(a, b, sems.at[0, i]) for i, (a, b) in enumerate(zip(ins, bufs))]
    stores = [pltpu.make_async_copy(b, o, sems.at[1, i]) for i, (b, o) in enumerate(zip(bufs, outs))]
    for c in loads:
        c.start()
    for i, w in enumerate(chunks):
        vectors[i][...] = packed[i:i + 1, :w]
    for c, o in zip(loads, stores):
        c.wait()
        o.start()
    for o in stores:
        o.wait()


def finish(chunks, arrays, packed):
    n = len(arrays)
    vmem, everywhere = pl.BlockSpec(memory_space=pltpu.VMEM), pl.BlockSpec(memory_space=pl.ANY)
    out = pl.pallas_call(
        functools.partial(finish_kernel, chunks),
        out_shape=[jax.ShapeDtypeStruct(a.shape, a.dtype) for a in arrays] + [jax.ShapeDtypeStruct((1, w), packed.dtype) for w in chunks],
        in_specs=[vmem] + [everywhere] * n,
        out_specs=[everywhere] * n + [vmem] * len(chunks),
        scratch_shapes=[pltpu.VMEM(a.shape, a.dtype) for a in arrays] + [pltpu.SemaphoreType.DMA((2, n))],
        name="finish",
    )(packed, *arrays)
    return out[:n], [v[0] for v in out[n:]]


HEAD_DIM = 64
PASSES = 4
EPSILON = 1e-05
SCORE_SCALE = 0.125
GELU_COEF = 0.7978845608028654
GELU_CUBE = 0.044715


def dot(left, right, dims=((1,), (0,))):
    return lax.dot_general(left, right, (dims, ((), ())), preferred_element_type=jnp.float32)


NT, TN = ((1,), (1,)), ((0,), (0,))


def normalise(values):
    centre = values - jnp.mean(values, axis=-1, keepdims=True)
    scale = lax.rsqrt(jnp.mean(centre * centre, axis=-1, keepdims=True) + EPSILON)
    return centre * scale, scale


def normalise_back(grad, unit, scale):
    return scale * (grad - jnp.mean(grad, axis=-1, keepdims=True) - unit * jnp.mean(grad * unit, axis=-1, keepdims=True))


def block_kernel(chunk, prepare, sections, lengths, token_mask, hidden, cotangent, g1, b1, qkv_b, out_b, g2, b2, fc_b, proj_b,
                 qkv_hbm, out_hbm, fc_hbm, proj_hbm,
                 hidden_out, grad_hidden, a_t, o_t, c_t, g_t, dqkv_st, do_st, du_st, dm_st,
                 dg1, db1, dqkv_b, dout_b, dg2, db2, dfc_b, dproj_b,
                 qkv_w, out_w, fc_w, proj_w, state, unit1, unit2, scale1, scale2, qkv_st, prob_st, slope_st, mixed, wide, allow, sems):
    rows, width = hidden.shape
    hidden_width = fc_w.shape[1]
    pair = 2 * HEAD_DIM
    pairs = width // pair
    loads = [pltpu.make_async_copy(src, dst, sems.at[i]) for i, (src, dst) in enumerate(
        ((qkv_hbm, qkv_w), (out_hbm, out_w), (fc_hbm, fc_w), (proj_hbm, proj_w)))]
    for c in loads:
        c.start()
    prepare()
    for ref in (dg1, db1, dqkv_b, dout_b, dg2, db2, dfc_b, dproj_b):
        ref[...] = jnp.zeros_like(ref)
    query = lax.broadcasted_iota(jnp.int32, (rows, 2 * rows), 0)
    key = lax.rem(lax.broadcasted_iota(jnp.int32, (rows, 2 * rows), 1), rows)
    ok = (key < lengths[0]) & (jnp.broadcast_to(jnp.concatenate([token_mask[...]] * 2, axis=1), (rows, 2 * rows)) == 1)
    allow[...] = jnp.where((key < query) & ok | (key == query), 1.0, 0.0)
    state[...] = hidden[...].astype(jnp.float32)
    first = lax.broadcasted_iota(jnp.int32, (rows, pair), 1) < HEAD_DIM

    def both(block):
        wide = block.astype(jnp.float32)
        return jnp.concatenate([jnp.where(first, wide, 0.0), jnp.where(first, 0.0, wide)], axis=0).astype(jnp.bfloat16)

    def merge(block):
        return jnp.where(first, block[:rows], block[rows:])

    def halves(fn, block, *others):
        return [fn(block[:, s], *(o[:, s] for o in others)) for s in (slice(0, rows), slice(rows, 2 * rows))]

    def forward(k, wait):
        x = state[...]
        unit, scale = normalise(x)
        unit1[k] = unit
        scale1[k] = jnp.broadcast_to(scale, scale1.shape[1:])
        at = pl.ds(pl.multiple_of(k * rows, rows), rows)
        a = (unit * g1[...] + b1[...]).astype(jnp.bfloat16)
        mixed[...] = a
        a_t[:, at] = a.T
        if wait:
            loads[0].wait()
        for lo in range(0, 3 * width, chunk):
            cols = slice(lo, lo + chunk)
            qkv_st[k, :, cols] = (dot(mixed[...], qkv_w[:, cols]) + qkv_b[:, cols]).astype(jnp.bfloat16)
        for i in range(pairs):
            q = qkv_st[k, :, i * pair:(i + 1) * pair]
            keys = both(qkv_st[k, :, width + i * pair:width + (i + 1) * pair])
            values = both(qkv_st[k, :, 2 * width + i * pair:2 * width + (i + 1) * pair])
            scores = jnp.where(allow[...] > 0.5, dot(q, keys, NT) * SCORE_SCALE, -1e30)

            def softmax(s):
                e = jnp.exp(s - jnp.max(s, axis=-1, keepdims=True))
                return e / jnp.sum(e, axis=-1, keepdims=True)

            probs = jnp.concatenate(halves(softmax, scores), axis=1)
            prob_st[k, i] = probs
            o = dot(probs.astype(jnp.bfloat16), values).astype(jnp.bfloat16)
            mixed[:, i * pair:(i + 1) * pair] = o
            o_t[i * pair:(i + 1) * pair, at] = o.T
        if wait:
            loads[1].wait()
        h = x + (dot(mixed[...], out_w[...]) + out_b[...])
        unit, scale = normalise(h)
        unit2[k] = unit
        scale2[k] = jnp.broadcast_to(scale, scale2.shape[1:])
        c = (unit * g2[...] + b2[...]).astype(jnp.bfloat16)
        mixed[...] = c
        c_t[:, at] = c.T
        if wait:
            loads[2].wait()
        for lo in range(0, hidden_width, chunk):
            cols = slice(lo, lo + chunk)
            u = dot(mixed[...], fc_w[:, cols]) + fc_b[:, cols]
            square = u * u
            t = jnp.tanh(GELU_COEF * (u + GELU_CUBE * (square * u)))
            half = 0.5 * (1.0 + t)
            g = (u * half).astype(jnp.bfloat16)
            wide[:, cols] = g
            g_t[cols, at] = g.T
            slope_st[k, :, cols] = half + 0.5 * u * (1.0 - t * t) * (GELU_COEF * (1.0 + 3.0 * GELU_CUBE * square))
        if wait:
            loads[3].wait()
        y = h + (dot(wide[...], proj_w[...]) + proj_b[...])

        @pl.when(sections[0] >= k)
        def _():
            state[...] = y

    forward(0, True)
    lax.fori_loop(1, PASSES, lambda k, c: (forward(k, False), c)[1], 0)
    hidden_out[...] = state[...].astype(jnp.bfloat16)
    state[...] = cotangent[...].astype(jnp.float32)

    def column_sums(ref, cols, block):
        ref[:, cols] += jnp.sum(block.astype(jnp.float32), axis=0, keepdims=True)

    def backward(step, carry):
        k = PASSES - 1 - step
        live = (sections[0] >= k).astype(jnp.float32)
        dx = state[...]
        dy = dx * live
        dm_st[k] = dy.astype(jnp.bfloat16)
        column_sums(dproj_b, slice(None), dm_st[k])
        for lo in range(0, hidden_width, chunk):
            cols = slice(lo, lo + chunk)
            du = (dot(dm_st[k], proj_w[cols, :], NT) * slope_st[k, :, cols]).astype(jnp.bfloat16)
            du_st[k, :, cols] = du
            column_sums(dfc_b, cols, du)
        dc = dot(du_st[k], fc_w[...], NT)
        unit = unit2[k]
        dg2[...] += jnp.sum(dc * unit, axis=0, keepdims=True)
        column_sums(db2, slice(None), dc)
        dh = dy + normalise_back(dc * g2[...], unit, scale2[k, :, 0:1])
        state[...] = dh + dx * (1.0 - live)
        do_st[k] = dh.astype(jnp.bfloat16)
        column_sums(dout_b, slice(None), do_st[k])
        mixed[...] = dot(do_st[k], out_w[...], NT).astype(jnp.bfloat16)
        for i in range(pairs):
            at = [slice(j * width + i * pair, j * width + (i + 1) * pair) for j in range(3)]
            q = qkv_st[k, :, at[0]]
            keys, values = both(qkv_st[k, :, at[1]]), both(qkv_st[k, :, at[2]])
            grad = mixed[:, at[0]]
            probs = prob_st[k, i]
            dp = dot(grad, values, NT)

            def scores_back(d, p):
                return p * (d - jnp.sum(d * p, axis=-1, keepdims=True))

            ds = jnp.concatenate(halves(scores_back, dp, probs), axis=1).astype(jnp.bfloat16)
            dv = merge(dot(probs.astype(jnp.bfloat16), grad, TN))
            dq = dot(ds, keys) * SCORE_SCALE
            dk = merge(dot(ds, q, TN)) * SCORE_SCALE
            for j, d in enumerate((dq, dk, dv)):
                dqkv_st[k, :, at[j]] = d.astype(jnp.bfloat16)
        column_sums(dqkv_b, slice(None), dqkv_st[k])
        da = dot(dqkv_st[k], qkv_w[...], NT)
        unit = unit1[k]
        dg1[...] += jnp.sum(da * unit, axis=0, keepdims=True)
        column_sums(db1, slice(None), da)
        state[...] += normalise_back(da * g1[...], unit, scale1[k, :, 0:1])
        return carry

    lax.fori_loop(0, PASSES, backward, 0)
    grad_hidden[...] = state[...]


VECTORS = ("g1", "b1", "qv_b", "out_b", "g2", "b2", "fc_b", "proj_b")


class Spread:
    def __init__(self, devices, w):
        n = devices * w

        def owner(shape):
            return jnp.floor((lax.broadcasted_iota(jnp.int32, shape, 1).astype(jnp.float32) + 0.5) * (1.0 / w))

        place = lax.broadcasted_iota(jnp.int32, (128, n), 1).astype(jnp.float32) - owner((128, n)) * w
        lane = lax.broadcasted_iota(jnp.int32, (128, n), 0).astype(jnp.float32)
        self.pick = jnp.where(place == lane, 1.0, 0.0).astype(jnp.bfloat16)
        self.mine = owner((devices, n)) == lax.broadcasted_iota(jnp.int32, (devices, n), 0).astype(jnp.float32)

    def join(self, rows):
        return jnp.sum(jnp.where(self.mine, dot(rows.astype(jnp.bfloat16), self.pick), 0.0), axis=0, keepdims=True)

    def split(self, joined):
        values = jnp.where(self.mine, jnp.broadcast_to(joined, self.mine.shape), 0.0)
        high = values.astype(jnp.bfloat16)
        low = (values - high.astype(jnp.float32)).astype(jnp.bfloat16)
        return dot(high, self.pick, NT) + dot(low, self.pick, NT)


def packed_kernel(chunk, chunks, *refs):
    ins, packed, weights, outs = refs[:5], refs[5], refs[6:10], refs[10:20]
    packed_out, rest = refs[20], refs[21:]
    scratch, vectors, grads = rest[:-16], rest[-16:-8], rest[-8:]
    devices = packed.shape[0] // 8
    width = ins[3].shape[1]

    def prepare():
        for w in sorted(set(chunks)):
            spread = Spread(devices, w)
            for i, c in enumerate(chunks):
                if c != w:
                    continue
                row = spread.join(packed[pl.ds(i, devices, stride=8), :])
                if VECTORS[i] == "qv_b":
                    vectors[i][:, :width] = row[:, :width]
                    vectors[i][:, width:2 * width] = jnp.zeros((1, width), jnp.float32)
                    vectors[i][:, 2 * width:] = row[:, width:]
                else:
                    vectors[i][...] = row

    block_kernel(chunk, prepare, *ins, *vectors, *weights, *outs, *grads, *scratch)
    for w in sorted(set(chunks)):
        spread = Spread(devices, w)
        for i, c in enumerate(chunks):
            if c == w:
                row = grads[i][...]
                if VECTORS[i] == "qv_b":
                    row = jnp.concatenate([row[:, :width], row[:, 2 * width:]], axis=1)
                packed_out[pl.ds(i, devices, stride=8), :] = spread.split(row)


def run_block(sections, lengths, token_mask, hidden, cotangent, vectors, chunks, weights):
    packed = chunks is not None
    qkv_w, out_w, fc_w, proj_w = weights
    rows, width = hidden.shape
    ff = fc_w.shape[1]
    low, high = jnp.bfloat16, jnp.float32
    sizes = [width, width, 3 * width, width, width, width, ff, width]
    if packed:
        given = [vectors]
    else:
        qv_b = vectors[2]
        bias = jnp.concatenate([qv_b[:width], jnp.zeros_like(qv_b[:width]), qv_b[width:]])
        given = [v.astype(high)[None] for v in (*vectors[:2], bias, *vectors[3:])]
    lefts, rights = [width, width, width, ff], [3 * width, width, ff, width]
    pairs = width // (2 * HEAD_DIM)
    chunk = 512 if ff % 512 == 0 and width * 3 % 512 == 0 else 256
    smem, vmem, everywhere = [pl.BlockSpec(memory_space=m) for m in (pltpu.SMEM, pltpu.VMEM, pl.ANY)]
    rows_of = [pltpu.VMEM((1, n), high) for n in sizes]
    outs = pl.pallas_call(
        functools.partial(packed_kernel, chunk, chunks) if packed else functools.partial(block_kernel, chunk, lambda: None),
        out_shape=[jax.ShapeDtypeStruct((rows, width), low), jax.ShapeDtypeStruct((rows, width), high)]
        + [jax.ShapeDtypeStruct((n, PASSES * rows), low) for n in lefts]
        + [jax.ShapeDtypeStruct((PASSES, rows, n), low) for n in rights]
        + [jax.ShapeDtypeStruct(v.shape, high) for v in given],
        in_specs=[smem] * 2 + [vmem] * (3 + len(given)) + [everywhere] * 4,
        out_specs=[vmem] * (10 + len(given)),
        scratch_shapes=[pltpu.VMEM(w.shape, low) for w in (qkv_w, out_w, fc_w, proj_w)] + [
            pltpu.VMEM((rows, width), high),
            pltpu.VMEM((PASSES, rows, width), high),
            pltpu.VMEM((PASSES, rows, width), high),
            pltpu.VMEM((PASSES, rows, 128), high),
            pltpu.VMEM((PASSES, rows, 128), high),
            pltpu.VMEM((PASSES, rows, 3 * width), low),
            pltpu.VMEM((PASSES, pairs, rows, 2 * rows), high),
            pltpu.VMEM((PASSES, rows, ff), high),
            pltpu.VMEM((rows, width), low),
            pltpu.VMEM((rows, ff), low),
            pltpu.VMEM((rows, 2 * rows), high),
            pltpu.SemaphoreType.DMA((4,)),
        ] + (rows_of * 2 if packed else []),
        compiler_params=pltpu.CompilerParams(vmem_limit_bytes=67000000),
        name="block",
    )(sections, lengths, token_mask, hidden, cotangent, *given, qkv_w, out_w, fc_w, proj_w)
    hidden_out, grad_hidden = outs[:2]
    a, o, c, g = outs[2:6]
    dqkv, do, du, dm = [s.reshape(PASSES * rows, -1) for s in outs[6:10]]
    factors = ((a, dqkv), (o, do), (c, du), (g, dm))
    if packed:
        return hidden_out, grad_hidden, factors, outs[10]
    grads = [v[0] for v in outs[10:]]
    grads[2] = jnp.concatenate([grads[2][:width], grads[2][2 * width:]])
    return hidden_out, grad_hidden, factors, grads


def fetch_all(sizes, big, small):
    if any(w.shape[0] % 8 for w in big):
        whole = [lax.all_gather(v, ("dp", "fsdp"), axis=0, tiled=True) for v in (*big, *small)]
        return whole[:4], whole[4:], None
    chunks = tuple(v.shape[0] for v in small)
    width = -(-max(chunks) // 128) * 128
    packed = jnp.stack([jnp.pad(v.astype(jnp.float32), (0, width - v.shape[0])) for v in small])
    *full, packed = [w.reshape(-1, w.shape[-1]) for w in gather(sizes, (*big, packed))]
    return full, packed, chunks


def sum_all(sizes, factors, vectors, chunks):
    if chunks is None:
        big = [dot(left, right).astype(jnp.bfloat16) for left, right in factors]
        qkv, out, fc, proj, *sums = [
            lax.psum_scatter(v, ("dp", "fsdp"), scatter_dimension=0, tiled=True).astype(jnp.float32) for v in (*big, *vectors)
        ]
    else:
        packed = vectors.reshape(sizes["x"], 2, sizes["z"], sizes["y"], 8, -1)
        *big, packed = reduce_scatter(sizes, factors, packed)
        (qkv, out, fc, proj), sums = finish(chunks, big, packed)
    g1, b1, qv, ob, g2, b2, fb, pb = sums
    return (g1, b1, qkv, qv, out, ob), (g2, b2, fc, fb, proj, pb)


def body(
    sizes,
    hidden,
    sections,
    lengths,
    token_mask,
    cotangent,
    ln1_gain,
    ln1_bias,
    qkv_weight,
    qv_bias,
    out_weight,
    out_bias,
    ln2_gain,
    ln2_bias,
    fc_weight,
    fc_bias,
    proj_weight,
    proj_bias,
):
    seq_count, seq_len, model_width = hidden.shape
    row_count = seq_count * seq_len
    weights, vectors, chunks = fetch_all(
        sizes,
        (qkv_weight, out_weight, fc_weight, proj_weight),
        (ln1_gain, ln1_bias, qv_bias, out_bias, ln2_gain, ln2_bias, fc_bias, proj_bias),
    )
    hidden_out, grad_hidden, factors, terms = run_block(
        sections, lengths, token_mask, hidden.reshape(row_count, model_width), cotangent.reshape(row_count, model_width),
        vectors, chunks, weights,
    )
    attention_grads, finished = sum_all(sizes, factors, terms, chunks)
    hidden_out = hidden_out.reshape(hidden.shape)
    grad_hidden = grad_hidden.reshape(hidden.shape)
    return (
        hidden_out,
        grad_hidden,
        attention_grads[0],
        attention_grads[1],
        attention_grads[2],
        attention_grads[3],
        attention_grads[4],
        attention_grads[5],
        finished[0],
        finished[1],
        finished[2],
        finished[3],
        finished[4],
        finished[5],
    )


def solution(mesh):
    chips_x = mesh.shape["dp"] // 2
    sizes = {"x": chips_x, "y": chips_x, "z": mesh.shape["fsdp"] // chips_x}
    return jax.shard_map(
        functools.partial(body, sizes),
        mesh=mesh,
        in_specs=(
            P(("dp", "fsdp"), None, None),
            P(("dp", "fsdp")),
            P(("dp", "fsdp")),
            P(("dp", "fsdp"), None),
            P(("dp", "fsdp"), None, None),
            P(("dp", "fsdp")),
            P(("dp", "fsdp")),
            P(("dp", "fsdp"), None),
            P(("dp", "fsdp")),
            P(("dp", "fsdp"), None),
            P(("dp", "fsdp")),
            P(("dp", "fsdp")),
            P(("dp", "fsdp")),
            P(("dp", "fsdp"), None),
            P(("dp", "fsdp")),
            P(("dp", "fsdp"), None),
            P(("dp", "fsdp")),
        ),
        out_specs=(
            P(("dp", "fsdp"), None, None),
            P(("dp", "fsdp"), None, None),
            P(("dp", "fsdp")),
            P(("dp", "fsdp")),
            P(("dp", "fsdp"), None),
            P(("dp", "fsdp")),
            P(("dp", "fsdp"), None),
            P(("dp", "fsdp")),
            P(("dp", "fsdp")),
            P(("dp", "fsdp")),
            P(("dp", "fsdp"), None),
            P(("dp", "fsdp")),
            P(("dp", "fsdp"), None),
            P(("dp", "fsdp")),
        ),
        check_vma=False,
    )
```

```python
import functools
import heapq
import itertools

import jax
import jax.numpy as jnp
from jax import lax
from jax.experimental import pallas as pl
from jax.experimental.pallas import tpu as pltpu
from jax.sharding import PartitionSpec as P
MESH = pl.DeviceIdType.MESH

TREES = ("zyx", "zxy", "xyz")


def offsets(length):
    return [0, "o"] if length == 2 else list(range(-(length - 1), length))


class Place:
    def __init__(self, sizes):
        self.sizes = sizes
        dp, fs = lax.axis_index("dp"), lax.axis_index("fsdp")
        self.core = lax.rem(dp, 2)
        self.pos = {"x": dp // 2, "z": fs // sizes["y"], "y": lax.rem(fs, sizes["y"])}

    def device(self, pos, core):
        return (pos["x"] * 2 + core, pos["z"] * self.sizes["y"] + pos["y"])

    def index(self, pos, core):
        dp, fs = self.device(pos, core)
        return dp * (self.sizes["z"] * self.sizes["y"]) + fs

    def chip(self, pos):
        return (pos["x"] * self.sizes["z"] + pos["z"]) * self.sizes["y"] + pos["y"]

    def neighbours(self):
        out = [(None, self.device(self.pos, 1 - self.core))]
        for d, length in self.sizes.items():
            if length == 2:
                out.append((None, self.device({**self.pos, d: 1 - self.pos[d]}, self.core)))
            elif length > 2:
                for s in (1, -1):
                    q = self.pos[d] + s
                    out.append(((q >= 0) & (q < length), self.device({**self.pos, d: q}, self.core)))
        return out


def when(conds, fn):
    conds = [c for c in conds if c is not None]
    if not conds:
        fn()
    else:
        pl.when(functools.reduce(jnp.logical_and, conds))(lambda: (fn(), None)[1])


def entry_barrier(place):
    barrier = pltpu.get_barrier_semaphore()
    total = 0
    for cond, dev in place.neighbours():
        when([cond], lambda dev=dev: pl.semaphore_signal(barrier, inc=1, device_id=dev, device_id_type=MESH))
        total = total + (1 if cond is None else cond.astype(jnp.int32))
    pl.semaphore_wait(barrier, total)


def gather_kernel(sizes, pieces, order, n_in, *refs):
    ins, outs = refs[:n_in], refs[n_in:2 * n_in]
    send_sem, recv_sem, pair_send, pair_recv, local_sem = refs[2 * n_in:]
    place = Place(sizes)
    pos, core = place.pos, place.core
    entry_barrier(place)
    partner = place.device(pos, 1 - core)
    locals_ = []
    for a in range(n_in):
        c = pltpu.make_async_copy(ins[a], outs[a].at[pos["x"], core, pos["z"], pos["y"]], local_sem.at[a])
        c.start()
        locals_.append(c)

    def part(pi, at, who):
        a, tree, lo, n = pieces[pi]
        return outs[a].at[at["x"], who, at["z"], at["y"], :, pl.ds(lo, n)]

    def remote(src, dst, send, recv, dev):
        return pltpu.make_async_remote_copy(src_ref=src, dst_ref=dst, send_sem=send, recv_sem=recv, device_id=dev, device_id_type=MESH)

    def line(d):
        if sizes[d] == 1:
            return []
        if sizes[d] == 2:
            return [(0, None, 1 - pos[d])]
        return [(0, pos[d] + 1 < sizes[d], pos[d] + 1), (1, pos[d] > 0, pos[d] - 1)]

    left = {}
    for pi, t in order:
        left[pi] = left.get(pi, 0) + 1
    seen = dict.fromkeys(left, 0)
    whole = [slice(None)] * 3
    for pi, t in order:
        a, tree, lo, n = pieces[pi]
        own = all(v == 0 for v in t)
        at, conds = dict(pos), []
        for d, v in zip(tree, t):
            if v == "o":
                at[d] = 1 - pos[d]
            elif v != 0:
                at[d] = pos[d] + v
                conds.append((at[d] >= 0) if v < 0 else (at[d] < sizes[d]))
        chip = place.chip(at)
        dst = part(pi, at, core)
        src = ins[a].at[:, pl.ds(lo, n)] if own else dst
        k = max([j for j, v in enumerate(t) if v != 0], default=-1)

        def handle(tree=tree, t=t, own=own, chip=chip, dst=dst, src=src, k=k, pi=pi):
            if not own:
                remote(dst, dst, pair_send.at[pi], recv_sem.at[pi, chip], partner).wait_recv()
            for j in (2, 1, 0):
                d = tree[j]
                if j < k:
                    continue
                for slot, ok, q in line(d):
                    if j == k and (t[j] == "o" or (t[j] < 0) != (slot == 0)):
                        continue
                    when([ok], remote(src, dst, send_sem.at[pi, 2 * "xyz".index(d) + slot], recv_sem.at[pi, chip],
                                      place.device({**pos, d: q}, core)).start)
            remote(src, dst, pair_send.at[pi], pair_recv.at[pi], partner).start()
        when(conds, handle)
        seen[pi] += 1

    full = dict.fromkeys("xyz", slice(None))
    for pi, (a, tree, lo, n) in enumerate(pieces):
        for j, d in enumerate(tree):
            at = {e: (slice(None) if tree.index(e) < j else pos[e]) for e in "xyz"}
            for slot, ok, q in line(d):
                sem = send_sem.at[pi, 2 * "xyz".index(d) + slot]
                if sizes[d] == 2:
                    ref = part(pi, at, core)
                    remote(ref, ref, sem, recv_sem.at[pi, 0], partner).wait_send()
                else:
                    for z in range(sizes[d]):
                        ref = part(pi, {**at, d: z}, core)
                        sent = (pos[d] >= z) if slot == 0 else (pos[d] <= z)
                        when([ok, sent], remote(ref, ref, sem, recv_sem.at[pi, 0], partner).wait_send)
        ref = part(pi, full, core)
        remote(ref, ref, pair_send.at[pi], pair_recv.at[pi], partner).wait_send()
        ref = part(pi, full, 1 - core)
        remote(ref, ref, pair_send.at[pi], pair_recv.at[pi], partner).wait_recv()
    for c in locals_:
        c.wait()


def gather_order(sizes, pieces, alpha):
    ev = []
    for pi, (a, tree, lo, n) in enumerate(pieces):
        for t in itertools.product(*[offsets(sizes[d]) for d in tree]):
            hops = sum(1 if v == "o" else abs(v) for v in t)
            ev.append((pi * alpha + hops, pi, t))
    ev.sort(key=lambda e: (e[0], e[1]))
    return [(pi, t) for _, pi, t in ev]


def gather(sizes, shards, alpha=0.05):
    chips = sizes["x"] * sizes["y"] * sizes["z"]
    pieces = []
    for a, s in enumerate(shards):
        tiles = s.shape[1] // 128
        first = [round(tiles * v) for v in ((0.0, 0.375, 0.78, 1.0) if a % 2 else (0.0, 0.4, 0.78, 1.0))]
        for tree, lo, hi in zip(TREES, first, first[1:]):
            if hi > lo:
                pieces.append((a, tree, lo * 128, (hi - lo) * 128))
    order = gather_order(sizes, pieces, alpha)
    n_in = len(shards)
    return pl.pallas_call(
        functools.partial(gather_kernel, sizes, pieces, order, n_in),
        out_shape=[jax.ShapeDtypeStruct((sizes["x"], 2, sizes["z"], sizes["y"]) + s.shape, s.dtype) for s in shards],
        in_specs=[pl.BlockSpec(memory_space=pltpu.VMEM)] * n_in,
        out_specs=[pl.BlockSpec(memory_space=pl.ANY)] * n_in,
        scratch_shapes=[
            pltpu.SemaphoreType.DMA((len(pieces), 6)),
            pltpu.SemaphoreType.DMA((len(pieces), chips)),
            pltpu.SemaphoreType.DMA((len(pieces),)),
            pltpu.SemaphoreType.DMA((len(pieces),)),
            pltpu.SemaphoreType.DMA((n_in,)),
        ],
        compiler_params=pltpu.CompilerParams(collective_id=0, has_side_effects=True),
        name="gather",
    )(*shards)


class View:
    def __init__(self, ref, dims, fixed=None, core=None):
        self.ref, self.dims, self.fixed, self.core = ref, dims, fixed or {}, core

    def fix(self, d, v):
        return View(self.ref, self.dims, {**self.fixed, d: v}, self.core)

    def free(self):
        return [d for d in self.dims if d not in self.fixed]

    def index(self, at, cols=None):
        idx = [self.fixed.get(d, at.get(d, slice(None))) for d in self.dims]
        if self.core is not None:
            core, lo, n = self.core
            return (idx[0], core, *idx[1:], slice(None), pl.ds(lo, n))
        return tuple(idx)

    def whole(self):
        return self.ref.at[self.index({})]


def accumulate(sizes, dst, terms):
    dims = terms[0].free()

    def step(i, carry):
        at = {}
        for d in reversed(dims):
            at[d] = lax.rem(i, sizes[d])
            i = i // sizes[d]
        total = None
        for t in terms:
            v = t.ref[t.index(at)].astype(jnp.float32)
            total = v if total is None else total + v
        if isinstance(dst, View):
            dst.ref[dst.index(at)] = total.astype(dst.ref.dtype)
        else:
            dst(total)
        return carry

    count = 1
    for d in dims:
        count *= sizes[d]
    if count == 1:
        step(0, 0)
    else:
        lax.fori_loop(0, count, step, 0)


def piece_buffers(sizes, piece, rows):
    a, tree, lo, n = piece
    dims = list("xzy")
    shapes = [tuple(sizes[d] for d in dims) + (rows, n)]
    for d in tree:
        dims.remove(d)
        rest = tuple(sizes[e] for e in dims) + (rows, n)
        if sizes[d] == 2:
            shapes.append(rest)
        elif sizes[d] > 2:
            shapes += [(sizes[d],) + rest] * 2
    return shapes


def piece_copies(sizes, tree):
    return 1 + sum(0 if sizes[d] == 1 else 1 if sizes[d] == 2 else 2 * sizes[d] for d in tree)


def tree_loads(sizes, tree):
    share, loads = 1.0, {}
    for d in tree:
        loads[d] = share * (sizes[d] - 1) / sizes[d]
        share /= sizes[d]
    return loads


def cut(shapes):
    order = sorted(range(len(shapes)), key=lambda a: -shapes[a][0] * shapes[a][1])
    out = []
    for i, a in enumerate(order):
        rows, cols = shapes[a]
        wide = max(256, 18432 // rows // 256 * 256)
        lo, small = 0, [256, 512] if i == 0 else [256] * 9 if i == len(order) - 1 else []
        while lo < cols:
            n = min(small.pop(0) if small else wide, cols - lo)
            out.append((a, lo, n))
            lo += n
    return out


def plan(sizes, shapes, rates):
    make_us, pair_us, link_us, hop_us = rates
    used, pieces, size = dict.fromkeys("xyz", 0.0), [], {}
    for a, lo, n in cut(shapes):
        rows = shapes[a][0]
        units = rows * n / 6144

        def worst(tree):
            loads = tree_loads(sizes, tree)
            return max(used[d] + units * loads[d] for d in tree), used[tree[0]]

        tree = min(("xzy", "yzx", "xyz", "yxz"), key=worst)
        for d, v in tree_loads(sizes, tree).items():
            used[d] += units * v
        size[len(pieces)] = units
        pieces.append((a, tree, lo, n))
    order, free, heap, count = [], dict.fromkeys(("pair", "x", "y", "z"), 0.0), [], itertools.count()
    now = 0.0

    def push(t, pi, what):
        heapq.heappush(heap, (t, next(count), pi, what))

    def carry(link, t, us):
        free[link] = max(t, free[link]) + us
        return free[link] + hop_us

    def launch(t, pi, j):
        tree = pieces[pi][1]
        if j == 3:
            return
        d = tree[j]
        part = size[pi]
        for e in tree[:j + 1]:
            part /= sizes[e]
        if sizes[d] == 1:
            launch(t, pi, j + 1)
        elif sizes[d] == 2:
            push(carry(d, t, part * link_us), pi, ("swap", j))
        else:
            top = sizes[d] - 1
            arrive = [carry(d, t, part * link_us) for _ in range(top)]
            for hop in range(1, top):
                for dest in range(top, hop, -1):
                    when_us = arrive[top - dest] + (hop - 1) * (hop_us + part * link_us)
                    push(when_us, pi, ("up", j, hop, dest))
                    push(when_us, pi, ("down", j, top - hop, top - dest))
            push(arrive[-1] + (top - 1) * hop_us + part * link_us, pi, ("land", j))

    for pi in range(len(pieces)):
        now += make_us * size[pi]
        push(now, pi, ("make",))
    while heap:
        t, _, pi, what = heapq.heappop(heap)
        order.append((pi, what))
        if what[0] == "make":
            push(carry("pair", t, size[pi] / 2 * pair_us), pi, ("pair",))
        elif what[0] == "pair":
            launch(t, pi, 0)
        elif what[0] in ("swap", "land"):
            launch(t, pi, what[1] + 1)
    return pieces, order


def reduce_kernel(sizes, pieces, order, weights, *refs):
    lefts, rights, packed = refs[:weights], refs[weights:2 * weights], refs[2 * weights]
    outs, rest = refs[2 * weights + 1:3 * weights + 2], list(refs[3 * weights + 2:])
    send_sem, recv_sem = rest[-2:]
    ins, rest = [*rest[:weights], packed], rest[weights:]
    place = Place(sizes)
    pos, core = place.pos, place.core
    partner = place.device(pos, 1 - core)
    state, base, sent = [], 0, []
    for pi, (a, tree, lo, n) in enumerate(pieces):
        k = len(piece_buffers(sizes, pieces[pi], 8))
        bufs, rest = rest[:k], rest[k:]
        copies = {"pair": (0, 0)}
        c, b = 1, 1
        for j, d in enumerate(tree):
            if sizes[d] > 1:
                copies[j] = (c, b)
                c += 1 if sizes[d] == 2 else 2 * sizes[d]
                b += 1 if sizes[d] == 2 else 2
        state.append({"bufs": bufs, "base": base, "copies": copies, "cur": None})
        base += c

    def copy(src, dst, sem, dev):
        return pltpu.make_async_remote_copy(src_ref=src, dst_ref=dst, send_sem=send_sem.at[sem], recv_sem=recv_sem.at[sem], device_id=dev, device_id_type=MESH)

    def send(conds, src, dst, sem, dev):
        c = copy(src, dst, sem, dev)
        when(conds, c.start)
        sent.append((conds, c))

    def await_copy(buf, sem):
        copy(buf, buf, sem, partner).wait_recv()

    entry_barrier(place)

    def make(a, lo, n):
        total, rows = lefts[a].shape[0], ins[a].shape[4]
        places = list(itertools.product(*[range(v) for v in ins[a].shape[:4]]))
        step = min(total, 768)
        for top in range(0, total, step):
            for left in range(lo, lo + n, 256):
                cols = slice(left, min(left + 256, lo + n))
                block = dot(lefts[a][top:top + step, :], rights[a][:, cols]).astype(ins[a].dtype)
                for i in range(step // rows):
                    ins[a][(*places[top // rows + i], slice(None), cols)] = block[i * rows:(i + 1) * rows]

    def launch(pi, j):
        a, tree, lo, n = pieces[pi]
        st = state[pi]
        while j < 3 and sizes[tree[j]] == 1:
            st["cur"] = st["cur"].fix(tree[j], 0)
            j += 1
        if j == 3:
            return
        d, cur = tree[j], st["cur"]
        c, b = st["copies"][j]
        c += st["base"]
        p, size = pos[d], sizes[d]
        if size == 2:
            send([], cur.fix(d, 1 - p).whole(), st["bufs"][b], c, place.device({**pos, d: 1 - p}, core))
            return
        for t in range(size - 1, 0, -1):
            send([p == 0], cur.fix(d, t).whole(), st["bufs"][b].at[t], c + t, place.device({**pos, d: p + 1}, core))
            t = size - 1 - t
            send([p == size - 1], cur.fix(d, t).whole(), st["bufs"][b + 1].at[t], c + size + t, place.device({**pos, d: p - 1}, core))

    def run(pi, what):
        a, tree, lo, n = pieces[pi]
        st = state[pi]
        if what[0] == "make":
            if a < weights:
                make(a, lo, n)
            src = View(ins[a], list("xzy"), core=(1 - core, lo, n))
            send([], src.whole(), st["bufs"][0], st["base"], partner)
            return
        if what[0] == "pair":
            buf = st["bufs"][0]
            await_copy(buf, st["base"])
            mine = View(ins[a], list("xzy"), core=(core, lo, n))
            st["cur"] = View(buf, list("xzy"))
            accumulate(sizes, st["cur"], [st["cur"], mine])
            launch(pi, 0)
            return
        j = what[1]
        d, cur = tree[j], st["cur"]
        c, b = st["copies"][j]
        c += st["base"]
        p, size = pos[d], sizes[d]
        last = all(sizes[e] == 1 for e in tree[j + 1:])
        left = [e for e in cur.free() if e != d]

        def store(total):
            outs[a][:, pl.ds(lo, n)] = total

        if what[0] == "swap":
            buf = st["bufs"][b]
            await_copy(buf, c)
            new = View(buf, left)
            accumulate(sizes, store if last else new, [cur.fix(d, p), new])
            st["cur"] = new
            launch(pi, j + 1)
        elif what[0] in ("up", "down"):
            up = what[0] == "up"
            here, t = what[2], what[3]
            sem = c + t if up else c + size + t
            buf = st["bufs"][b if up else b + 1]

            def relay():
                await_copy(buf.at[t], sem)
                new = View(buf, [d] + left, {d: t})
                accumulate(sizes, new, [cur.fix(d, t), new])

            when([p == here], relay)
            send([p == here], buf.at[t], buf.at[t], sem, place.device({**pos, d: p + 1 if up else p - 1}, core))
        else:
            ups, downs = st["bufs"][b], st["bufs"][b + 1]
            new = cur.fix(d, p)
            below, above = View(ups, [d] + left, {d: p}), View(downs, [d] + left, {d: p})
            for p_below, p_above, conds in ((False, True, [p == 0]), (True, True, [p > 0, p < size - 1]), (True, False, [p == size - 1])):
                def land(p_below=p_below, p_above=p_above):
                    terms = [new]
                    if p_below:
                        await_copy(ups.at[p], c + p)
                        terms.append(below)
                    if p_above:
                        await_copy(downs.at[p], c + size + p)
                        terms.append(above)
                    accumulate(sizes, store if last else new, terms)
                when(conds, land)
            st["cur"] = new
            launch(pi, j + 1)

    for pi, what in order:
        run(pi, what)
    for conds, c in sent:
        when(conds, c.wait_send)


def reduce_scatter(sizes, factors, packed, rates=(0.3, 1.2, 4.3, 1.2)):
    chips = sizes["x"] * sizes["y"] * sizes["z"]
    lead = (sizes["x"], 2, sizes["z"], sizes["y"])
    low = [(left.shape[0] // (2 * chips), right.shape[1]) for left, right in factors]
    shapes = low + [packed.shape[-2:]]
    pieces, order = plan(sizes, shapes, rates)
    buffers, copies = [], 0
    for piece in pieces:
        kind = jnp.bfloat16 if piece[0] < len(low) else packed.dtype
        buffers += [pltpu.VMEM(s, kind) for s in piece_buffers(sizes, piece, shapes[piece[0]][0])]
        copies += piece_copies(sizes, piece[1])
    vmem = pl.BlockSpec(memory_space=pltpu.VMEM)
    return pl.pallas_call(
        functools.partial(reduce_kernel, sizes, pieces, order, len(low)),
        out_shape=[jax.ShapeDtypeStruct(s, jnp.float32) for s in shapes],
        in_specs=[vmem] * (2 * len(low) + 1),
        out_specs=[vmem] * len(shapes),
        scratch_shapes=[pltpu.VMEM(lead + s, jnp.bfloat16) for s in low] + buffers
        + [pltpu.SemaphoreType.DMA((copies,)), pltpu.SemaphoreType.DMA((copies,))],
        compiler_params=pltpu.CompilerParams(collective_id=1, has_side_effects=True, vmem_limit_bytes=67000000),
        name="reduce",
    )(*[left for left, _ in factors], *[right for _, right in factors], packed)


def finish_kernel(chunks, packed, *refs):
    n = (len(refs) - 1 - len(chunks)) // 3
    ins, outs, vectors, bufs, sems = refs[:n], refs[n:2 * n], refs[2 * n:2 * n + len(chunks)], refs[2 * n + len(chunks):-1], refs[-1]
    loads = [pltpu.make_async_copy(a, b, sems.at[0, i]) for i, (a, b) in enumerate(zip(ins, bufs))]
    stores = [pltpu.make_async_copy(b, o, sems.at[1, i]) for i, (b, o) in enumerate(zip(bufs, outs))]
    for c in loads:
        c.start()
    for i, w in enumerate(chunks):
        vectors[i][...] = packed[i:i + 1, :w]
    for c, o in zip(loads, stores):
        c.wait()
        o.start()
    for o in stores:
        o.wait()


def finish(chunks, arrays, packed):
    n = len(arrays)
    vmem, everywhere = pl.BlockSpec(memory_space=pltpu.VMEM), pl.BlockSpec(memory_space=pl.ANY)
    out = pl.pallas_call(
        functools.partial(finish_kernel, chunks),
        out_shape=[jax.ShapeDtypeStruct(a.shape, a.dtype) for a in arrays] + [jax.ShapeDtypeStruct((1, w), packed.dtype) for w in chunks],
        in_specs=[vmem] + [everywhere] * n,
        out_specs=[everywhere] * n + [vmem] * len(chunks),
        scratch_shapes=[pltpu.VMEM(a.shape, a.dtype) for a in arrays] + [pltpu.SemaphoreType.DMA((2, n))],
        name="finish",
    )(packed, *arrays)
    return out[:n], [v[0] for v in out[n:]]


HEAD_DIM = 64
PASSES = 4
EPSILON = 1e-05
SCORE_SCALE = 0.125
GELU_COEF = 0.7978845608028654
GELU_CUBE = 0.044715


def dot(left, right, dims=((1,), (0,))):
    return lax.dot_general(left, right, (dims, ((), ())), preferred_element_type=jnp.float32)


NT, TN = ((1,), (1,)), ((0,), (0,))


def normalise(values):
    centre = values - jnp.mean(values, axis=-1, keepdims=True)
    scale = lax.rsqrt(jnp.mean(centre * centre, axis=-1, keepdims=True) + EPSILON)
    return centre * scale, scale


def normalise_back(grad, unit, scale):
    return scale * (grad - jnp.mean(grad, axis=-1, keepdims=True) - unit * jnp.mean(grad * unit, axis=-1, keepdims=True))


def block_kernel(chunk, prepare, sections, lengths, token_mask, hidden, cotangent, g1, b1, qkv_b, out_b, g2, b2, fc_b, proj_b,
                 qkv_hbm, out_hbm, fc_hbm, proj_hbm,
                 hidden_out, grad_hidden, a_t, o_t, c_t, g_t, dqkv_st, do_st, du_st, dm_st,
                 dg1, db1, dqkv_b, dout_b, dg2, db2, dfc_b, dproj_b,
                 qkv_w, out_w, fc_w, proj_w, state, unit1, unit2, scale1, scale2, qkv_st, prob_st, slope_st, mixed, wide, allow, sems):
    rows, width = hidden.shape
    hidden_width = fc_w.shape[1]
    pair = 2 * HEAD_DIM
    pairs = width // pair
    loads = [pltpu.make_async_copy(src, dst, sems.at[i]) for i, (src, dst) in enumerate(
        ((qkv_hbm, qkv_w), (out_hbm, out_w), (fc_hbm, fc_w), (proj_hbm, proj_w)))]
    for c in loads:
        c.start()
    prepare()
    for ref in (dg1, db1, dqkv_b, dout_b, dg2, db2, dfc_b, dproj_b):
        ref[...] = jnp.zeros_like(ref)
    query = lax.broadcasted_iota(jnp.int32, (rows, 2 * rows), 0)
    key = lax.rem(lax.broadcasted_iota(jnp.int32, (rows, 2 * rows), 1), rows)
    ok = (key < lengths[0]) & (jnp.broadcast_to(jnp.concatenate([token_mask[...]] * 2, axis=1), (rows, 2 * rows)) == 1)
    allow[...] = jnp.where((key < query) & ok | (key == query), 1.0, 0.0)
    state[...] = hidden[...].astype(jnp.float32)
    first = lax.broadcasted_iota(jnp.int32, (rows, pair), 1) < HEAD_DIM

    def both(block):
        wide = block.astype(jnp.float32)
        return jnp.concatenate([jnp.where(first, wide, 0.0), jnp.where(first, 0.0, wide)], axis=0).astype(jnp.bfloat16)

    def merge(block):
        return jnp.where(first, block[:rows], block[rows:])

    def halves(fn, block, *others):
        return [fn(block[:, s], *(o[:, s] for o in others)) for s in (slice(0, rows), slice(rows, 2 * rows))]

    def forward(k, wait):
        x = state[...]
        unit, scale = normalise(x)
        unit1[k] = unit
        scale1[k] = jnp.broadcast_to(scale, scale1.shape[1:])
        at = pl.ds(pl.multiple_of(k * rows, rows), rows)
        a = (unit * g1[...] + b1[...]).astype(jnp.bfloat16)
        mixed[...] = a
        a_t[:, at] = a.T
        if wait:
            loads[0].wait()
        for lo in range(0, 3 * width, chunk):
            cols = slice(lo, lo + chunk)
            qkv_st[k, :, cols] = (dot(mixed[...], qkv_w[:, cols]) + qkv_b[:, cols]).astype(jnp.bfloat16)
        for i in range(pairs):
            q = qkv_st[k, :, i * pair:(i + 1) * pair]
            keys = both(qkv_st[k, :, width + i * pair:width + (i + 1) * pair])
            values = both(qkv_st[k, :, 2 * width + i * pair:2 * width + (i + 1) * pair])
            scores = jnp.where(allow[...] > 0.5, dot(q, keys, NT) * SCORE_SCALE, -1e30)

            def softmax(s):
                e = jnp.exp(s - jnp.max(s, axis=-1, keepdims=True))
                return e / jnp.sum(e, axis=-1, keepdims=True)

            probs = jnp.concatenate(halves(softmax, scores), axis=1)
            prob_st[k, i] = probs
            o = dot(probs.astype(jnp.bfloat16), values).astype(jnp.bfloat16)
            mixed[:, i * pair:(i + 1) * pair] = o
            o_t[i * pair:(i + 1) * pair, at] = o.T
        if wait:
            loads[1].wait()
        h = x + (dot(mixed[...], out_w[...]) + out_b[...])
        unit, scale = normalise(h)
        unit2[k] = unit
        scale2[k] = jnp.broadcast_to(scale, scale2.shape[1:])
        c = (unit * g2[...] + b2[...]).astype(jnp.bfloat16)
        mixed[...] = c
        c_t[:, at] = c.T
        if wait:
            loads[2].wait()
        for lo in range(0, hidden_width, chunk):
            cols = slice(lo, lo + chunk)
            u = dot(mixed[...], fc_w[:, cols]) + fc_b[:, cols]
            square = u * u
            t = jnp.tanh(GELU_COEF * (u + GELU_CUBE * (square * u)))
            half = 0.5 * (1.0 + t)
            g = (u * half).astype(jnp.bfloat16)
            wide[:, cols] = g
            g_t[cols, at] = g.T
            slope_st[k, :, cols] = half + 0.5 * u * (1.0 - t * t) * (GELU_COEF * (1.0 + 3.0 * GELU_CUBE * square))
        if wait:
            loads[3].wait()
        y = h + (dot(wide[...], proj_w[...]) + proj_b[...])

        @pl.when(sections[0] >= k)
        def _():
            state[...] = y

    forward(0, True)
    lax.fori_loop(1, PASSES, lambda k, c: (forward(k, False), c)[1], 0)
    hidden_out[...] = state[...].astype(jnp.bfloat16)
    state[...] = cotangent[...].astype(jnp.float32)

    def column_sums(ref, cols, block):
        ref[:, cols] += jnp.sum(block.astype(jnp.float32), axis=0, keepdims=True)

    def backward(step, carry):
        k = PASSES - 1 - step
        live = (sections[0] >= k).astype(jnp.float32)
        dx = state[...]
        dy = dx * live
        dm_st[k] = dy.astype(jnp.bfloat16)
        column_sums(dproj_b, slice(None), dm_st[k])
        for lo in range(0, hidden_width, chunk):
            cols = slice(lo, lo + chunk)
            du = (dot(dm_st[k], proj_w[cols, :], NT) * slope_st[k, :, cols]).astype(jnp.bfloat16)
            du_st[k, :, cols] = du
            column_sums(dfc_b, cols, du)
        dc = dot(du_st[k], fc_w[...], NT)
        unit = unit2[k]
        dg2[...] += jnp.sum(dc * unit, axis=0, keepdims=True)
        column_sums(db2, slice(None), dc)
        dh = dy + normalise_back(dc * g2[...], unit, scale2[k, :, 0:1])
        state[...] = dh + dx * (1.0 - live)
        do_st[k] = dh.astype(jnp.bfloat16)
        column_sums(dout_b, slice(None), do_st[k])
        mixed[...] = dot(do_st[k], out_w[...], NT).astype(jnp.bfloat16)
        for i in range(pairs):
            at = [slice(j * width + i * pair, j * width + (i + 1) * pair) for j in range(3)]
            q = qkv_st[k, :, at[0]]
            keys, values = both(qkv_st[k, :, at[1]]), both(qkv_st[k, :, at[2]])
            grad = mixed[:, at[0]]
            probs = prob_st[k, i]
            dp = dot(grad, values, NT)

            def scores_back(d, p):
                return p * (d - jnp.sum(d * p, axis=-1, keepdims=True))

            ds = jnp.concatenate(halves(scores_back, dp, probs), axis=1).astype(jnp.bfloat16)
            dv = merge(dot(probs.astype(jnp.bfloat16), grad, TN))
            dq = dot(ds, keys) * SCORE_SCALE
            dk = merge(dot(ds, q, TN)) * SCORE_SCALE
            for j, d in enumerate((dq, dk, dv)):
                dqkv_st[k, :, at[j]] = d.astype(jnp.bfloat16)
        column_sums(dqkv_b, slice(None), dqkv_st[k])
        da = dot(dqkv_st[k], qkv_w[...], NT)
        unit = unit1[k]
        dg1[...] += jnp.sum(da * unit, axis=0, keepdims=True)
        column_sums(db1, slice(None), da)
        state[...] += normalise_back(da * g1[...], unit, scale1[k, :, 0:1])
        return carry

    lax.fori_loop(0, PASSES, backward, 0)
    grad_hidden[...] = state[...]


VECTORS = ("g1", "b1", "qv_b", "out_b", "g2", "b2", "fc_b", "proj_b")


class Spread:
    def __init__(self, devices, w):
        n = devices * w

        def owner(shape):
            return jnp.floor((lax.broadcasted_iota(jnp.int32, shape, 1).astype(jnp.float32) + 0.5) * (1.0 / w))

        place = lax.broadcasted_iota(jnp.int32, (128, n), 1).astype(jnp.float32) - owner((128, n)) * w
        lane = lax.broadcasted_iota(jnp.int32, (128, n), 0).astype(jnp.float32)
        self.pick = jnp.where(place == lane, 1.0, 0.0).astype(jnp.bfloat16)
        self.mine = owner((devices, n)) == lax.broadcasted_iota(jnp.int32, (devices, n), 0).astype(jnp.float32)

    def join(self, rows):
        return jnp.sum(jnp.where(self.mine, dot(rows.astype(jnp.bfloat16), self.pick), 0.0), axis=0, keepdims=True)

    def split(self, joined):
        values = jnp.where(self.mine, jnp.broadcast_to(joined, self.mine.shape), 0.0)
        high = values.astype(jnp.bfloat16)
        low = (values - high.astype(jnp.float32)).astype(jnp.bfloat16)
        return dot(high, self.pick, NT) + dot(low, self.pick, NT)


def packed_kernel(chunk, chunks, *refs):
    ins, packed, weights, outs = refs[:5], refs[5], refs[6:10], refs[10:20]
    packed_out, rest = refs[20], refs[21:]
    scratch, vectors, grads = rest[:-16], rest[-16:-8], rest[-8:]
    devices = packed.shape[0] // 8
    width = ins[3].shape[1]

    def prepare():
        for w in sorted(set(chunks)):
            spread = Spread(devices, w)
            for i, c in enumerate(chunks):
                if c != w:
                    continue
                row = spread.join(packed[pl.ds(i, devices, stride=8), :])
                if VECTORS[i] == "qv_b":
                    vectors[i][:, :width] = row[:, :width]
                    vectors[i][:, width:2 * width] = jnp.zeros((1, width), jnp.float32)
                    vectors[i][:, 2 * width:] = row[:, width:]
                else:
                    vectors[i][...] = row

    block_kernel(chunk, prepare, *ins, *vectors, *weights, *outs, *grads, *scratch)
    for w in sorted(set(chunks)):
        spread = Spread(devices, w)
        for i, c in enumerate(chunks):
            if c == w:
                row = grads[i][...]
                if VECTORS[i] == "qv_b":
                    row = jnp.concatenate([row[:, :width], row[:, 2 * width:]], axis=1)
                packed_out[pl.ds(i, devices, stride=8), :] = spread.split(row)


def run_block(sections, lengths, token_mask, hidden, cotangent, vectors, chunks, weights):
    packed = chunks is not None
    qkv_w, out_w, fc_w, proj_w = weights
    rows, width = hidden.shape
    ff = fc_w.shape[1]
    low, high = jnp.bfloat16, jnp.float32
    sizes = [width, width, 3 * width, width, width, width, ff, width]
    if packed:
        given = [vectors]
    else:
        qv_b = vectors[2]
        bias = jnp.concatenate([qv_b[:width], jnp.zeros_like(qv_b[:width]), qv_b[width:]])
        given = [v.astype(high)[None] for v in (*vectors[:2], bias, *vectors[3:])]
    lefts, rights = [width, width, width, ff], [3 * width, width, ff, width]
    pairs = width // (2 * HEAD_DIM)
    chunk = 512 if ff % 512 == 0 and width * 3 % 512 == 0 else 256
    smem, vmem, everywhere = [pl.BlockSpec(memory_space=m) for m in (pltpu.SMEM, pltpu.VMEM, pl.ANY)]
    rows_of = [pltpu.VMEM((1, n), high) for n in sizes]
    outs = pl.pallas_call(
        functools.partial(packed_kernel, chunk, chunks) if packed else functools.partial(block_kernel, chunk, lambda: None),
        out_shape=[jax.ShapeDtypeStruct((rows, width), low), jax.ShapeDtypeStruct((rows, width), high)]
        + [jax.ShapeDtypeStruct((n, PASSES * rows), low) for n in lefts]
        + [jax.ShapeDtypeStruct((PASSES, rows, n), low) for n in rights]
        + [jax.ShapeDtypeStruct(v.shape, high) for v in given],
        in_specs=[smem] * 2 + [vmem] * (3 + len(given)) + [everywhere] * 4,
        out_specs=[vmem] * (10 + len(given)),
        scratch_shapes=[pltpu.VMEM(w.shape, low) for w in (qkv_w, out_w, fc_w, proj_w)] + [
            pltpu.VMEM((rows, width), high),
            pltpu.VMEM((PASSES, rows, width), high),
            pltpu.VMEM((PASSES, rows, width), high),
            pltpu.VMEM((PASSES, rows, 128), high),
            pltpu.VMEM((PASSES, rows, 128), high),
            pltpu.VMEM((PASSES, rows, 3 * width), low),
            pltpu.VMEM((PASSES, pairs, rows, 2 * rows), high),
            pltpu.VMEM((PASSES, rows, ff), high),
            pltpu.VMEM((rows, width), low),
            pltpu.VMEM((rows, ff), low),
            pltpu.VMEM((rows, 2 * rows), high),
            pltpu.SemaphoreType.DMA((4,)),
        ] + (rows_of * 2 if packed else []),
        compiler_params=pltpu.CompilerParams(vmem_limit_bytes=67000000),
        name="block",
    )(sections, lengths, token_mask, hidden, cotangent, *given, qkv_w, out_w, fc_w, proj_w)
    hidden_out, grad_hidden = outs[:2]
    a, o, c, g = outs[2:6]
    dqkv, do, du, dm = [s.reshape(PASSES * rows, -1) for s in outs[6:10]]
    factors = ((a, dqkv), (o, do), (c, du), (g, dm))
    if packed:
        return hidden_out, grad_hidden, factors, outs[10]
    grads = [v[0] for v in outs[10:]]
    grads[2] = jnp.concatenate([grads[2][:width], grads[2][2 * width:]])
    return hidden_out, grad_hidden, factors, grads


def fetch_all(sizes, big, small):
    if any(w.shape[0] % 8 for w in big):
        whole = [lax.all_gather(v, ("dp", "fsdp"), axis=0, tiled=True) for v in (*big, *small)]
        return whole[:4], whole[4:], None
    chunks = tuple(v.shape[0] for v in small)
    width = -(-max(chunks) // 128) * 128
    packed = jnp.stack([jnp.pad(v.astype(jnp.float32), (0, width - v.shape[0])) for v in small])
    *full, packed = [w.reshape(-1, w.shape[-1]) for w in gather(sizes, (*big, packed))]
    return full, packed, chunks


def sum_all(sizes, factors, vectors, chunks):
    if chunks is None:
        big = [dot(left, right).astype(jnp.bfloat16) for left, right in factors]
        qkv, out, fc, proj, *sums = [
            lax.psum_scatter(v, ("dp", "fsdp"), scatter_dimension=0, tiled=True).astype(jnp.float32) for v in (*big, *vectors)
        ]
    else:
        packed = vectors.reshape(sizes["x"], 2, sizes["z"], sizes["y"], 8, -1)
        *big, packed = reduce_scatter(sizes, factors, packed)
        (qkv, out, fc, proj), sums = finish(chunks, big, packed)
    g1, b1, qv, ob, g2, b2, fb, pb = sums
    return (g1, b1, qkv, qv, out, ob), (g2, b2, fc, fb, proj, pb)


def body(
    sizes,
    hidden,
    sections,
    lengths,
    token_mask,
    cotangent,
    ln1_gain,
    ln1_bias,
    qkv_weight,
    qv_bias,
    out_weight,
    out_bias,
    ln2_gain,
    ln2_bias,
    fc_weight,
    fc_bias,
    proj_weight,
    proj_bias,
):
    seq_count, seq_len, model_width = hidden.shape
    row_count = seq_count * seq_len
    weights, vectors, chunks = fetch_all(
        sizes,
        (qkv_weight, out_weight, fc_weight, proj_weight),
        (ln1_gain, ln1_bias, qv_bias, out_bias, ln2_gain, ln2_bias, fc_bias, proj_bias),
    )
    hidden_out, grad_hidden, factors, terms = run_block(
        sections, lengths, token_mask, hidden.reshape(row_count, model_width), cotangent.reshape(row_count, model_width),
        vectors, chunks, weights,
    )
    attention_grads, finished = sum_all(sizes, factors, terms, chunks)
    hidden_out = hidden_out.reshape(hidden.shape)
    grad_hidden = grad_hidden.reshape(hidden.shape)
    return (
        hidden_out,
        grad_hidden,
        attention_grads[0],
        attention_grads[1],
        attention_grads[2],
        attention_grads[3],
        attention_grads[4],
        attention_grads[5],
        finished[0],
        finished[1],
        finished[2],
        finished[3],
        finished[4],
        finished[5],
    )


def solution(mesh):
    chips_x = mesh.shape["dp"] // 2
    sizes = {"x": chips_x, "y": chips_x, "z": mesh.shape["fsdp"] // chips_x}
    return jax.shard_map(
        functools.partial(body, sizes),
        mesh=mesh,
        in_specs=(
            P(("dp", "fsdp"), None, None),
            P(("dp", "fsdp")),
            P(("dp", "fsdp")),
            P(("dp", "fsdp"), None),
            P(("dp", "fsdp"), None, None),
            P(("dp", "fsdp")),
            P(("dp", "fsdp")),
            P(("dp", "fsdp"), None),
            P(("dp", "fsdp")),
            P(("dp", "fsdp"), None),
            P(("dp", "fsdp")),
            P(("dp", "fsdp")),
            P(("dp", "fsdp")),
            P(("dp", "fsdp"), None),
            P(("dp", "fsdp")),
            P(("dp", "fsdp"), None),
            P(("dp", "fsdp")),
        ),
        out_specs=(
            P(("dp", "fsdp"), None, None),
            P(("dp", "fsdp"), None, None),
            P(("dp", "fsdp")),
            P(("dp", "fsdp")),
            P(("dp", "fsdp"), None),
            P(("dp", "fsdp")),
            P(("dp", "fsdp"), None),
            P(("dp", "fsdp")),
            P(("dp", "fsdp")),
            P(("dp", "fsdp")),
            P(("dp", "fsdp"), None),
            P(("dp", "fsdp")),
            P(("dp", "fsdp"), None),
            P(("dp", "fsdp")),
        ),
        check_vma=False,
    )
```

```python
import functools
import heapq
import itertools

import jax
import jax.numpy as jnp
from jax import lax
from jax.experimental import pallas as pl
from jax.experimental.pallas import tpu as pltpu
from jax.sharding import PartitionSpec as P
MESH = pl.DeviceIdType.MESH

TREES = ("zyx", "zxy", "xyz")


def offsets(length):
    return [0, "o"] if length == 2 else list(range(-(length - 1), length))


class Place:
    def __init__(self, sizes):
        self.sizes = sizes
        dp, fs = lax.axis_index("dp"), lax.axis_index("fsdp")
        self.core = lax.rem(dp, 2)
        self.pos = {"x": dp // 2, "z": fs // sizes["y"], "y": lax.rem(fs, sizes["y"])}

    def device(self, pos, core):
        return (pos["x"] * 2 + core, pos["z"] * self.sizes["y"] + pos["y"])

    def index(self, pos, core):
        dp, fs = self.device(pos, core)
        return dp * (self.sizes["z"] * self.sizes["y"]) + fs

    def chip(self, pos):
        return (pos["x"] * self.sizes["z"] + pos["z"]) * self.sizes["y"] + pos["y"]

    def neighbours(self):
        out = [(None, self.device(self.pos, 1 - self.core))]
        for d, length in self.sizes.items():
            if length == 2:
                out.append((None, self.device({**self.pos, d: 1 - self.pos[d]}, self.core)))
            elif length > 2:
                for s in (1, -1):
                    q = self.pos[d] + s
                    out.append(((q >= 0) & (q < length), self.device({**self.pos, d: q}, self.core)))
        return out


def when(conds, fn):
    conds = [c for c in conds if c is not None]
    if not conds:
        fn()
    else:
        pl.when(functools.reduce(jnp.logical_and, conds))(lambda: (fn(), None)[1])


def entry_barrier(place):
    barrier = pltpu.get_barrier_semaphore()
    total = 0
    for cond, dev in place.neighbours():
        when([cond], lambda dev=dev: pl.semaphore_signal(barrier, inc=1, device_id=dev, device_id_type=MESH))
        total = total + (1 if cond is None else cond.astype(jnp.int32))
    pl.semaphore_wait(barrier, total)


def gather_kernel(sizes, pieces, order, n_in, *refs):
    ins, outs = refs[:n_in], refs[n_in:2 * n_in]
    send_sem, recv_sem, pair_send, pair_recv, local_sem = refs[2 * n_in:]
    place = Place(sizes)
    pos, core = place.pos, place.core
    entry_barrier(place)
    partner = place.device(pos, 1 - core)
    locals_ = []
    for a in range(n_in):
        c = pltpu.make_async_copy(ins[a], outs[a].at[pos["x"], core, pos["z"], pos["y"]], local_sem.at[a])
        c.start()
        locals_.append(c)

    def part(pi, at, who):
        a, tree, lo, n = pieces[pi]
        return outs[a].at[at["x"], who, at["z"], at["y"], pl.ds(lo, n)]

    def remote(src, dst, send, recv, dev):
        return pltpu.make_async_remote_copy(src_ref=src, dst_ref=dst, send_sem=send, recv_sem=recv, device_id=dev, device_id_type=MESH)

    def line(d):
        if sizes[d] == 1:
            return []
        if sizes[d] == 2:
            return [(0, None, 1 - pos[d])]
        return [(0, pos[d] + 1 < sizes[d], pos[d] + 1), (1, pos[d] > 0, pos[d] - 1)]

    left = {}
    for pi, t in order:
        left[pi] = left.get(pi, 0) + 1
    seen = dict.fromkeys(left, 0)
    whole = [slice(None)] * 3
    for pi, t in order:
        a, tree, lo, n = pieces[pi]
        own = all(v == 0 for v in t)
        at, conds = dict(pos), []
        for d, v in zip(tree, t):
            if v == "o":
                at[d] = 1 - pos[d]
            elif v != 0:
                at[d] = pos[d] + v
                conds.append((at[d] >= 0) if v < 0 else (at[d] < sizes[d]))
        chip = place.chip(at)
        dst = part(pi, at, core)
        src = ins[a].at[pl.ds(lo, n)] if own else dst
        k = max([j for j, v in enumerate(t) if v != 0], default=-1)

        def handle(tree=tree, t=t, own=own, chip=chip, dst=dst, src=src, k=k, pi=pi):
            if not own:
                remote(dst, dst, pair_send.at[pi], recv_sem.at[pi, chip], partner).wait_recv()
            for j in (2, 1, 0):
                d = tree[j]
                if j < k:
                    continue
                for slot, ok, q in line(d):
                    if j == k and (t[j] == "o" or (t[j] < 0) != (slot == 0)):
                        continue
                    when([ok], remote(src, dst, send_sem.at[pi, 2 * "xyz".index(d) + slot], recv_sem.at[pi, chip],
                                      place.device({**pos, d: q}, core)).start)
            remote(src, dst, pair_send.at[pi], pair_recv.at[pi], partner).start()
        when(conds, handle)
        seen[pi] += 1

    full = dict.fromkeys("xyz", slice(None))
    for pi, (a, tree, lo, n) in enumerate(pieces):
        for j, d in enumerate(tree):
            at = {e: (slice(None) if tree.index(e) < j else pos[e]) for e in "xyz"}
            for slot, ok, q in line(d):
                sem = send_sem.at[pi, 2 * "xyz".index(d) + slot]
                if sizes[d] == 2:
                    ref = part(pi, at, core)
                    remote(ref, ref, sem, recv_sem.at[pi, 0], partner).wait_send()
                else:
                    for z in range(sizes[d]):
                        ref = part(pi, {**at, d: z}, core)
                        sent = (pos[d] >= z) if slot == 0 else (pos[d] <= z)
                        when([ok, sent], remote(ref, ref, sem, recv_sem.at[pi, 0], partner).wait_send)
        ref = part(pi, full, core)
        remote(ref, ref, pair_send.at[pi], pair_recv.at[pi], partner).wait_send()
        ref = part(pi, full, 1 - core)
        remote(ref, ref, pair_send.at[pi], pair_recv.at[pi], partner).wait_recv()
    for c in locals_:
        c.wait()


def gather_order(sizes, pieces, alpha):
    ev = []
    for pi, (a, tree, lo, n) in enumerate(pieces):
        for t in itertools.product(*[offsets(sizes[d]) for d in tree]):
            hops = sum(1 if v == "o" else abs(v) for v in t)
            ev.append((pi * alpha + hops, pi, t))
    ev.sort(key=lambda e: (e[0], e[1]))
    return [(pi, t) for _, pi, t in ev]


def gather(sizes, shards, alpha=0.05):
    chips = sizes["x"] * sizes["y"] * sizes["z"]
    pieces = []
    for a, s in enumerate(shards):
        tiles = s.shape[0] // 8
        if tiles % 3 == 0 and tiles < 12:
            cuts = [(i, i * tiles // 3, tiles // 3) for i in range(3)]
        elif tiles % 2 == 0:
            cuts = [(i, i * tiles // 2, tiles // 2) for i in range(2)]
        else:
            cuts = [(2, 0, tiles)]
        for tree, lo, n in cuts:
            pieces.append((a, TREES[tree], lo * 8, n * 8))
    order = gather_order(sizes, pieces, alpha)
    n_in = len(shards)
    return pl.pallas_call(
        functools.partial(gather_kernel, sizes, pieces, order, n_in),
        out_shape=[jax.ShapeDtypeStruct((sizes["x"], 2, sizes["z"], sizes["y"]) + s.shape, s.dtype) for s in shards],
        in_specs=[pl.BlockSpec(memory_space=pltpu.VMEM)] * n_in,
        out_specs=[pl.BlockSpec(memory_space=pl.ANY)] * n_in,
        scratch_shapes=[
            pltpu.SemaphoreType.DMA((len(pieces), 6)),
            pltpu.SemaphoreType.DMA((len(pieces), chips)),
            pltpu.SemaphoreType.DMA((len(pieces),)),
            pltpu.SemaphoreType.DMA((len(pieces),)),
            pltpu.SemaphoreType.DMA((n_in,)),
        ],
        compiler_params=pltpu.CompilerParams(collective_id=0, has_side_effects=True),
        name="gather",
    )(*shards)


class View:
    def __init__(self, ref, dims, fixed=None, core=None):
        self.ref, self.dims, self.fixed, self.core = ref, dims, fixed or {}, core

    def fix(self, d, v):
        return View(self.ref, self.dims, {**self.fixed, d: v}, self.core)

    def free(self):
        return [d for d in self.dims if d not in self.fixed]

    def index(self, at, cols=None):
        idx = [self.fixed.get(d, at.get(d, slice(None))) for d in self.dims]
        if self.core is not None:
            core, lo, n = self.core
            return (idx[0], core, *idx[1:], slice(None), pl.ds(lo, n))
        return tuple(idx)

    def whole(self):
        return self.ref.at[self.index({})]


def accumulate(sizes, dst, terms):
    dims = terms[0].free()

    def step(i, carry):
        at = {}
        for d in reversed(dims):
            at[d] = lax.rem(i, sizes[d])
            i = i // sizes[d]
        total = None
        for t in terms:
            v = t.ref[t.index(at)].astype(jnp.float32)
            total = v if total is None else total + v
        if isinstance(dst, View):
            dst.ref[dst.index(at)] = total.astype(dst.ref.dtype)
        else:
            dst(total)
        return carry

    count = 1
    for d in dims:
        count *= sizes[d]
    if count == 1:
        step(0, 0)
    else:
        lax.fori_loop(0, count, step, 0)


def piece_buffers(sizes, piece, rows):
    a, tree, lo, n = piece
    dims = list("xzy")
    shapes = [tuple(sizes[d] for d in dims) + (rows, n)]
    for d in tree:
        dims.remove(d)
        rest = tuple(sizes[e] for e in dims) + (rows, n)
        if sizes[d] == 2:
            shapes.append(rest)
        elif sizes[d] > 2:
            shapes += [(sizes[d],) + rest] * 2
    return shapes


def piece_copies(sizes, tree):
    return 1 + sum(0 if sizes[d] == 1 else 1 if sizes[d] == 2 else 2 * sizes[d] for d in tree)


def tree_loads(sizes, tree):
    share, loads = 1.0, {}
    for d in tree:
        loads[d] = share * (sizes[d] - 1) / sizes[d]
        share /= sizes[d]
    return loads


def cut(shapes):
    order = sorted(range(len(shapes)), key=lambda a: -shapes[a][0] * shapes[a][1])
    out = []
    for i, a in enumerate(order):
        rows, cols = shapes[a]
        wide = max(256, 18432 // rows // 256 * 256)
        lo, small = 0, [256, 512] if i == 0 else [256] * 9 if i == len(order) - 1 else []
        while lo < cols:
            n = min(small.pop(0) if small else wide, cols - lo)
            out.append((a, lo, n))
            lo += n
    return out


def plan(sizes, shapes, rates):
    make_us, pair_us, link_us, hop_us = rates
    used, pieces, size = dict.fromkeys("xyz", 0.0), [], {}
    for a, lo, n in cut(shapes):
        rows = shapes[a][0]
        units = rows * n / 6144

        def worst(tree):
            loads = tree_loads(sizes, tree)
            return max(used[d] + units * loads[d] for d in tree), used[tree[0]]

        tree = min(("xzy", "yzx", "xyz", "yxz"), key=worst)
        for d, v in tree_loads(sizes, tree).items():
            used[d] += units * v
        size[len(pieces)] = units
        pieces.append((a, tree, lo, n))
    order, free, heap, count = [], dict.fromkeys(("pair", "x", "y", "z"), 0.0), [], itertools.count()
    now = 0.0

    def push(t, pi, what):
        heapq.heappush(heap, (t, next(count), pi, what))

    def carry(link, t, us):
        free[link] = max(t, free[link]) + us
        return free[link] + hop_us

    def launch(t, pi, j):
        tree = pieces[pi][1]
        if j == 3:
            return
        d = tree[j]
        part = size[pi]
        for e in tree[:j + 1]:
            part /= sizes[e]
        if sizes[d] == 1:
            launch(t, pi, j + 1)
        elif sizes[d] == 2:
            push(carry(d, t, part * link_us), pi, ("swap", j))
        else:
            top = sizes[d] - 1
            arrive = [carry(d, t, part * link_us) for _ in range(top)]
            for hop in range(1, top):
                for dest in range(top, hop, -1):
                    when_us = arrive[top - dest] + (hop - 1) * (hop_us + part * link_us)
                    push(when_us, pi, ("up", j, hop, dest))
                    push(when_us, pi, ("down", j, top - hop, top - dest))
            push(arrive[-1] + (top - 1) * hop_us + part * link_us, pi, ("land", j))

    for pi in range(len(pieces)):
        now += make_us * size[pi]
        push(now, pi, ("make",))
    while heap:
        t, _, pi, what = heapq.heappop(heap)
        order.append((pi, what))
        if what[0] == "make":
            push(carry("pair", t, size[pi] / 2 * pair_us), pi, ("pair",))
        elif what[0] == "pair":
            launch(t, pi, 0)
        elif what[0] in ("swap", "land"):
            launch(t, pi, what[1] + 1)
    return pieces, order


def reduce_kernel(sizes, pieces, order, weights, *refs):
    lefts, rights, packed = refs[:weights], refs[weights:2 * weights], refs[2 * weights]
    outs, rest = refs[2 * weights + 1:3 * weights + 2], list(refs[3 * weights + 2:])
    send_sem, recv_sem = rest[-2:]
    ins, rest = [*rest[:weights], packed], rest[weights:]
    place = Place(sizes)
    pos, core = place.pos, place.core
    partner = place.device(pos, 1 - core)
    state, base, sent = [], 0, []
    for pi, (a, tree, lo, n) in enumerate(pieces):
        k = len(piece_buffers(sizes, pieces[pi], 8))
        bufs, rest = rest[:k], rest[k:]
        copies = {"pair": (0, 0)}
        c, b = 1, 1
        for j, d in enumerate(tree):
            if sizes[d] > 1:
                copies[j] = (c, b)
                c += 1 if sizes[d] == 2 else 2 * sizes[d]
                b += 1 if sizes[d] == 2 else 2
        state.append({"bufs": bufs, "base": base, "copies": copies, "cur": None})
        base += c

    def copy(src, dst, sem, dev):
        return pltpu.make_async_remote_copy(src_ref=src, dst_ref=dst, send_sem=send_sem.at[sem], recv_sem=recv_sem.at[sem], device_id=dev, device_id_type=MESH)

    def send(conds, src, dst, sem, dev):
        c = copy(src, dst, sem, dev)
        when(conds, c.start)
        sent.append((conds, c))

    def await_copy(buf, sem):
        copy(buf, buf, sem, partner).wait_recv()

    entry_barrier(place)

    def make(a, lo, n):
        total, rows = lefts[a].shape[0], ins[a].shape[4]
        places = list(itertools.product(*[range(v) for v in ins[a].shape[:4]]))
        step = min(total, 768)
        for top in range(0, total, step):
            for left in range(lo, lo + n, 256):
                cols = slice(left, min(left + 256, lo + n))
                block = dot(lefts[a][top:top + step, :], rights[a][:, cols]).astype(ins[a].dtype)
                for i in range(step // rows):
                    ins[a][(*places[top // rows + i], slice(None), cols)] = block[i * rows:(i + 1) * rows]

    def launch(pi, j):
        a, tree, lo, n = pieces[pi]
        st = state[pi]
        while j < 3 and sizes[tree[j]] == 1:
            st["cur"] = st["cur"].fix(tree[j], 0)
            j += 1
        if j == 3:
            return
        d, cur = tree[j], st["cur"]
        c, b = st["copies"][j]
        c += st["base"]
        p, size = pos[d], sizes[d]
        if size == 2:
            send([], cur.fix(d, 1 - p).whole(), st["bufs"][b], c, place.device({**pos, d: 1 - p}, core))
            return
        for t in range(size - 1, 0, -1):
            send([p == 0], cur.fix(d, t).whole(), st["bufs"][b].at[t], c + t, place.device({**pos, d: p + 1}, core))
            t = size - 1 - t
            send([p == size - 1], cur.fix(d, t).whole(), st["bufs"][b + 1].at[t], c + size + t, place.device({**pos, d: p - 1}, core))

    def run(pi, what):
        a, tree, lo, n = pieces[pi]
        st = state[pi]
        if what[0] == "make":
            if a < weights:
                make(a, lo, n)
            src = View(ins[a], list("xzy"), core=(1 - core, lo, n))
            send([], src.whole(), st["bufs"][0], st["base"], partner)
            return
        if what[0] == "pair":
            buf = st["bufs"][0]
            await_copy(buf, st["base"])
            mine = View(ins[a], list("xzy"), core=(core, lo, n))
            st["cur"] = View(buf, list("xzy"))
            accumulate(sizes, st["cur"], [st["cur"], mine])
            launch(pi, 0)
            return
        j = what[1]
        d, cur = tree[j], st["cur"]
        c, b = st["copies"][j]
        c += st["base"]
        p, size = pos[d], sizes[d]
        last = all(sizes[e] == 1 for e in tree[j + 1:])
        left = [e for e in cur.free() if e != d]

        def store(total):
            outs[a][:, pl.ds(lo, n)] = total

        if what[0] == "swap":
            buf = st["bufs"][b]
            await_copy(buf, c)
            new = View(buf, left)
            accumulate(sizes, store if last else new, [cur.fix(d, p), new])
            st["cur"] = new
            launch(pi, j + 1)
        elif what[0] in ("up", "down"):
            up = what[0] == "up"
            here, t = what[2], what[3]
            sem = c + t if up else c + size + t
            buf = st["bufs"][b if up else b + 1]

            def relay():
                await_copy(buf.at[t], sem)
                new = View(buf, [d] + left, {d: t})
                accumulate(sizes, new, [cur.fix(d, t), new])

            when([p == here], relay)
            send([p == here], buf.at[t], buf.at[t], sem, place.device({**pos, d: p + 1 if up else p - 1}, core))
        else:
            ups, downs = st["bufs"][b], st["bufs"][b + 1]
            new = cur.fix(d, p)
            below, above = View(ups, [d] + left, {d: p}), View(downs, [d] + left, {d: p})
            for p_below, p_above, conds in ((False, True, [p == 0]), (True, True, [p > 0, p < size - 1]), (True, False, [p == size - 1])):
                def land(p_below=p_below, p_above=p_above):
                    terms = [new]
                    if p_below:
                        await_copy(ups.at[p], c + p)
                        terms.append(below)
                    if p_above:
                        await_copy(downs.at[p], c + size + p)
                        terms.append(above)
                    accumulate(sizes, store if last else new, terms)
                when(conds, land)
            st["cur"] = new
            launch(pi, j + 1)

    for pi, what in order:
        run(pi, what)
    for conds, c in sent:
        when(conds, c.wait_send)


def reduce_scatter(sizes, factors, packed, rates=(0.3, 1.2, 4.3, 1.2)):
    chips = sizes["x"] * sizes["y"] * sizes["z"]
    lead = (sizes["x"], 2, sizes["z"], sizes["y"])
    low = [(left.shape[0] // (2 * chips), right.shape[1]) for left, right in factors]
    shapes = low + [packed.shape[-2:]]
    pieces, order = plan(sizes, shapes, rates)
    buffers, copies = [], 0
    for piece in pieces:
        kind = jnp.bfloat16 if piece[0] < len(low) else packed.dtype
        buffers += [pltpu.VMEM(s, kind) for s in piece_buffers(sizes, piece, shapes[piece[0]][0])]
        copies += piece_copies(sizes, piece[1])
    vmem = pl.BlockSpec(memory_space=pltpu.VMEM)
    return pl.pallas_call(
        functools.partial(reduce_kernel, sizes, pieces, order, len(low)),
        out_shape=[jax.ShapeDtypeStruct(s, jnp.float32) for s in shapes],
        in_specs=[vmem] * (2 * len(low) + 1),
        out_specs=[vmem] * len(shapes),
        scratch_shapes=[pltpu.VMEM(lead + s, jnp.bfloat16) for s in low] + buffers
        + [pltpu.SemaphoreType.DMA((copies,)), pltpu.SemaphoreType.DMA((copies,))],
        compiler_params=pltpu.CompilerParams(collective_id=1, has_side_effects=True, vmem_limit_bytes=67000000),
        name="reduce",
    )(*[left for left, _ in factors], *[right for _, right in factors], packed)


def finish_kernel(chunks, packed, *refs):
    n = (len(refs) - 1 - len(chunks)) // 3
    ins, outs, vectors, bufs, sems = refs[:n], refs[n:2 * n], refs[2 * n:2 * n + len(chunks)], refs[2 * n + len(chunks):-1], refs[-1]
    loads = [pltpu.make_async_copy(a, b, sems.at[0, i]) for i, (a, b) in enumerate(zip(ins, bufs))]
    stores = [pltpu.make_async_copy(b, o, sems.at[1, i]) for i, (b, o) in enumerate(zip(bufs, outs))]
    for c in loads:
        c.start()
    for i, w in enumerate(chunks):
        vectors[i][...] = packed[i:i + 1, :w]
    for c, o in zip(loads, stores):
        c.wait()
        o.start()
    for o in stores:
        o.wait()


def finish(chunks, arrays, packed):
    n = len(arrays)
    vmem, everywhere = pl.BlockSpec(memory_space=pltpu.VMEM), pl.BlockSpec(memory_space=pl.ANY)
    out = pl.pallas_call(
        functools.partial(finish_kernel, chunks),
        out_shape=[jax.ShapeDtypeStruct(a.shape, a.dtype) for a in arrays] + [jax.ShapeDtypeStruct((1, w), packed.dtype) for w in chunks],
        in_specs=[vmem] + [everywhere] * n,
        out_specs=[everywhere] * n + [vmem] * len(chunks),
        scratch_shapes=[pltpu.VMEM(a.shape, a.dtype) for a in arrays] + [pltpu.SemaphoreType.DMA((2, n))],
        name="finish",
    )(packed, *arrays)
    return out[:n], [v[0] for v in out[n:]]


HEAD_DIM = 64
PASSES = 4
EPSILON = 1e-05
SCORE_SCALE = 0.125
GELU_COEF = 0.7978845608028654
GELU_CUBE = 0.044715


def dot(left, right, dims=((1,), (0,))):
    return lax.dot_general(left, right, (dims, ((), ())), preferred_element_type=jnp.float32)


NT, TN = ((1,), (1,)), ((0,), (0,))


def normalise(values):
    centre = values - jnp.mean(values, axis=-1, keepdims=True)
    scale = lax.rsqrt(jnp.mean(centre * centre, axis=-1, keepdims=True) + EPSILON)
    return centre * scale, scale


def normalise_back(grad, unit, scale):
    return scale * (grad - jnp.mean(grad, axis=-1, keepdims=True) - unit * jnp.mean(grad * unit, axis=-1, keepdims=True))


def block_kernel(chunk, prepare, sections, lengths, token_mask, hidden, cotangent, g1, b1, qkv_b, out_b, g2, b2, fc_b, proj_b,
                 qkv_hbm, out_hbm, fc_hbm, proj_hbm,
                 hidden_out, grad_hidden, a_t, o_t, c_t, g_t, dqkv_st, do_st, du_st, dm_st,
                 dg1, db1, dqkv_b, dout_b, dg2, db2, dfc_b, dproj_b,
                 qkv_w, out_w, fc_w, proj_w, state, unit1, unit2, scale1, scale2, qkv_st, prob_st, slope_st, mixed, wide, allow, sems):
    rows, width = hidden.shape
    hidden_width = fc_w.shape[1]
    pair = 2 * HEAD_DIM
    pairs = width // pair
    loads = [pltpu.make_async_copy(src, dst, sems.at[i]) for i, (src, dst) in enumerate(
        ((qkv_hbm, qkv_w), (out_hbm, out_w), (fc_hbm, fc_w), (proj_hbm, proj_w)))]
    for c in loads:
        c.start()
    prepare()
    for ref in (dg1, db1, dqkv_b, dout_b, dg2, db2, dfc_b, dproj_b):
        ref[...] = jnp.zeros_like(ref)
    query = lax.broadcasted_iota(jnp.int32, (rows, 2 * rows), 0)
    key = lax.rem(lax.broadcasted_iota(jnp.int32, (rows, 2 * rows), 1), rows)
    ok = (key < lengths[0]) & (jnp.broadcast_to(jnp.concatenate([token_mask[...]] * 2, axis=1), (rows, 2 * rows)) == 1)
    allow[...] = jnp.where((key < query) & ok | (key == query), 1.0, 0.0)
    state[...] = hidden[...].astype(jnp.float32)
    first = lax.broadcasted_iota(jnp.int32, (rows, pair), 1) < HEAD_DIM

    def both(block):
        wide = block.astype(jnp.float32)
        return jnp.concatenate([jnp.where(first, wide, 0.0), jnp.where(first, 0.0, wide)], axis=0).astype(jnp.bfloat16)

    def merge(block):
        return jnp.where(first, block[:rows], block[rows:])

    def halves(fn, block, *others):
        return [fn(block[:, s], *(o[:, s] for o in others)) for s in (slice(0, rows), slice(rows, 2 * rows))]

    def forward(k, wait):
        x = state[...]
        unit, scale = normalise(x)
        unit1[k] = unit
        scale1[k] = jnp.broadcast_to(scale, scale1.shape[1:])
        at = pl.ds(pl.multiple_of(k * rows, rows), rows)
        a = (unit * g1[...] + b1[...]).astype(jnp.bfloat16)
        mixed[...] = a
        a_t[:, at] = a.T
        if wait:
            loads[0].wait()
        for lo in range(0, 3 * width, chunk):
            cols = slice(lo, lo + chunk)
            qkv_st[k, :, cols] = (dot(mixed[...], qkv_w[:, cols]) + qkv_b[:, cols]).astype(jnp.bfloat16)
        for i in range(pairs):
            q = qkv_st[k, :, i * pair:(i + 1) * pair]
            keys = both(qkv_st[k, :, width + i * pair:width + (i + 1) * pair])
            values = both(qkv_st[k, :, 2 * width + i * pair:2 * width + (i + 1) * pair])
            scores = jnp.where(allow[...] > 0.5, dot(q, keys, NT) * SCORE_SCALE, -1e30)

            def softmax(s):
                e = jnp.exp(s - jnp.max(s, axis=-1, keepdims=True))
                return e / jnp.sum(e, axis=-1, keepdims=True)

            probs = jnp.concatenate(halves(softmax, scores), axis=1)
            prob_st[k, i] = probs
            o = dot(probs.astype(jnp.bfloat16), values).astype(jnp.bfloat16)
            mixed[:, i * pair:(i + 1) * pair] = o
            o_t[i * pair:(i + 1) * pair, at] = o.T
        if wait:
            loads[1].wait()
        h = x + (dot(mixed[...], out_w[...]) + out_b[...])
        unit, scale = normalise(h)
        unit2[k] = unit
        scale2[k] = jnp.broadcast_to(scale, scale2.shape[1:])
        c = (unit * g2[...] + b2[...]).astype(jnp.bfloat16)
        mixed[...] = c
        c_t[:, at] = c.T
        if wait:
            loads[2].wait()
        for lo in range(0, hidden_width, chunk):
            cols = slice(lo, lo + chunk)
            u = dot(mixed[...], fc_w[:, cols]) + fc_b[:, cols]
            square = u * u
            t = jnp.tanh(GELU_COEF * (u + GELU_CUBE * (square * u)))
            half = 0.5 * (1.0 + t)
            g = (u * half).astype(jnp.bfloat16)
            wide[:, cols] = g
            g_t[cols, at] = g.T
            slope_st[k, :, cols] = half + 0.5 * u * (1.0 - t * t) * (GELU_COEF * (1.0 + 3.0 * GELU_CUBE * square))
        if wait:
            loads[3].wait()
        y = h + (dot(wide[...], proj_w[...]) + proj_b[...])

        @pl.when(sections[0] >= k)
        def _():
            state[...] = y

    forward(0, True)
    lax.fori_loop(1, PASSES, lambda k, c: (forward(k, False), c)[1], 0)
    hidden_out[...] = state[...].astype(jnp.bfloat16)
    state[...] = cotangent[...].astype(jnp.float32)

    def column_sums(ref, cols, block):
        ref[:, cols] += jnp.sum(block.astype(jnp.float32), axis=0, keepdims=True)

    def backward(step, carry):
        k = PASSES - 1 - step
        live = (sections[0] >= k).astype(jnp.float32)
        dx = state[...]
        dy = dx * live
        dm_st[k] = dy.astype(jnp.bfloat16)
        column_sums(dproj_b, slice(None), dm_st[k])
        for lo in range(0, hidden_width, chunk):
            cols = slice(lo, lo + chunk)
            du = (dot(dm_st[k], proj_w[cols, :], NT) * slope_st[k, :, cols]).astype(jnp.bfloat16)
            du_st[k, :, cols] = du
            column_sums(dfc_b, cols, du)
        dc = dot(du_st[k], fc_w[...], NT)
        unit = unit2[k]
        dg2[...] += jnp.sum(dc * unit, axis=0, keepdims=True)
        column_sums(db2, slice(None), dc)
        dh = dy + normalise_back(dc * g2[...], unit, scale2[k, :, 0:1])
        state[...] = dh + dx * (1.0 - live)
        do_st[k] = dh.astype(jnp.bfloat16)
        column_sums(dout_b, slice(None), do_st[k])
        mixed[...] = dot(do_st[k], out_w[...], NT).astype(jnp.bfloat16)
        for i in range(pairs):
            at = [slice(j * width + i * pair, j * width + (i + 1) * pair) for j in range(3)]
            q = qkv_st[k, :, at[0]]
            keys, values = both(qkv_st[k, :, at[1]]), both(qkv_st[k, :, at[2]])
            grad = mixed[:, at[0]]
            probs = prob_st[k, i]
            dp = dot(grad, values, NT)

            def scores_back(d, p):
                return p * (d - jnp.sum(d * p, axis=-1, keepdims=True))

            ds = jnp.concatenate(halves(scores_back, dp, probs), axis=1).astype(jnp.bfloat16)
            dv = merge(dot(probs.astype(jnp.bfloat16), grad, TN))
            dq = dot(ds, keys) * SCORE_SCALE
            dk = merge(dot(ds, q, TN)) * SCORE_SCALE
            for j, d in enumerate((dq, dk, dv)):
                dqkv_st[k, :, at[j]] = d.astype(jnp.bfloat16)
        column_sums(dqkv_b, slice(None), dqkv_st[k])
        da = dot(dqkv_st[k], qkv_w[...], NT)
        unit = unit1[k]
        dg1[...] += jnp.sum(da * unit, axis=0, keepdims=True)
        column_sums(db1, slice(None), da)
        state[...] += normalise_back(da * g1[...], unit, scale1[k, :, 0:1])
        return carry

    lax.fori_loop(0, PASSES, backward, 0)
    grad_hidden[...] = state[...]


VECTORS = ("g1", "b1", "qv_b", "out_b", "g2", "b2", "fc_b", "proj_b")


class Spread:
    def __init__(self, devices, w):
        n = devices * w

        def owner(shape):
            return jnp.floor((lax.broadcasted_iota(jnp.int32, shape, 1).astype(jnp.float32) + 0.5) * (1.0 / w))

        place = lax.broadcasted_iota(jnp.int32, (128, n), 1).astype(jnp.float32) - owner((128, n)) * w
        lane = lax.broadcasted_iota(jnp.int32, (128, n), 0).astype(jnp.float32)
        self.pick = jnp.where(place == lane, 1.0, 0.0).astype(jnp.bfloat16)
        self.mine = owner((devices, n)) == lax.broadcasted_iota(jnp.int32, (devices, n), 0).astype(jnp.float32)

    def join(self, rows):
        return jnp.sum(jnp.where(self.mine, dot(rows.astype(jnp.bfloat16), self.pick), 0.0), axis=0, keepdims=True)

    def split(self, joined):
        values = jnp.where(self.mine, jnp.broadcast_to(joined, self.mine.shape), 0.0)
        high = values.astype(jnp.bfloat16)
        low = (values - high.astype(jnp.float32)).astype(jnp.bfloat16)
        return dot(high, self.pick, NT) + dot(low, self.pick, NT)


def packed_kernel(chunk, chunks, *refs):
    ins, packed, weights, outs = refs[:5], refs[5], refs[6:10], refs[10:20]
    packed_out, rest = refs[20], refs[21:]
    scratch, vectors, grads = rest[:-16], rest[-16:-8], rest[-8:]
    devices = packed.shape[0] // 8
    width = ins[3].shape[1]

    def prepare():
        for w in sorted(set(chunks)):
            spread = Spread(devices, w)
            for i, c in enumerate(chunks):
                if c != w:
                    continue
                row = spread.join(packed[pl.ds(i, devices, stride=8), :])
                if VECTORS[i] == "qv_b":
                    vectors[i][:, :width] = row[:, :width]
                    vectors[i][:, width:2 * width] = jnp.zeros((1, width), jnp.float32)
                    vectors[i][:, 2 * width:] = row[:, width:]
                else:
                    vectors[i][...] = row

    block_kernel(chunk, prepare, *ins, *vectors, *weights, *outs, *grads, *scratch)
    for w in sorted(set(chunks)):
        spread = Spread(devices, w)
        for i, c in enumerate(chunks):
            if c == w:
                row = grads[i][...]
                if VECTORS[i] == "qv_b":
                    row = jnp.concatenate([row[:, :width], row[:, 2 * width:]], axis=1)
                packed_out[pl.ds(i, devices, stride=8), :] = spread.split(row)


def run_block(sections, lengths, token_mask, hidden, cotangent, vectors, chunks, weights):
    packed = chunks is not None
    qkv_w, out_w, fc_w, proj_w = weights
    rows, width = hidden.shape
    ff = fc_w.shape[1]
    low, high = jnp.bfloat16, jnp.float32
    sizes = [width, width, 3 * width, width, width, width, ff, width]
    if packed:
        given = [vectors]
    else:
        qv_b = vectors[2]
        bias = jnp.concatenate([qv_b[:width], jnp.zeros_like(qv_b[:width]), qv_b[width:]])
        given = [v.astype(high)[None] for v in (*vectors[:2], bias, *vectors[3:])]
    lefts, rights = [width, width, width, ff], [3 * width, width, ff, width]
    pairs = width // (2 * HEAD_DIM)
    chunk = 512 if ff % 512 == 0 and width * 3 % 512 == 0 else 256
    smem, vmem, everywhere = [pl.BlockSpec(memory_space=m) for m in (pltpu.SMEM, pltpu.VMEM, pl.ANY)]
    rows_of = [pltpu.VMEM((1, n), high) for n in sizes]
    outs = pl.pallas_call(
        functools.partial(packed_kernel, chunk, chunks) if packed else functools.partial(block_kernel, chunk, lambda: None),
        out_shape=[jax.ShapeDtypeStruct((rows, width), low), jax.ShapeDtypeStruct((rows, width), high)]
        + [jax.ShapeDtypeStruct((n, PASSES * rows), low) for n in lefts]
        + [jax.ShapeDtypeStruct((PASSES, rows, n), low) for n in rights]
        + [jax.ShapeDtypeStruct(v.shape, high) for v in given],
        in_specs=[smem] * 2 + [vmem] * (3 + len(given)) + [everywhere] * 4,
        out_specs=[vmem] * (10 + len(given)),
        scratch_shapes=[pltpu.VMEM(w.shape, low) for w in (qkv_w, out_w, fc_w, proj_w)] + [
            pltpu.VMEM((rows, width), high),
            pltpu.VMEM((PASSES, rows, width), high),
            pltpu.VMEM((PASSES, rows, width), high),
            pltpu.VMEM((PASSES, rows, 128), high),
            pltpu.VMEM((PASSES, rows, 128), high),
            pltpu.VMEM((PASSES, rows, 3 * width), low),
            pltpu.VMEM((PASSES, pairs, rows, 2 * rows), high),
            pltpu.VMEM((PASSES, rows, ff), high),
            pltpu.VMEM((rows, width), low),
            pltpu.VMEM((rows, ff), low),
            pltpu.VMEM((rows, 2 * rows), high),
            pltpu.SemaphoreType.DMA((4,)),
        ] + (rows_of * 2 if packed else []),
        compiler_params=pltpu.CompilerParams(vmem_limit_bytes=67000000),
        name="block",
    )(sections, lengths, token_mask, hidden, cotangent, *given, qkv_w, out_w, fc_w, proj_w)
    hidden_out, grad_hidden = outs[:2]
    a, o, c, g = outs[2:6]
    dqkv, do, du, dm = [s.reshape(PASSES * rows, -1) for s in outs[6:10]]
    factors = ((a, dqkv), (o, do), (c, du), (g, dm))
    if packed:
        return hidden_out, grad_hidden, factors, outs[10]
    grads = [v[0] for v in outs[10:]]
    grads[2] = jnp.concatenate([grads[2][:width], grads[2][2 * width:]])
    return hidden_out, grad_hidden, factors, grads


def fetch_all(sizes, big, small):
    if any(w.shape[0] % 8 for w in big):
        whole = [lax.all_gather(v, ("dp", "fsdp"), axis=0, tiled=True) for v in (*big, *small)]
        return whole[:4], whole[4:], None
    chunks = tuple(v.shape[0] for v in small)
    width = -(-max(chunks) // 128) * 128
    count = len(small)
    packed = sum(
        jnp.pad(v.astype(jnp.float32)[None], ((i, count - 1 - i), (0, width - v.shape[0]))) for i, v in enumerate(small)
    )
    *full, packed = [w.reshape(-1, w.shape[-1]) for w in gather(sizes, (*big, packed))]
    return full, packed, chunks


def sum_all(sizes, factors, vectors, chunks):
    if chunks is None:
        big = [dot(left, right).astype(jnp.bfloat16) for left, right in factors]
        qkv, out, fc, proj, *sums = [
            lax.psum_scatter(v, ("dp", "fsdp"), scatter_dimension=0, tiled=True).astype(jnp.float32) for v in (*big, *vectors)
        ]
    else:
        packed = vectors.reshape(sizes["x"], 2, sizes["z"], sizes["y"], 8, -1)
        *big, packed = reduce_scatter(sizes, factors, packed)
        (qkv, out, fc, proj), sums = finish(chunks, big, packed)
    g1, b1, qv, ob, g2, b2, fb, pb = sums
    return (g1, b1, qkv, qv, out, ob), (g2, b2, fc, fb, proj, pb)


def body(
    sizes,
    hidden,
    sections,
    lengths,
    token_mask,
    cotangent,
    ln1_gain,
    ln1_bias,
    qkv_weight,
    qv_bias,
    out_weight,
    out_bias,
    ln2_gain,
    ln2_bias,
    fc_weight,
    fc_bias,
    proj_weight,
    proj_bias,
):
    seq_count, seq_len, model_width = hidden.shape
    row_count = seq_count * seq_len
    weights, vectors, chunks = fetch_all(
        sizes,
        (qkv_weight, out_weight, fc_weight, proj_weight),
        (ln1_gain, ln1_bias, qv_bias, out_bias, ln2_gain, ln2_bias, fc_bias, proj_bias),
    )
    hidden_out, grad_hidden, factors, terms = run_block(
        sections, lengths, token_mask, hidden.reshape(row_count, model_width), cotangent.reshape(row_count, model_width),
        vectors, chunks, weights,
    )
    attention_grads, finished = sum_all(sizes, factors, terms, chunks)
    hidden_out = hidden_out.reshape(hidden.shape)
    grad_hidden = grad_hidden.reshape(hidden.shape)
    return (
        hidden_out,
        grad_hidden,
        attention_grads[0],
        attention_grads[1],
        attention_grads[2],
        attention_grads[3],
        attention_grads[4],
        attention_grads[5],
        finished[0],
        finished[1],
        finished[2],
        finished[3],
        finished[4],
        finished[5],
    )


def solution(mesh):
    chips_x = mesh.shape["dp"] // 2
    sizes = {"x": chips_x, "y": chips_x, "z": mesh.shape["fsdp"] // chips_x}
    return jax.shard_map(
        functools.partial(body, sizes),
        mesh=mesh,
        in_specs=(
            P(("dp", "fsdp"), None, None),
            P(("dp", "fsdp")),
            P(("dp", "fsdp")),
            P(("dp", "fsdp"), None),
            P(("dp", "fsdp"), None, None),
            P(("dp", "fsdp")),
            P(("dp", "fsdp")),
            P(("dp", "fsdp"), None),
            P(("dp", "fsdp")),
            P(("dp", "fsdp"), None),
            P(("dp", "fsdp")),
            P(("dp", "fsdp")),
            P(("dp", "fsdp")),
            P(("dp", "fsdp"), None),
            P(("dp", "fsdp")),
            P(("dp", "fsdp"), None),
            P(("dp", "fsdp")),
        ),
        out_specs=(
            P(("dp", "fsdp"), None, None),
            P(("dp", "fsdp"), None, None),
            P(("dp", "fsdp")),
            P(("dp", "fsdp")),
            P(("dp", "fsdp"), None),
            P(("dp", "fsdp")),
            P(("dp", "fsdp"), None),
            P(("dp", "fsdp")),
            P(("dp", "fsdp")),
            P(("dp", "fsdp")),
            P(("dp", "fsdp"), None),
            P(("dp", "fsdp")),
            P(("dp", "fsdp"), None),
            P(("dp", "fsdp")),
        ),
        check_vma=False,
    )
```

```python
import functools
import heapq
import itertools

import jax
import jax.numpy as jnp
from jax import lax
from jax.experimental import pallas as pl
from jax.experimental.pallas import tpu as pltpu
from jax.sharding import PartitionSpec as P
MESH = pl.DeviceIdType.MESH

TREES = ("zyx", "zxy", "xyz")


def offsets(length):
    return [0, "o"] if length == 2 else list(range(-(length - 1), length))


class Place:
    def __init__(self, sizes):
        self.sizes = sizes
        dp, fs = lax.axis_index("dp"), lax.axis_index("fsdp")
        self.core = lax.rem(dp, 2)
        self.pos = {"x": dp // 2, "z": fs // sizes["y"], "y": lax.rem(fs, sizes["y"])}

    def device(self, pos, core):
        return (pos["x"] * 2 + core, pos["z"] * self.sizes["y"] + pos["y"])

    def index(self, pos, core):
        dp, fs = self.device(pos, core)
        return dp * (self.sizes["z"] * self.sizes["y"]) + fs

    def chip(self, pos):
        return (pos["x"] * self.sizes["z"] + pos["z"]) * self.sizes["y"] + pos["y"]

    def neighbours(self):
        out = [(None, self.device(self.pos, 1 - self.core))]
        for d, length in self.sizes.items():
            if length == 2:
                out.append((None, self.device({**self.pos, d: 1 - self.pos[d]}, self.core)))
            elif length > 2:
                for s in (1, -1):
                    q = self.pos[d] + s
                    out.append(((q >= 0) & (q < length), self.device({**self.pos, d: q}, self.core)))
        return out


def when(conds, fn):
    conds = [c for c in conds if c is not None]
    if not conds:
        fn()
    else:
        pl.when(functools.reduce(jnp.logical_and, conds))(lambda: (fn(), None)[1])


def entry_barrier(place):
    barrier = pltpu.get_barrier_semaphore()
    total = 0
    for cond, dev in place.neighbours():
        when([cond], lambda dev=dev: pl.semaphore_signal(barrier, inc=1, device_id=dev, device_id_type=MESH))
        total = total + (1 if cond is None else cond.astype(jnp.int32))
    pl.semaphore_wait(barrier, total)


def gather_kernel(sizes, pieces, order, n_in, *refs):
    ins, outs = refs[:n_in], refs[n_in:2 * n_in]
    send_sem, recv_sem, pair_send, pair_recv, local_sem = refs[2 * n_in:]
    place = Place(sizes)
    pos, core = place.pos, place.core
    entry_barrier(place)
    partner = place.device(pos, 1 - core)
    locals_ = []
    for a in range(n_in):
        c = pltpu.make_async_copy(ins[a], outs[a].at[pos["x"], core, pos["z"], pos["y"]], local_sem.at[a])
        c.start()
        locals_.append(c)

    def part(pi, at, who):
        a, tree, lo, n = pieces[pi]
        return outs[a].at[at["x"], who, at["z"], at["y"], pl.ds(lo, n)]

    def remote(src, dst, send, recv, dev):
        return pltpu.make_async_remote_copy(src_ref=src, dst_ref=dst, send_sem=send, recv_sem=recv, device_id=dev, device_id_type=MESH)

    def line(d):
        if sizes[d] == 1:
            return []
        if sizes[d] == 2:
            return [(0, None, 1 - pos[d])]
        return [(0, pos[d] + 1 < sizes[d], pos[d] + 1), (1, pos[d] > 0, pos[d] - 1)]

    left = {}
    for pi, t in order:
        left[pi] = left.get(pi, 0) + 1
    seen = dict.fromkeys(left, 0)
    whole = [slice(None)] * 3
    for pi, t in order:
        a, tree, lo, n = pieces[pi]
        own = all(v == 0 for v in t)
        at, conds = dict(pos), []
        for d, v in zip(tree, t):
            if v == "o":
                at[d] = 1 - pos[d]
            elif v != 0:
                at[d] = pos[d] + v
                conds.append((at[d] >= 0) if v < 0 else (at[d] < sizes[d]))
        chip = place.chip(at)
        dst = part(pi, at, core)
        src = ins[a].at[pl.ds(lo, n)] if own else dst
        k = max([j for j, v in enumerate(t) if v != 0], default=-1)

        def handle(tree=tree, t=t, own=own, chip=chip, dst=dst, src=src, k=k, pi=pi):
            if not own:
                remote(dst, dst, pair_send.at[pi], recv_sem.at[pi, chip], partner).wait_recv()
            for j in (2, 1, 0):
                d = tree[j]
                if j < k:
                    continue
                for slot, ok, q in line(d):
                    if j == k and (t[j] == "o" or (t[j] < 0) != (slot == 0)):
                        continue
                    when([ok], remote(src, dst, send_sem.at[pi, 2 * "xyz".index(d) + slot], recv_sem.at[pi, chip],
                                      place.device({**pos, d: q}, core)).start)
            remote(src, dst, pair_send.at[pi], pair_recv.at[pi], partner).start()
        when(conds, handle)
        seen[pi] += 1

    full = dict.fromkeys("xyz", slice(None))
    for pi, (a, tree, lo, n) in enumerate(pieces):
        for j, d in enumerate(tree):
            at = {e: (slice(None) if tree.index(e) < j else pos[e]) for e in "xyz"}
            for slot, ok, q in line(d):
                sem = send_sem.at[pi, 2 * "xyz".index(d) + slot]
                if sizes[d] == 2:
                    ref = part(pi, at, core)
                    remote(ref, ref, sem, recv_sem.at[pi, 0], partner).wait_send()
                else:
                    for z in range(sizes[d]):
                        ref = part(pi, {**at, d: z}, core)
                        sent = (pos[d] >= z) if slot == 0 else (pos[d] <= z)
                        when([ok, sent], remote(ref, ref, sem, recv_sem.at[pi, 0], partner).wait_send)
        ref = part(pi, full, core)
        remote(ref, ref, pair_send.at[pi], pair_recv.at[pi], partner).wait_send()
        ref = part(pi, full, 1 - core)
        remote(ref, ref, pair_send.at[pi], pair_recv.at[pi], partner).wait_recv()
    for c in locals_:
        c.wait()


def gather_order(sizes, pieces, alpha):
    ev = []
    for pi, (a, tree, lo, n) in enumerate(pieces):
        for t in itertools.product(*[offsets(sizes[d]) for d in tree]):
            hops = sum(1 if v == "o" else abs(v) for v in t)
            ev.append((pi * alpha + hops, pi, t))
    ev.sort(key=lambda e: (e[0], e[1]))
    return [(pi, t) for _, pi, t in ev]


def gather(sizes, shards, alpha=0.05):
    chips = sizes["x"] * sizes["y"] * sizes["z"]
    pieces = []
    for a, s in enumerate(shards):
        tiles = s.shape[0] // 8
        if tiles % 3 == 0 and tiles < 12:
            cuts = [(i, i * tiles // 3, tiles // 3) for i in range(3)]
        elif tiles % 2 == 0:
            cuts = [(i, i * tiles // 2, tiles // 2) for i in range(2)]
        else:
            cuts = [(2, 0, tiles)]
        for tree, lo, n in cuts:
            pieces.append((a, TREES[tree], lo * 8, n * 8))
    order = gather_order(sizes, pieces, alpha)
    n_in = len(shards)
    return pl.pallas_call(
        functools.partial(gather_kernel, sizes, pieces, order, n_in),
        out_shape=[jax.ShapeDtypeStruct((sizes["x"], 2, sizes["z"], sizes["y"]) + s.shape, s.dtype) for s in shards],
        in_specs=[pl.BlockSpec(memory_space=pltpu.VMEM)] * n_in,
        out_specs=[pl.BlockSpec(memory_space=pl.ANY)] * n_in,
        scratch_shapes=[
            pltpu.SemaphoreType.DMA((len(pieces), 6)),
            pltpu.SemaphoreType.DMA((len(pieces), chips)),
            pltpu.SemaphoreType.DMA((len(pieces),)),
            pltpu.SemaphoreType.DMA((len(pieces),)),
            pltpu.SemaphoreType.DMA((n_in,)),
        ],
        compiler_params=pltpu.CompilerParams(collective_id=0, has_side_effects=True),
        name="gather",
    )(*shards)


class View:
    def __init__(self, ref, dims, fixed=None, core=None):
        self.ref, self.dims, self.fixed, self.core = ref, dims, fixed or {}, core

    def fix(self, d, v):
        return View(self.ref, self.dims, {**self.fixed, d: v}, self.core)

    def free(self):
        return [d for d in self.dims if d not in self.fixed]

    def index(self, at, cols=None):
        idx = [self.fixed.get(d, at.get(d, slice(None))) for d in self.dims]
        if self.core is not None:
            core, lo, n = self.core
            return (idx[0], core, *idx[1:], slice(None), pl.ds(lo, n))
        return tuple(idx)

    def whole(self):
        return self.ref.at[self.index({})]


def accumulate(sizes, dst, terms):
    dims = terms[0].free()

    def step(i, carry):
        at = {}
        for d in reversed(dims):
            at[d] = lax.rem(i, sizes[d])
            i = i // sizes[d]
        total = None
        for t in terms:
            v = t.ref[t.index(at)].astype(jnp.float32)
            total = v if total is None else total + v
        if isinstance(dst, View):
            dst.ref[dst.index(at)] = total.astype(dst.ref.dtype)
        else:
            dst(total)
        return carry

    count = 1
    for d in dims:
        count *= sizes[d]
    if count == 1:
        step(0, 0)
    else:
        lax.fori_loop(0, count, step, 0)


def piece_buffers(sizes, piece, rows):
    a, tree, lo, n = piece
    dims = list("xzy")
    shapes = [tuple(sizes[d] for d in dims) + (rows, n)]
    for d in tree:
        dims.remove(d)
        rest = tuple(sizes[e] for e in dims) + (rows, n)
        if sizes[d] == 2:
            shapes.append(rest)
        elif sizes[d] > 2:
            shapes += [(sizes[d],) + rest] * 2
    return shapes


def piece_copies(sizes, tree):
    return 1 + sum(0 if sizes[d] == 1 else 1 if sizes[d] == 2 else 2 * sizes[d] for d in tree)


def tree_loads(sizes, tree):
    share, loads = 1.0, {}
    for d in tree:
        loads[d] = share * (sizes[d] - 1) / sizes[d]
        share /= sizes[d]
    return loads


def cut(shapes):
    order = sorted(range(len(shapes)), key=lambda a: -shapes[a][0] * shapes[a][1])
    out = []
    for i, a in enumerate(order):
        rows, cols = shapes[a]
        wide = max(256, 18432 // rows // 256 * 256)
        lo, small = 0, [256, 512] if i == 0 else [256] * 9 if i == len(order) - 1 else []
        while lo < cols:
            n = min(small.pop(0) if small else wide, cols - lo)
            out.append((a, lo, n))
            lo += n
    return out


def plan(sizes, shapes, rates):
    make_us, pair_us, link_us, hop_us = rates
    used, pieces, size = dict.fromkeys("xyz", 0.0), [], {}
    for a, lo, n in cut(shapes):
        rows = shapes[a][0]
        units = rows * n / 6144

        def worst(tree):
            loads = tree_loads(sizes, tree)
            return max(used[d] + units * loads[d] for d in tree), used[tree[0]]

        tree = min(("xzy", "yzx", "xyz", "yxz"), key=worst)
        for d, v in tree_loads(sizes, tree).items():
            used[d] += units * v
        size[len(pieces)] = units
        pieces.append((a, tree, lo, n))
    order, free, heap, count = [], dict.fromkeys(("pair", "x", "y", "z"), 0.0), [], itertools.count()
    now = 0.0

    def push(t, pi, what):
        heapq.heappush(heap, (t, next(count), pi, what))

    def carry(link, t, us):
        free[link] = max(t, free[link]) + us
        return free[link] + hop_us

    def launch(t, pi, j):
        tree = pieces[pi][1]
        if j == 3:
            return
        d = tree[j]
        part = size[pi]
        for e in tree[:j + 1]:
            part /= sizes[e]
        if sizes[d] == 1:
            launch(t, pi, j + 1)
        elif sizes[d] == 2:
            push(carry(d, t, part * link_us), pi, ("swap", j))
        else:
            top = sizes[d] - 1
            arrive = [carry(d, t, part * link_us) for _ in range(top)]
            for hop in range(1, top):
                for dest in range(top, hop, -1):
                    when_us = arrive[top - dest] + (hop - 1) * (hop_us + part * link_us)
                    push(when_us, pi, ("up", j, hop, dest))
                    push(when_us, pi, ("down", j, top - hop, top - dest))
            push(arrive[-1] + (top - 1) * hop_us + part * link_us, pi, ("land", j))

    for pi in range(len(pieces)):
        now += make_us * size[pi]
        push(now, pi, ("make",))
    while heap:
        t, _, pi, what = heapq.heappop(heap)
        order.append((pi, what))
        if what[0] == "make":
            push(carry("pair", t, size[pi] / 2 * pair_us), pi, ("pair",))
        elif what[0] == "pair":
            launch(t, pi, 0)
        elif what[0] in ("swap", "land"):
            launch(t, pi, what[1] + 1)
    return pieces, order


def reduce_kernel(sizes, pieces, order, weights, *refs):
    lefts, rights, packed = refs[:weights], refs[weights:2 * weights], refs[2 * weights]
    outs, rest = refs[2 * weights + 1:3 * weights + 2], list(refs[3 * weights + 2:])
    send_sem, recv_sem = rest[-2:]
    ins, rest = [*rest[:weights], packed], rest[weights:]
    place = Place(sizes)
    pos, core = place.pos, place.core
    partner = place.device(pos, 1 - core)
    state, base, sent = [], 0, []
    for pi, (a, tree, lo, n) in enumerate(pieces):
        k = len(piece_buffers(sizes, pieces[pi], 8))
        bufs, rest = rest[:k], rest[k:]
        copies = {"pair": (0, 0)}
        c, b = 1, 1
        for j, d in enumerate(tree):
            if sizes[d] > 1:
                copies[j] = (c, b)
                c += 1 if sizes[d] == 2 else 2 * sizes[d]
                b += 1 if sizes[d] == 2 else 2
        state.append({"bufs": bufs, "base": base, "copies": copies, "cur": None})
        base += c

    def copy(src, dst, sem, dev):
        return pltpu.make_async_remote_copy(src_ref=src, dst_ref=dst, send_sem=send_sem.at[sem], recv_sem=recv_sem.at[sem], device_id=dev, device_id_type=MESH)

    def send(conds, src, dst, sem, dev):
        c = copy(src, dst, sem, dev)
        when(conds, c.start)
        sent.append((conds, c))

    def await_copy(buf, sem):
        copy(buf, buf, sem, partner).wait_recv()

    entry_barrier(place)

    def make(a, lo, n):
        total, rows = lefts[a].shape[0], ins[a].shape[4]
        places = list(itertools.product(*[range(v) for v in ins[a].shape[:4]]))
        step = min(total, 768)
        for top in range(0, total, step):
            for left in range(lo, lo + n, 256):
                cols = slice(left, min(left + 256, lo + n))
                block = dot(lefts[a][top:top + step, :], rights[a][:, cols]).astype(ins[a].dtype)
                for i in range(step // rows):
                    ins[a][(*places[top // rows + i], slice(None), cols)] = block[i * rows:(i + 1) * rows]

    def launch(pi, j):
        a, tree, lo, n = pieces[pi]
        st = state[pi]
        while j < 3 and sizes[tree[j]] == 1:
            st["cur"] = st["cur"].fix(tree[j], 0)
            j += 1
        if j == 3:
            return
        d, cur = tree[j], st["cur"]
        c, b = st["copies"][j]
        c += st["base"]
        p, size = pos[d], sizes[d]
        if size == 2:
            send([], cur.fix(d, 1 - p).whole(), st["bufs"][b], c, place.device({**pos, d: 1 - p}, core))
            return
        for t in range(size - 1, 0, -1):
            send([p == 0], cur.fix(d, t).whole(), st["bufs"][b].at[t], c + t, place.device({**pos, d: p + 1}, core))
            t = size - 1 - t
            send([p == size - 1], cur.fix(d, t).whole(), st["bufs"][b + 1].at[t], c + size + t, place.device({**pos, d: p - 1}, core))

    def run(pi, what):
        a, tree, lo, n = pieces[pi]
        st = state[pi]
        if what[0] == "make":
            if a < weights:
                make(a, lo, n)
            src = View(ins[a], list("xzy"), core=(1 - core, lo, n))
            send([], src.whole(), st["bufs"][0], st["base"], partner)
            return
        if what[0] == "pair":
            buf = st["bufs"][0]
            await_copy(buf, st["base"])
            mine = View(ins[a], list("xzy"), core=(core, lo, n))
            st["cur"] = View(buf, list("xzy"))
            accumulate(sizes, st["cur"], [st["cur"], mine])
            launch(pi, 0)
            return
        j = what[1]
        d, cur = tree[j], st["cur"]
        c, b = st["copies"][j]
        c += st["base"]
        p, size = pos[d], sizes[d]
        last = all(sizes[e] == 1 for e in tree[j + 1:])
        left = [e for e in cur.free() if e != d]

        def store(total):
            outs[a][:, pl.ds(lo, n)] = total

        if what[0] == "swap":
            buf = st["bufs"][b]
            await_copy(buf, c)
            new = View(buf, left)
            accumulate(sizes, store if last else new, [cur.fix(d, p), new])
            st["cur"] = new
            launch(pi, j + 1)
        elif what[0] in ("up", "down"):
            up = what[0] == "up"
            here, t = what[2], what[3]
            sem = c + t if up else c + size + t
            buf = st["bufs"][b if up else b + 1]

            def relay():
                await_copy(buf.at[t], sem)
                new = View(buf, [d] + left, {d: t})
                accumulate(sizes, new, [cur.fix(d, t), new])

            when([p == here], relay)
            send([p == here], buf.at[t], buf.at[t], sem, place.device({**pos, d: p + 1 if up else p - 1}, core))
        else:
            ups, downs = st["bufs"][b], st["bufs"][b + 1]
            new = cur.fix(d, p)
            below, above = View(ups, [d] + left, {d: p}), View(downs, [d] + left, {d: p})
            for p_below, p_above, conds in ((False, True, [p == 0]), (True, True, [p > 0, p < size - 1]), (True, False, [p == size - 1])):
                def land(p_below=p_below, p_above=p_above):
                    terms = [new]
                    if p_below:
                        await_copy(ups.at[p], c + p)
                        terms.append(below)
                    if p_above:
                        await_copy(downs.at[p], c + size + p)
                        terms.append(above)
                    accumulate(sizes, store if last else new, terms)
                when(conds, land)
            st["cur"] = new
            launch(pi, j + 1)

    for pi, what in order:
        run(pi, what)
    for conds, c in sent:
        when(conds, c.wait_send)


def reduce_scatter(sizes, factors, packed, rates=(0.3, 1.2, 4.3, 1.2)):
    chips = sizes["x"] * sizes["y"] * sizes["z"]
    lead = (sizes["x"], 2, sizes["z"], sizes["y"])
    low = [(left.shape[0] // (2 * chips), right.shape[1]) for left, right in factors]
    shapes = low + [packed.shape[-2:]]
    pieces, order = plan(sizes, shapes, rates)
    buffers, copies = [], 0
    for piece in pieces:
        kind = jnp.bfloat16 if piece[0] < len(low) else packed.dtype
        buffers += [pltpu.VMEM(s, kind) for s in piece_buffers(sizes, piece, shapes[piece[0]][0])]
        copies += piece_copies(sizes, piece[1])
    vmem = pl.BlockSpec(memory_space=pltpu.VMEM)
    return pl.pallas_call(
        functools.partial(reduce_kernel, sizes, pieces, order, len(low)),
        out_shape=[jax.ShapeDtypeStruct(s, jnp.float32) for s in shapes],
        in_specs=[vmem] * (2 * len(low) + 1),
        out_specs=[vmem] * len(shapes),
        scratch_shapes=[pltpu.VMEM(lead + s, jnp.bfloat16) for s in low] + buffers
        + [pltpu.SemaphoreType.DMA((copies,)), pltpu.SemaphoreType.DMA((copies,))],
        compiler_params=pltpu.CompilerParams(collective_id=1, has_side_effects=True, vmem_limit_bytes=67000000),
        name="reduce",
    )(*[left for left, _ in factors], *[right for _, right in factors], packed)


def finish_kernel(chunks, packed, *refs):
    n = (len(refs) - 1 - len(chunks)) // 2
    ins, outs, vectors, sems = refs[:n], refs[n:2 * n], refs[2 * n:-1], refs[-1]
    stores = [pltpu.make_async_copy(a, o, sems.at[i]) for i, (a, o) in enumerate(zip(ins, outs))]
    for o in stores:
        o.start()
    for i, w in enumerate(chunks):
        vectors[i][...] = packed[i:i + 1, :w]
    for o in stores:
        o.wait()


def finish(chunks, arrays, packed):
    n = len(arrays)
    vmem, everywhere = pl.BlockSpec(memory_space=pltpu.VMEM), pl.BlockSpec(memory_space=pl.ANY)
    out = pl.pallas_call(
        functools.partial(finish_kernel, chunks),
        out_shape=[jax.ShapeDtypeStruct(a.shape, a.dtype) for a in arrays] + [jax.ShapeDtypeStruct((1, w), packed.dtype) for w in chunks],
        in_specs=[vmem] * (n + 1),
        out_specs=[everywhere] * n + [vmem] * len(chunks),
        scratch_shapes=[pltpu.SemaphoreType.DMA((n,))],
        name="finish",
    )(packed, *arrays)
    return out[:n], [v[0] for v in out[n:]]


HEAD_DIM = 64
PASSES = 4
EPSILON = 1e-05
SCORE_SCALE = 0.125
GELU_COEF = 0.7978845608028654
GELU_CUBE = 0.044715


def dot(left, right, dims=((1,), (0,))):
    return lax.dot_general(left, right, (dims, ((), ())), preferred_element_type=jnp.float32)


NT, TN = ((1,), (1,)), ((0,), (0,))


def normalise(values):
    centre = values - jnp.mean(values, axis=-1, keepdims=True)
    scale = lax.rsqrt(jnp.mean(centre * centre, axis=-1, keepdims=True) + EPSILON)
    return centre * scale, scale


def normalise_back(grad, unit, scale):
    return scale * (grad - jnp.mean(grad, axis=-1, keepdims=True) - unit * jnp.mean(grad * unit, axis=-1, keepdims=True))


def block_kernel(chunk, prepare, sections, lengths, token_mask, hidden, cotangent, g1, b1, qkv_b, out_b, g2, b2, fc_b, proj_b,
                 qkv_hbm, out_hbm, fc_hbm, proj_hbm,
                 hidden_out, grad_hidden, a_t, o_t, c_t, g_t, dqkv_st, do_st, du_st, dm_st,
                 dg1, db1, dqkv_b, dout_b, dg2, db2, dfc_b, dproj_b,
                 qkv_w, out_w, fc_w, proj_w, state, unit1, unit2, scale1, scale2, qkv_st, prob_st, slope_st, mixed, wide, allow, sems):
    rows, width = hidden.shape
    hidden_width = fc_w.shape[1]
    pair = 2 * HEAD_DIM
    pairs = width // pair
    loads = [pltpu.make_async_copy(src, dst, sems.at[i]) for i, (src, dst) in enumerate(
        ((qkv_hbm, qkv_w), (out_hbm, out_w), (fc_hbm, fc_w), (proj_hbm, proj_w)))]
    for c in loads:
        c.start()
    prepare()
    for ref in (dg1, db1, dqkv_b, dout_b, dg2, db2, dfc_b, dproj_b):
        ref[...] = jnp.zeros_like(ref)
    query = lax.broadcasted_iota(jnp.int32, (rows, 2 * rows), 0)
    key = lax.rem(lax.broadcasted_iota(jnp.int32, (rows, 2 * rows), 1), rows)
    ok = (key < lengths[0]) & (jnp.broadcast_to(jnp.concatenate([token_mask[...]] * 2, axis=1), (rows, 2 * rows)) == 1)
    allow[...] = jnp.where((key < query) & ok | (key == query), 1.0, 0.0)
    state[...] = hidden[...].astype(jnp.float32)
    first = lax.broadcasted_iota(jnp.int32, (rows, pair), 1) < HEAD_DIM

    def both(block):
        wide = block.astype(jnp.float32)
        return jnp.concatenate([jnp.where(first, wide, 0.0), jnp.where(first, 0.0, wide)], axis=0).astype(jnp.bfloat16)

    def merge(block):
        return jnp.where(first, block[:rows], block[rows:])

    def halves(fn, block, *others):
        return [fn(block[:, s], *(o[:, s] for o in others)) for s in (slice(0, rows), slice(rows, 2 * rows))]

    def forward(k, wait):
        x = state[...]
        unit, scale = normalise(x)
        unit1[k] = unit
        scale1[k] = jnp.broadcast_to(scale, scale1.shape[1:])
        at = pl.ds(pl.multiple_of(k * rows, rows), rows)
        a = (unit * g1[...] + b1[...]).astype(jnp.bfloat16)
        mixed[...] = a
        a_t[:, at] = a.T
        if wait:
            loads[0].wait()
        for lo in range(0, 3 * width, chunk):
            cols = slice(lo, lo + chunk)
            qkv_st[k, :, cols] = (dot(mixed[...], qkv_w[:, cols]) + qkv_b[:, cols]).astype(jnp.bfloat16)
        for i in range(pairs):
            q = qkv_st[k, :, i * pair:(i + 1) * pair]
            keys = both(qkv_st[k, :, width + i * pair:width + (i + 1) * pair])
            values = both(qkv_st[k, :, 2 * width + i * pair:2 * width + (i + 1) * pair])
            scores = jnp.where(allow[...] > 0.5, dot(q, keys, NT) * SCORE_SCALE, -1e30)

            def softmax(s):
                e = jnp.exp(s - jnp.max(s, axis=-1, keepdims=True))
                return e / jnp.sum(e, axis=-1, keepdims=True)

            probs = jnp.concatenate(halves(softmax, scores), axis=1)
            prob_st[k, i] = probs
            o = dot(probs.astype(jnp.bfloat16), values).astype(jnp.bfloat16)
            mixed[:, i * pair:(i + 1) * pair] = o
            o_t[i * pair:(i + 1) * pair, at] = o.T
        if wait:
            loads[1].wait()
        h = x + (dot(mixed[...], out_w[...]) + out_b[...])
        unit, scale = normalise(h)
        unit2[k] = unit
        scale2[k] = jnp.broadcast_to(scale, scale2.shape[1:])
        c = (unit * g2[...] + b2[...]).astype(jnp.bfloat16)
        mixed[...] = c
        c_t[:, at] = c.T
        if wait:
            loads[2].wait()
        for lo in range(0, hidden_width, chunk):
            cols = slice(lo, lo + chunk)
            u = dot(mixed[...], fc_w[:, cols]) + fc_b[:, cols]
            square = u * u
            t = jnp.tanh(GELU_COEF * (u + GELU_CUBE * (square * u)))
            half = 0.5 * (1.0 + t)
            g = (u * half).astype(jnp.bfloat16)
            wide[:, cols] = g
            g_t[cols, at] = g.T
            slope_st[k, :, cols] = half + 0.5 * u * (1.0 - t * t) * (GELU_COEF * (1.0 + 3.0 * GELU_CUBE * square))
        if wait:
            loads[3].wait()
        y = h + (dot(wide[...], proj_w[...]) + proj_b[...])

        @pl.when(sections[0] >= k)
        def _():
            state[...] = y

    forward(0, True)
    lax.fori_loop(1, PASSES, lambda k, c: (forward(k, False), c)[1], 0)
    hidden_out[...] = state[...].astype(jnp.bfloat16)
    state[...] = cotangent[...].astype(jnp.float32)

    def column_sums(ref, cols, block):
        ref[:, cols] += jnp.sum(block.astype(jnp.float32), axis=0, keepdims=True)

    def backward(step, carry):
        k = PASSES - 1 - step
        live = (sections[0] >= k).astype(jnp.float32)
        dx = state[...]
        dy = dx * live
        dm_st[k] = dy.astype(jnp.bfloat16)
        column_sums(dproj_b, slice(None), dm_st[k])
        for lo in range(0, hidden_width, chunk):
            cols = slice(lo, lo + chunk)
            du = (dot(dm_st[k], proj_w[cols, :], NT) * slope_st[k, :, cols]).astype(jnp.bfloat16)
            du_st[k, :, cols] = du
            column_sums(dfc_b, cols, du)
        dc = dot(du_st[k], fc_w[...], NT)
        unit = unit2[k]
        dg2[...] += jnp.sum(dc * unit, axis=0, keepdims=True)
        column_sums(db2, slice(None), dc)
        dh = dy + normalise_back(dc * g2[...], unit, scale2[k, :, 0:1])
        state[...] = dh + dx * (1.0 - live)
        do_st[k] = dh.astype(jnp.bfloat16)
        column_sums(dout_b, slice(None), do_st[k])
        mixed[...] = dot(do_st[k], out_w[...], NT).astype(jnp.bfloat16)
        for i in range(pairs):
            at = [slice(j * width + i * pair, j * width + (i + 1) * pair) for j in range(3)]
            q = qkv_st[k, :, at[0]]
            keys, values = both(qkv_st[k, :, at[1]]), both(qkv_st[k, :, at[2]])
            grad = mixed[:, at[0]]
            probs = prob_st[k, i]
            dp = dot(grad, values, NT)

            def scores_back(d, p):
                return p * (d - jnp.sum(d * p, axis=-1, keepdims=True))

            ds = jnp.concatenate(halves(scores_back, dp, probs), axis=1).astype(jnp.bfloat16)
            dv = merge(dot(probs.astype(jnp.bfloat16), grad, TN))
            dq = dot(ds, keys) * SCORE_SCALE
            dk = merge(dot(ds, q, TN)) * SCORE_SCALE
            for j, d in enumerate((dq, dk, dv)):
                dqkv_st[k, :, at[j]] = d.astype(jnp.bfloat16)
        column_sums(dqkv_b, slice(None), dqkv_st[k])
        da = dot(dqkv_st[k], qkv_w[...], NT)
        unit = unit1[k]
        dg1[...] += jnp.sum(da * unit, axis=0, keepdims=True)
        column_sums(db1, slice(None), da)
        state[...] += normalise_back(da * g1[...], unit, scale1[k, :, 0:1])
        return carry

    lax.fori_loop(0, PASSES, backward, 0)
    grad_hidden[...] = state[...]


VECTORS = ("g1", "b1", "qv_b", "out_b", "g2", "b2", "fc_b", "proj_b")


class Spread:
    def __init__(self, devices, w):
        n = devices * w

        def owner(shape):
            return jnp.floor((lax.broadcasted_iota(jnp.int32, shape, 1).astype(jnp.float32) + 0.5) * (1.0 / w))

        place = lax.broadcasted_iota(jnp.int32, (128, n), 1).astype(jnp.float32) - owner((128, n)) * w
        lane = lax.broadcasted_iota(jnp.int32, (128, n), 0).astype(jnp.float32)
        self.pick = jnp.where(place == lane, 1.0, 0.0).astype(jnp.bfloat16)
        self.mine = owner((devices, n)) == lax.broadcasted_iota(jnp.int32, (devices, n), 0).astype(jnp.float32)

    def join(self, rows):
        return jnp.sum(jnp.where(self.mine, dot(rows.astype(jnp.bfloat16), self.pick), 0.0), axis=0, keepdims=True)

    def split(self, joined):
        values = jnp.where(self.mine, jnp.broadcast_to(joined, self.mine.shape), 0.0)
        high = values.astype(jnp.bfloat16)
        low = (values - high.astype(jnp.float32)).astype(jnp.bfloat16)
        return dot(high, self.pick, NT) + dot(low, self.pick, NT)


def packed_kernel(chunk, chunks, *refs):
    ins, packed, weights, outs = refs[:5], refs[5], refs[6:10], refs[10:20]
    packed_out, rest = refs[20], refs[21:]
    scratch, vectors, grads = rest[:-16], rest[-16:-8], rest[-8:]
    devices = packed.shape[0] // 8
    width = ins[3].shape[1]

    def prepare():
        for w in sorted(set(chunks)):
            spread = Spread(devices, w)
            for i, c in enumerate(chunks):
                if c != w:
                    continue
                row = spread.join(packed[pl.ds(i, devices, stride=8), :])
                if VECTORS[i] == "qv_b":
                    vectors[i][:, :width] = row[:, :width]
                    vectors[i][:, width:2 * width] = jnp.zeros((1, width), jnp.float32)
                    vectors[i][:, 2 * width:] = row[:, width:]
                else:
                    vectors[i][...] = row

    block_kernel(chunk, prepare, *ins, *vectors, *weights, *outs, *grads, *scratch)
    for w in sorted(set(chunks)):
        spread = Spread(devices, w)
        for i, c in enumerate(chunks):
            if c == w:
                row = grads[i][...]
                if VECTORS[i] == "qv_b":
                    row = jnp.concatenate([row[:, :width], row[:, 2 * width:]], axis=1)
                packed_out[pl.ds(i, devices, stride=8), :] = spread.split(row)


def run_block(sections, lengths, token_mask, hidden, cotangent, vectors, chunks, weights):
    packed = chunks is not None
    qkv_w, out_w, fc_w, proj_w = weights
    rows, width = hidden.shape
    ff = fc_w.shape[1]
    low, high = jnp.bfloat16, jnp.float32
    sizes = [width, width, 3 * width, width, width, width, ff, width]
    if packed:
        given = [vectors]
    else:
        qv_b = vectors[2]
        bias = jnp.concatenate([qv_b[:width], jnp.zeros_like(qv_b[:width]), qv_b[width:]])
        given = [v.astype(high)[None] for v in (*vectors[:2], bias, *vectors[3:])]
    lefts, rights = [width, width, width, ff], [3 * width, width, ff, width]
    pairs = width // (2 * HEAD_DIM)
    chunk = 512 if ff % 512 == 0 and width * 3 % 512 == 0 else 256
    smem, vmem, everywhere = [pl.BlockSpec(memory_space=m) for m in (pltpu.SMEM, pltpu.VMEM, pl.ANY)]
    rows_of = [pltpu.VMEM((1, n), high) for n in sizes]
    outs = pl.pallas_call(
        functools.partial(packed_kernel, chunk, chunks) if packed else functools.partial(block_kernel, chunk, lambda: None),
        out_shape=[jax.ShapeDtypeStruct((rows, width), low), jax.ShapeDtypeStruct((rows, width), high)]
        + [jax.ShapeDtypeStruct((n, PASSES * rows), low) for n in lefts]
        + [jax.ShapeDtypeStruct((PASSES, rows, n), low) for n in rights]
        + [jax.ShapeDtypeStruct(v.shape, high) for v in given],
        in_specs=[smem] * 2 + [vmem] * (3 + len(given)) + [everywhere] * 4,
        out_specs=[vmem] * (10 + len(given)),
        scratch_shapes=[pltpu.VMEM(w.shape, low) for w in (qkv_w, out_w, fc_w, proj_w)] + [
            pltpu.VMEM((rows, width), high),
            pltpu.VMEM((PASSES, rows, width), high),
            pltpu.VMEM((PASSES, rows, width), high),
            pltpu.VMEM((PASSES, rows, 128), high),
            pltpu.VMEM((PASSES, rows, 128), high),
            pltpu.VMEM((PASSES, rows, 3 * width), low),
            pltpu.VMEM((PASSES, pairs, rows, 2 * rows), high),
            pltpu.VMEM((PASSES, rows, ff), high),
            pltpu.VMEM((rows, width), low),
            pltpu.VMEM((rows, ff), low),
            pltpu.VMEM((rows, 2 * rows), high),
            pltpu.SemaphoreType.DMA((4,)),
        ] + (rows_of * 2 if packed else []),
        compiler_params=pltpu.CompilerParams(vmem_limit_bytes=67000000),
        name="block",
    )(sections, lengths, token_mask, hidden, cotangent, *given, qkv_w, out_w, fc_w, proj_w)
    hidden_out, grad_hidden = outs[:2]
    a, o, c, g = outs[2:6]
    dqkv, do, du, dm = [s.reshape(PASSES * rows, -1) for s in outs[6:10]]
    factors = ((a, dqkv), (o, do), (c, du), (g, dm))
    if packed:
        return hidden_out, grad_hidden, factors, outs[10]
    grads = [v[0] for v in outs[10:]]
    grads[2] = jnp.concatenate([grads[2][:width], grads[2][2 * width:]])
    return hidden_out, grad_hidden, factors, grads


def fetch_all(sizes, big, small):
    if any(w.shape[0] % 8 for w in big):
        whole = [lax.all_gather(v, ("dp", "fsdp"), axis=0, tiled=True) for v in (*big, *small)]
        return whole[:4], whole[4:], None
    chunks = tuple(v.shape[0] for v in small)
    width = -(-max(chunks) // 128) * 128
    count = len(small)
    packed = sum(
        jnp.pad(v.astype(jnp.float32)[None], ((i, count - 1 - i), (0, width - v.shape[0]))) for i, v in enumerate(small)
    )
    *full, packed = [w.reshape(-1, w.shape[-1]) for w in gather(sizes, (*big, packed))]
    return full, packed, chunks


def sum_all(sizes, factors, vectors, chunks):
    if chunks is None:
        big = [dot(left, right).astype(jnp.bfloat16) for left, right in factors]
        qkv, out, fc, proj, *sums = [
            lax.psum_scatter(v, ("dp", "fsdp"), scatter_dimension=0, tiled=True).astype(jnp.float32) for v in (*big, *vectors)
        ]
    else:
        packed = vectors.reshape(sizes["x"], 2, sizes["z"], sizes["y"], 8, -1)
        *big, packed = reduce_scatter(sizes, factors, packed)
        (qkv, out, fc, proj), sums = finish(chunks, big, packed)
    g1, b1, qv, ob, g2, b2, fb, pb = sums
    return (g1, b1, qkv, qv, out, ob), (g2, b2, fc, fb, proj, pb)


def body(
    sizes,
    hidden,
    sections,
    lengths,
    token_mask,
    cotangent,
    ln1_gain,
    ln1_bias,
    qkv_weight,
    qv_bias,
    out_weight,
    out_bias,
    ln2_gain,
    ln2_bias,
    fc_weight,
    fc_bias,
    proj_weight,
    proj_bias,
):
    seq_count, seq_len, model_width = hidden.shape
    row_count = seq_count * seq_len
    weights, vectors, chunks = fetch_all(
        sizes,
        (qkv_weight, out_weight, fc_weight, proj_weight),
        (ln1_gain, ln1_bias, qv_bias, out_bias, ln2_gain, ln2_bias, fc_bias, proj_bias),
    )
    hidden_out, grad_hidden, factors, terms = run_block(
        sections, lengths, token_mask, hidden.reshape(row_count, model_width), cotangent.reshape(row_count, model_width),
        vectors, chunks, weights,
    )
    attention_grads, finished = sum_all(sizes, factors, terms, chunks)
    hidden_out = hidden_out.reshape(hidden.shape)
    grad_hidden = grad_hidden.reshape(hidden.shape)
    return (
        hidden_out,
        grad_hidden,
        attention_grads[0],
        attention_grads[1],
        attention_grads[2],
        attention_grads[3],
        attention_grads[4],
        attention_grads[5],
        finished[0],
        finished[1],
        finished[2],
        finished[3],
        finished[4],
        finished[5],
    )


def solution(mesh):
    chips_x = mesh.shape["dp"] // 2
    sizes = {"x": chips_x, "y": chips_x, "z": mesh.shape["fsdp"] // chips_x}
    return jax.shard_map(
        functools.partial(body, sizes),
        mesh=mesh,
        in_specs=(
            P(("dp", "fsdp"), None, None),
            P(("dp", "fsdp")),
            P(("dp", "fsdp")),
            P(("dp", "fsdp"), None),
            P(("dp", "fsdp"), None, None),
            P(("dp", "fsdp")),
            P(("dp", "fsdp")),
            P(("dp", "fsdp"), None),
            P(("dp", "fsdp")),
            P(("dp", "fsdp"), None),
            P(("dp", "fsdp")),
            P(("dp", "fsdp")),
            P(("dp", "fsdp")),
            P(("dp", "fsdp"), None),
            P(("dp", "fsdp")),
            P(("dp", "fsdp"), None),
            P(("dp", "fsdp")),
        ),
        out_specs=(
            P(("dp", "fsdp"), None, None),
            P(("dp", "fsdp"), None, None),
            P(("dp", "fsdp")),
            P(("dp", "fsdp")),
            P(("dp", "fsdp"), None),
            P(("dp", "fsdp")),
            P(("dp", "fsdp"), None),
            P(("dp", "fsdp")),
            P(("dp", "fsdp")),
            P(("dp", "fsdp")),
            P(("dp", "fsdp"), None),
            P(("dp", "fsdp")),
            P(("dp", "fsdp"), None),
            P(("dp", "fsdp")),
        ),
        check_vma=False,
    )
```
